768 devices in a mesh: lat: 96 (over y, z), lon: 8 (over x, core).
Axes of the slice: x: 4, y: 8, z: 12, core: 2. Of those that a mesh axis runs over, the one named last changes fastest.
Arguments:
- prognostic: bfloat16 [9, 768, 3072], P(None, 'lat', 'lon'), may hold values from -6 to 6
- departure: int32 [768, 3072], P('lat', 'lon'), may hold values from 0 to 63
- lat_weight: float32 [768, 3072], P('lat', 'lon'), may hold values from 0 to 1
- lon_weight: float32 [768, 3072], P('lat', 'lon'), may hold values from 0 to 1
- cycle_waves: int32 [768], P('lat'), may hold values from 192 to 768
- wave_order: int32 [768], replicated, may hold values from 0 to 767, each once
Outputs:
- spectral: float32 [768, 2, 9, 768], P(('lat', 'lon'))
The draws below stay inside these ranges and needn't reach their ends.
Inputs may be any that keep to these rules, and one draw needn't show every extreme that they name: `wave_order`: each of the 768 wavenumbers stands in exactly one slot.
All inputs are finite; a program needn't handle non-finite values.
Results may differ from the reference program's by a relative error of at most 0.0025.
The reference program's roundings to bfloat16 on the way count: a program that leaves them out, or rounds other values in their place, can miss the bound.
Values may be sent and summed in bfloat16 or wider, within the bound.
No kernel may reach another device: no remote copies, remote signals or barrier semaphores. Data moves between devices by JAX's collectives and lax.ppermute only.
A program may use at most 128 MiB of HBM per device.

```python
import math
import jax
import jax.numpy as jnp
from jax import lax

C = 9
NLON = 3072
HALO = 4
NLAT = 768
M = 768


def plant(entries, own_key, smallest, top_value):
    longest = entries.shape.index(max(entries.shape))
    spots = []
    for shift in (0, 1):
        where = [jax.random.randint(jax.random.fold_in(own_key, axis), (), 0, length) for axis, length in enumerate(entries.shape)]
        where[longest] = (where[longest] + shift) % entries.shape[longest]
        spots.append(tuple(where))
    return entries.at[spots[0]].set(smallest).at[spots[1]].set(top_value)


def levels(stream_key, dims, pieces, smallest, largest):
    def one(dim, blocks):
        draws = jax.random.uniform(jax.random.fold_in(jax.random.fold_in(stream_key, 6), dim), (blocks,), jnp.float32, smallest / len(pieces), largest / len(pieces))
        return jnp.repeat(jnp.exp(draws), dims[dim] // blocks).reshape((-1,) + (1,) * (len(dims) - dim - 1))

    gain = one(*pieces[0])
    for cut in pieces[1:]:
        gain = gain * one(*cut)
    return gain


def normal_values(rng, shape, scale, limit, cuts=(), held_as=jnp.bfloat16):
    loudness = levels(rng, shape, cuts, -0.22, 0.18) if cuts else 1.0
    array = jax.random.normal(rng, shape, jnp.float32) * scale * loudness
    return jnp.minimum(jnp.maximum(array, -limit), limit).astype(held_as)


def setup_inputs(seed: int = 0) -> dict:
    keys = jax.random.split(jax.random.key(seed), 7)
    prognostic = normal_values(keys[0], (C, NLAT, NLON), 1.0, 6.0, ((1, 96), (2, 8)))
    departure = plant(jax.random.randint(keys[1], (NLAT, NLON), 0, 4 * HALO * HALO), jax.random.fold_in(keys[1], 1), 0, (4 * HALO * HALO) - 1).astype(jnp.int32)
    lat_weight = jnp.clip(1.0 * jax.random.uniform(keys[2], (NLAT, NLON), jnp.float32) ** levels(keys[2], (NLAT, NLON), ((0, 96), (1, 8)), -0.2, 0.2), 0.0, 1.0)
    lon_weight = jnp.clip(1.0 * jax.random.uniform(keys[3], (NLAT, NLON), jnp.float32) ** levels(keys[3], (NLAT, NLON), ((0, 96), (1, 8)), -0.2, 0.2), 0.0, 1.0)
    cycle_waves = plant(jax.random.randint(keys[4], (NLAT,), M // 4, M + 1), jax.random.fold_in(keys[4], 1), M // 4, M).astype(jnp.int32)
    wave_order = jax.random.permutation(keys[5], M).astype(jnp.int32)
    return dict(prognostic=prognostic, departure=departure, lat_weight=lat_weight, lon_weight=lon_weight, cycle_waves=cycle_waves, wave_order=wave_order)


LGAMMA_HALF_THREE = 0.5 * math.log(math.pi) - math.log(2.0)

def legendre_rows(orders, angles, length, ceiling, unroll):
    order_real = orders.astype(jnp.float32)
    cosine = jnp.cos(angles)
    log_start = 0.5 * math.log(0.5) + 0.5 * (lax.lgamma(order_real + 1.5) - LGAMMA_HALF_THREE - lax.lgamma(order_real + 1.0)) + order_real * jnp.log(jnp.sin(angles))

    def advance(carry, offset):
        previous, second, log_scale = carry
        degree = order_real + offset
        factor_a = jnp.sqrt((4.0 * degree * degree - 1.0) / (degree * degree - order_real * order_real))
        factor_b = jnp.sqrt(jnp.maximum(((degree - 1.0) * (degree - 1.0) - order_real * order_real) / (4.0 * (degree - 1.0) * (degree - 1.0) - 1.0), 0.0))
        fresh = factor_a * (cosine * previous - factor_b * second)
        result = fresh * jnp.exp(log_scale + log_start)
        factor = jnp.maximum(jnp.maximum(jnp.abs(fresh), jnp.abs(previous)), 1.0)
        return ((fresh / factor, previous / factor, log_scale + jnp.log(factor)), result)
    indices = jnp.arange(1, length, dtype=jnp.int32).astype(jnp.float32)
    initial = (jnp.ones_like(cosine), jnp.zeros_like(cosine), jnp.zeros_like(cosine))
    _, later = lax.scan(advance, initial, indices, unroll=unroll)
    values = jnp.concatenate([jnp.exp(log_start)[None, :], later], axis=0)
    inside = jnp.arange(length, dtype=jnp.int32)[:, None] < (ceiling - orders)[None, :]
    return jnp.where(inside, values, 0.0)

def legendre_table(orders, cycle_ids, lat_total, wave_count, unroll):
    cycle_angles = (cycle_ids.astype(jnp.float32) + 0.5) * (math.pi / lat_total)
    slot_count = orders.shape[0]
    cycle_count = cycle_ids.shape[0]
    orders_flat = jnp.repeat(orders, cycle_count)
    angles_flat = jnp.tile(cycle_angles, slot_count)
    values = legendre_rows(orders_flat, angles_flat, wave_count, wave_count, unroll)
    scaled = values * (jnp.sin(angles_flat) * (math.pi / math.sqrt(lat_total)))[None, :]
    return scaled.reshape(wave_count, slot_count, cycle_count).astype(jnp.bfloat16)

def fourier_table(wave_order, points):
    doubled = jnp.repeat(wave_order, 2)
    column = lax.broadcasted_iota(jnp.int32, (points, doubled.shape[0]), 0)
    parity = lax.broadcasted_iota(jnp.int32, (points, doubled.shape[0]), 1) % 2
    phases = column * doubled[None, :] % points
    angles = phases.astype(jnp.float32) * (2.0 * math.pi / points) + parity.astype(jnp.float32) * (0.5 * math.pi)
    return (jnp.cos(angles) * (1.0 / math.sqrt(points))).astype(jnp.bfloat16)

def reference(prognostic, departure, lat_weight, lon_weight, cycle_waves, wave_order):
    margin = HALO
    channels = prognostic.shape[0]
    zero_rows = jnp.pad(prognostic, ((0, 0), (margin, margin), (0, 0)))
    padded = jnp.concatenate([zero_rows[:, :, NLON - margin:], zero_rows, zero_rows[:, :, :margin]], axis=2)
    ext_cols = NLON + 2 * margin
    flat_field = padded.reshape(channels, -1)
    stencil = 2 * margin
    row_shift = departure // stencil - margin
    col_shift = departure % stencil - margin
    row_grid = lax.broadcasted_iota(jnp.int32, (NLAT, NLON), 0)
    col_grid = lax.broadcasted_iota(jnp.int32, (NLAT, NLON), 1)
    corner = (row_grid + margin + row_shift) * ext_cols + col_grid + margin + col_shift
    corners = jnp.stack([corner, corner + ext_cols, corner + 1, corner + ext_cols + 1]).reshape(-1)

    def interpolate(channel):
        picked = jnp.take(channel, corners, axis=0).reshape(4, NLAT, NLON).astype(jnp.float32)
        northward = lat_weight
        eastward = lon_weight
        mixed = (1.0 - northward) * (1.0 - eastward) * picked[0] + northward * (1.0 - eastward) * picked[1] + (1.0 - northward) * eastward * picked[2] + northward * eastward * picked[3]
        return mixed.astype(jnp.bfloat16)
    arrival = lax.map(interpolate, flat_field)
    fourier = fourier_table(wave_order, NLON)
    spectrum = jnp.einsum('crj,jq->qcr', arrival.astype(jnp.float32), fourier.astype(jnp.float32)).reshape(M, 2, channels, NLAT)
    resolved = wave_order[:, None] < cycle_waves[None, :]
    masked = jnp.where(resolved[:, None, None, :], spectrum, 0.0).astype(jnp.bfloat16)
    cycle_ids = jnp.arange(NLAT, dtype=jnp.int32)

    def transform(inputs):
        wave_number, coeffs = inputs
        functions = legendre_table(wave_number[None], cycle_ids, NLAT, M, 1)[:, 0, :]
        return jnp.einsum('acr,kr->ack', coeffs.astype(jnp.float32), functions.astype(jnp.float32))
    return lax.map(transform, (wave_order, masked))
```

```python
import functools
import math

import jax
import jax.numpy as jnp
from jax import lax
from jax.experimental import pallas as pl
from jax.experimental.pallas import tpu as pltpu
from jax.sharding import PartitionSpec as P

HALO = 4
LANES = 128
BLOCK = 32
LGAMMA_HALF_THREE = 0.5 * math.log(math.pi) - math.log(2.0)
SINE = (
    3.1415926535897932,
    -5.1677127800499700,
    2.5501640398773455,
    -0.59926452932079211,
    0.082145886611128233,
    -0.0073704309457143504,
)


def fourier_kernel(waves, out, *, points):
    wave = waves[...].astype(jnp.float32)
    rows = wave.shape[0]
    turn = (lax.broadcasted_iota(jnp.int32, (rows, LANES), 0) % 2 * (points // 4)).astype(
        jnp.float32
    )
    lane = lax.broadcasted_iota(jnp.int32, (rows, LANES), 1)
    scale = 1.0 / math.sqrt(points)

    def tile(t, carry):
        column = (lane + t * LANES).astype(jnp.float32)
        phase = column * wave + turn
        phase = phase - jnp.floor(phase * (1.0 / points) + 0.5) * float(points)
        z = 0.5 - jnp.abs(phase) * (2.0 / points)
        square = z * z
        total = jnp.full_like(z, SINE[-1] * scale)
        for factor in SINE[-2::-1]:
            total = total * square + factor * scale
        start = pl.multiple_of(t * LANES, LANES)
        out[:, pl.ds(start, LANES)] = (total * z).astype(jnp.bfloat16)
        return carry

    lax.fori_loop(0, points // LANES, tile, 0)


def legendre_kernel(step_a, step_c, cosine, log_start, weight, out, stage, *, waves, band_rows):
    cos = cosine[...]
    start = log_start[...]
    scale = weight[...]

    def block(t, carry):
        current, last, log_scale = carry
        base = t * BLOCK
        size = jnp.exp(log_scale + start) * scale
        for u in range(BLOCK):
            stage[band_rows * u : band_rows * (u + 1), :] = current * size
            fresh = (step_a[base + u] * cos) * current - step_c[base + u] * last
            last = current
            current = fresh
        row = pl.multiple_of(base, BLOCK)
        for r in range(band_rows):
            out[pl.ds(row, BLOCK), r * LANES : (r + 1) * LANES] = stage[
                pl.ds(r, BLOCK, stride=band_rows), :
            ].astype(jnp.bfloat16)
        factor = jnp.maximum(jnp.maximum(jnp.abs(current), jnp.abs(last)), 1.0)
        inverse = 1.0 / factor
        return current * inverse, last * inverse, log_scale + jnp.log(factor)

    initial = (jnp.ones_like(cos), jnp.zeros_like(cos), jnp.zeros_like(cos))
    lax.fori_loop(0, waves // BLOCK, block, initial)


def arrival_kernel(
    field, north, south, west, east, departure, lat_weight, lon_weight, out, grid, shifted
):
    channels, rows, cols = field.shape
    tiles = cols // LANES
    copies = out.shape[0]
    stencil = 2 * HALO
    row_place = departure[...] // stencil
    col_place = departure[...] % stencil
    a = lat_weight[...]
    b = lon_weight[...]

    def spread(place, share):
        return [
            jnp.where(place == d, 1.0 - share, jnp.where(place == d - 1, share, 0.0))
            for d in range(stencil + 1)
        ]

    row_parts = spread(row_place, a)
    col_parts = spread(col_place, b)
    lane = lax.broadcasted_iota(jnp.int32, (rows + 2 * HALO, LANES), 1)
    for c in range(channels):
        grid[c, 0] = west[c].astype(jnp.float32)
        grid[c, tiles + 1] = east[c].astype(jnp.float32)
        up = north[c].astype(jnp.float32)
        mid = field[c].astype(jnp.float32)
        down = south[c].astype(jnp.float32)
        for t in range(tiles):
            span = slice(t * LANES, (t + 1) * LANES)
            grid[c, t + 1, 0:HALO, :] = up[:, span]
            grid[c, t + 1, HALO : HALO + rows, :] = mid[:, span]
            grid[c, t + 1, HALO + rows :, :] = down[:, span]

    def channel(c, carry):
        source = [grid[c, t] for t in range(tiles + 2)]
        for d in range(stencil + 1):
            move = d - HALO
            if move == 0:
                for t in range(tiles):
                    shifted[d, t] = source[t + 1]
                continue
            if move > 0:
                turned = [pltpu.roll(source[t], LANES - move, 1) for t in range(1, tiles + 2)]
                for t in range(tiles):
                    shifted[d, t] = jnp.where(lane < LANES - move, turned[t], turned[t + 1])
            else:
                turned = [pltpu.roll(source[t], -move, 1) for t in range(tiles + 1)]
                for t in range(tiles):
                    shifted[d, t] = jnp.where(lane < -move, turned[t], turned[t + 1])
        for t in range(tiles):
            span = slice(t * LANES, (t + 1) * LANES)
            total = None
            for e in range(stencil + 1):
                inner = None
                for d in range(stencil + 1):
                    term = col_parts[d][:, span] * shifted[d, t, e : e + rows, :]
                    inner = term if inner is None else inner + term
                term = row_parts[e][:, span] * inner
                total = term if total is None else total + term
            value = total.astype(jnp.bfloat16)
            for copy in range(copies):
                out[copy, c, :, span] = value
        return carry

    lax.fori_loop(0, channels, channel, 0)


def transform_kernel(cycles, fourier, waves, limits, out, gathered):
    sectors, channels, rows, cols = cycles.shape
    used = channels * rows
    gathered[used:, :] = jnp.zeros_like(gathered[used:, :])
    for sector in range(sectors):
        for c in range(channels):
            gathered[c * rows : (c + 1) * rows, sector * cols : (sector + 1) * cols] = cycles[
                sector, c
            ].astype(jnp.float32)
    spectrum = lax.dot_general(
        fourier[...],
        gathered[...].astype(jnp.bfloat16),
        (((1,), (1,)), ((), ())),
        preferred_element_type=jnp.float32,
    )
    out[...] = jnp.where(waves[...] < limits[...], spectrum, 0.0).astype(jnp.bfloat16)


def synthesis_kernel(order, data, functions, out, rows, turned, packed):
    channels, parts, waves = out.shape
    bands = data.shape[0] // parts
    band_rows = packed.shape[1] // LANES
    rows[parts * bands :, :] = jnp.zeros_like(rows[parts * bands :, :])
    rows[: parts * bands, :] = data[...].astype(jnp.float32)
    packed[...] = jnp.zeros_like(packed)
    step = packed.shape[0] // parts
    for e in range(parts):
        turned[e] = rows[pl.ds(e, LANES, stride=parts), :].T
        for r in range(band_rows):
            packed[e * step : e * step + channels, r * LANES : (r + 1) * LANES] = turned[
                e, pl.ds(r, channels, stride=band_rows), :
            ]
    result = lax.dot_general(
        packed[...].astype(jnp.bfloat16),
        functions[...],
        (((1,), (1,)), ((), ())),
        preferred_element_type=jnp.float32,
    )
    index = lax.broadcasted_iota(jnp.int32, (channels, waves), 1)
    inside = index < waves - order[0]
    for e in range(parts):
        out[:, e, :] = jnp.where(inside, result[e * step : e * step + channels, :], 0.0)


def legendre_inputs(order, bands, band_rows, waves, total_lat):
    spread = lax.optimization_barrier(jnp.broadcast_to(order, (band_rows, LANES)))
    order_real = spread.astype(jnp.float32)
    band = jnp.minimum(lax.broadcasted_iota(jnp.int32, (band_rows, LANES), 1), bands - 1)
    cycle = band * band_rows + lax.broadcasted_iota(jnp.int32, (band_rows, LANES), 0)
    angles = (cycle.astype(jnp.float32) + 0.5) * (math.pi / total_lat)
    sine = jnp.sin(angles)
    log_start = (
        0.5 * math.log(0.5)
        + 0.5 * (lax.lgamma(order_real + 1.5) - LGAMMA_HALF_THREE - lax.lgamma(order_real + 1.0))
        + order_real * jnp.log(sine)
    )
    order_real = order.astype(jnp.float32)
    degree = order_real + jnp.arange(1, waves + 1, dtype=jnp.int32).astype(jnp.float32)
    step_a = jnp.sqrt((4.0 * degree * degree - 1.0) / (degree * degree - order_real * order_real))
    before = degree - 1.0
    step_b = jnp.sqrt(
        jnp.maximum(
            (before * before - order_real * order_real) / (4.0 * before * before - 1.0), 0.0
        )
    )
    return (
        step_a,
        step_a * step_b,
        jnp.cos(angles),
        log_start,
        sine * (math.pi / math.sqrt(total_lat)),
    )


def smem():
    return pl.BlockSpec(memory_space=pltpu.SMEM)


def vmem():
    return pl.BlockSpec(memory_space=pltpu.VMEM)


def fourier_table(row_waves, points):
    return pl.pallas_call(
        functools.partial(fourier_kernel, points=points),
        out_shape=jax.ShapeDtypeStruct((row_waves.shape[0], points), jnp.bfloat16),
        in_specs=[vmem()],
        out_specs=vmem(),
        name="fourier",
    )(row_waves)


def legendre_table(order, bands, band_rows, waves):
    return pl.pallas_call(
        functools.partial(legendre_kernel, waves=waves, band_rows=band_rows),
        out_shape=jax.ShapeDtypeStruct((waves, band_rows * LANES), jnp.bfloat16),
        in_specs=[smem(), smem(), vmem(), vmem(), vmem()],
        out_specs=vmem(),
        scratch_shapes=[pltpu.VMEM((BLOCK * band_rows, LANES), jnp.float32)],
        name="legendre",
    )(*legendre_inputs(order, bands, band_rows, waves, bands * band_rows))


def interpolate(prognostic, north, south, west, east, departure, lat_weight, lon_weight, copies):
    channels, band_rows, sector_cols = prognostic.shape
    tall = band_rows + 2 * HALO
    tiles = sector_cols // LANES
    return pl.pallas_call(
        arrival_kernel,
        out_shape=jax.ShapeDtypeStruct((copies, channels, band_rows, sector_cols), jnp.bfloat16),
        in_specs=[vmem()] * 8,
        out_specs=vmem(),
        scratch_shapes=[
            pltpu.VMEM((channels, tiles + 2, tall, LANES), jnp.float32),
            pltpu.VMEM((2 * HALO + 1, tiles, tall, LANES), jnp.float32),
        ],
        name="arrival",
    )(prognostic, north, south, west, east, departure, lat_weight, lon_weight)


def transform(cycles, fourier, row_waves, limits):
    rows, points = fourier.shape
    return pl.pallas_call(
        transform_kernel,
        out_shape=jax.ShapeDtypeStruct((rows, LANES), jnp.bfloat16),
        in_specs=[vmem()] * 4,
        out_specs=vmem(),
        scratch_shapes=[pltpu.VMEM((LANES, points), jnp.float32)],
        name="transform",
    )(cycles, fourier, row_waves, limits)


def synthesize(order, data, functions, channels):
    waves, span = functions.shape
    return pl.pallas_call(
        synthesis_kernel,
        out_shape=jax.ShapeDtypeStruct((channels, 2, waves), jnp.float32),
        in_specs=[smem(), vmem(), vmem()],
        out_specs=vmem(),
        scratch_shapes=[
            pltpu.VMEM((2 * LANES, LANES), jnp.float32),
            pltpu.VMEM((2, LANES, LANES), jnp.float32),
            pltpu.VMEM((32, span), jnp.float32),
        ],
        name="synthesis",
    )(order, data, functions)


def shards(prognostic, departure, lat_weight, lon_weight, cycle_waves, wave_order):
    band_rows = prognostic.shape[1]
    bands = lax.axis_size("lat")
    sectors = lax.axis_size("lon")
    total_lon = prognostic.shape[2] * sectors
    waves = wave_order.shape[0]
    band_index = lax.axis_index("lat")
    sector_index = lax.axis_index("lon")

    north = lax.ppermute(
        prognostic[:, band_rows - HALO :, :], "lat", [(i, i + 1) for i in range(bands - 1)]
    )
    south = lax.ppermute(prognostic[:, :HALO, :], "lat", [(i + 1, i) for i in range(bands - 1)])

    slot_waves = wave_order.reshape(bands, sectors)
    own_waves = lax.dynamic_slice_in_dim(slot_waves, sector_index, 1, axis=1)
    row_waves = jnp.broadcast_to(own_waves[:, :, None], (bands, 2, LANES)).reshape(
        2 * bands, LANES
    )
    order = lax.dynamic_slice_in_dim(wave_order, band_index * sectors + sector_index, 1)
    limits = jnp.broadcast_to(
        cycle_waves[None, None, :], (1, LANES // band_rows, band_rows)
    ).reshape(1, LANES)
    fourier = fourier_table(row_waves, total_lon)
    functions = legendre_table(order, bands, band_rows, waves)

    tall_west = jnp.concatenate(
        [north[:, :, -LANES:], prognostic[:, :, -LANES:], south[:, :, -LANES:]], axis=1
    )
    tall_east = jnp.concatenate(
        [north[:, :, :LANES], prognostic[:, :, :LANES], south[:, :, :LANES]], axis=1
    )
    west = lax.ppermute(tall_west, "lon", [(i, (i + 1) % sectors) for i in range(sectors)])
    east = lax.ppermute(tall_east, "lon", [((i + 1) % sectors, i) for i in range(sectors)])
    arrival = interpolate(
        prognostic, north, south, west, east, departure, lat_weight, lon_weight, sectors
    )
    cycles = lax.all_to_all(arrival, "lon", split_axis=0, concat_axis=0, tiled=True)
    masked = transform(cycles, fourier, row_waves, limits)
    data = lax.all_to_all(
        masked.reshape(bands, 2, LANES), "lat", split_axis=0, concat_axis=0, tiled=True
    ).reshape(2 * bands, LANES)
    spectral = synthesize(order, data, functions, prognostic.shape[0])
    return spectral.transpose(1, 0, 2)[None]


def solution(mesh):
    in_specs = (
        P(None, "lat", "lon"),
        P("lat", "lon"),
        P("lat", "lon"),
        P("lat", "lon"),
        P("lat"),
        P(),
    )
    out_specs = P(("lat", "lon"), None, None, None)
    return jax.shard_map(shards, mesh=mesh, in_specs=in_specs, out_specs=out_specs, check_vma=False)
```

```python
import functools
import math

import jax
import jax.numpy as jnp
from jax import lax
from jax.experimental import pallas as pl
from jax.experimental.pallas import tpu as pltpu
from jax.sharding import PartitionSpec as P

HALO = 4
LANES = 128
BLOCK = 32
LGAMMA_HALF_THREE = 0.5 * math.log(math.pi) - math.log(2.0)
SINE = (
    3.1415926535897932,
    -5.1677127800499700,
    2.5501640398773455,
    -0.59926452932079211,
    0.082145886611128233,
    -0.0073704309457143504,
)


def fourier_kernel(waves, out, *, points):
    rows, group = waves.shape[0], 64
    scale = 1.0 / math.sqrt(points)
    row = lax.broadcasted_iota(jnp.int32, (group, LANES), 0)
    turn = (row % 2 * (points // 4)).astype(jnp.float32)
    lane = lax.broadcasted_iota(jnp.int32, (group, LANES), 1).astype(jnp.float32)

    def cosine(phase):
        phase = phase - jnp.floor(phase * (1.0 / points) + 0.5) * float(points)
        z = 0.5 - jnp.abs(phase) * (2.0 / points)
        square = z * z
        total = jnp.full_like(z, SINE[-1])
        for factor in SINE[-2::-1]:
            total = total * square + factor
        return total * z

    def block(g, carry):
        first = pl.multiple_of(g * group, group)
        wave = waves[pl.ds(first, group), :].astype(jnp.float32)
        phase = lane * wave + turn
        real = cosine(phase) * scale
        imag = cosine(phase - points / 4) * scale
        ahead = wave * float(LANES)
        turn_real = cosine(ahead)
        turn_imag = cosine(ahead - points / 4)
        for t in range(points // LANES):
            out[pl.ds(first, group), t * LANES : (t + 1) * LANES] = real.astype(jnp.bfloat16)
            real, imag = (
                real * turn_real - imag * turn_imag,
                imag * turn_real + real * turn_imag,
            )
        return carry

    lax.fori_loop(0, rows // group, block, 0)


def legendre_kernel(step_a, step_c, cosine, log_start, weight, out, stage, *, waves, band_rows):
    cos = cosine[...]
    start = log_start[...]
    scale = weight[...]

    def block(t, carry):
        current, last, log_scale = carry
        base = t * BLOCK
        size = jnp.exp(log_scale + start) * scale
        for u in range(BLOCK):
            stage[band_rows * u : band_rows * (u + 1), :] = current * size
            fresh = (step_a[base + u] * cos) * current - step_c[base + u] * last
            last = current
            current = fresh
        row = pl.multiple_of(base, BLOCK)
        for r in range(band_rows):
            out[pl.ds(row, BLOCK), r * LANES : (r + 1) * LANES] = stage[
                pl.ds(r, BLOCK, stride=band_rows), :
            ].astype(jnp.bfloat16)
        factor = jnp.maximum(jnp.maximum(jnp.abs(current), jnp.abs(last)), 1.0)
        inverse = 1.0 / factor
        return current * inverse, last * inverse, log_scale + jnp.log(factor)

    initial = (jnp.ones_like(cos), jnp.zeros_like(cos), jnp.zeros_like(cos))
    lax.fori_loop(0, waves // BLOCK, block, initial)


def arrival_kernel(
    field, north, south, west, east, departure, lat_weight, lon_weight, out, grid, shifted, stage
):
    channels, rows, cols = field.shape
    tiles = cols // LANES
    copies = out.shape[0]
    stencil = 2 * HALO
    row_place = departure[...] // stencil
    col_place = departure[...] % stencil
    a = lat_weight[...]
    b = lon_weight[...]

    def spread(place, share):
        return [
            jnp.where(place == d, 1.0 - share, jnp.where(place == d - 1, share, 0.0))
            for d in range(stencil + 1)
        ]

    row_parts = spread(row_place, a)
    col_parts = spread(col_place, b)
    lane = lax.broadcasted_iota(jnp.int32, (rows + 2 * HALO, LANES), 1)
    for c in range(channels):
        grid[c, 0] = west[c].astype(jnp.float32)[rows - HALO : 2 * rows + HALO]
        grid[c, tiles + 1] = east[c].astype(jnp.float32)[rows - HALO : 2 * rows + HALO]
        up = north[c].astype(jnp.float32)[rows - HALO :]
        mid = field[c].astype(jnp.float32)
        down = south[c].astype(jnp.float32)[:HALO]
        for t in range(tiles):
            span = slice(t * LANES, (t + 1) * LANES)
            grid[c, t + 1, 0:HALO, :] = up[:, span]
            grid[c, t + 1, HALO : HALO + rows, :] = mid[:, span]
            grid[c, t + 1, HALO + rows :, :] = down[:, span]

    def channel(c, carry):
        source = [grid[c, t] for t in range(tiles + 2)]
        for d in range(stencil + 1):
            move = d - HALO
            if move == 0:
                for t in range(tiles):
                    shifted[d, t] = source[t + 1]
                continue
            if move > 0:
                turned = [pltpu.roll(source[t], LANES - move, 1) for t in range(1, tiles + 2)]
                for t in range(tiles):
                    shifted[d, t] = jnp.where(lane < LANES - move, turned[t], turned[t + 1])
            else:
                turned = [pltpu.roll(source[t], -move, 1) for t in range(tiles + 1)]
                for t in range(tiles):
                    shifted[d, t] = jnp.where(lane < -move, turned[t], turned[t + 1])
        for t in range(tiles):
            span = slice(t * LANES, (t + 1) * LANES)
            total = None
            for e in range(stencil + 1):
                inner = None
                for d in range(stencil + 1):
                    term = col_parts[d][:, span] * shifted[d, t, e : e + rows, :]
                    inner = term if inner is None else inner + term
                term = row_parts[e][:, span] * inner
                total = term if total is None else total + term
            stage[pl.ds(pl.multiple_of(c * rows, rows), rows), span] = total
        return carry

    used = channels * rows
    stage[used:, :] = jnp.zeros_like(stage[used:, :])
    lax.fori_loop(0, channels, channel, 0)
    value = stage[...].astype(jnp.bfloat16)
    for copy in range(copies):
        out[copy] = value


def transform_kernel(cycles, fourier, waves, limits, out):
    sectors, used, _ = cycles.shape
    gathered = jnp.concatenate([cycles[sector] for sector in range(sectors)], axis=1)
    spectrum = lax.dot_general(
        fourier[...], gathered, (((1,), (1,)), ((), ())), preferred_element_type=jnp.float32
    )
    inside = waves[:, :used] < limits[:, :used]
    out[:, :used] = jnp.where(inside, spectrum, 0.0).astype(jnp.bfloat16)
    out[:, used:] = jnp.zeros((out.shape[0], out.shape[1] - used), jnp.bfloat16)


def synthesis_kernel(order, data, functions, out, rows, turned, packed):
    channels, parts, waves = out.shape
    bands = data.shape[0] // parts
    band_rows = packed.shape[1] // LANES
    rows[parts * bands :, :] = jnp.zeros_like(rows[parts * bands :, :])
    rows[: parts * bands, :] = data[...].astype(jnp.float32)
    packed[...] = jnp.zeros_like(packed)
    step = packed.shape[0] // parts
    for e in range(parts):
        turned[e] = rows[pl.ds(e, LANES, stride=parts), :].T
        for r in range(band_rows):
            packed[e * step : e * step + channels, r * LANES : (r + 1) * LANES] = turned[
                e, pl.ds(r, channels, stride=band_rows), :
            ]
    result = lax.dot_general(
        packed[...].astype(jnp.bfloat16),
        functions[...],
        (((1,), (1,)), ((), ())),
        preferred_element_type=jnp.float32,
    )
    index = lax.broadcasted_iota(jnp.int32, (channels, waves), 1)
    inside = index < waves - order[0]
    for e in range(parts):
        out[:, e, :] = jnp.where(inside, result[e * step : e * step + channels, :], 0.0)


def legendre_inputs(order, bands, band_rows, waves, total_lat):
    spread = lax.optimization_barrier(jnp.broadcast_to(order, (band_rows, LANES)))
    order_real = spread.astype(jnp.float32)
    band = jnp.minimum(lax.broadcasted_iota(jnp.int32, (band_rows, LANES), 1), bands - 1)
    cycle = band * band_rows + lax.broadcasted_iota(jnp.int32, (band_rows, LANES), 0)
    angles = (cycle.astype(jnp.float32) + 0.5) * (math.pi / total_lat)
    sine = jnp.sin(angles)
    log_start = (
        0.5 * math.log(0.5)
        + 0.5 * (lax.lgamma(order_real + 1.5) - LGAMMA_HALF_THREE - lax.lgamma(order_real + 1.0))
        + order_real * jnp.log(sine)
    )
    order_real = order.astype(jnp.float32)
    degree = order_real + jnp.arange(1, waves + 1, dtype=jnp.int32).astype(jnp.float32)
    step_a = jnp.sqrt((4.0 * degree * degree - 1.0) / (degree * degree - order_real * order_real))
    before = degree - 1.0
    step_b = jnp.sqrt(
        jnp.maximum(
            (before * before - order_real * order_real) / (4.0 * before * before - 1.0), 0.0
        )
    )
    return (
        step_a,
        step_a * step_b,
        jnp.cos(angles),
        log_start,
        sine * (math.pi / math.sqrt(total_lat)),
    )


def near(array):
    return pltpu.with_memory_space_constraint(array, pltpu.VMEM)


def smem():
    return pl.BlockSpec(memory_space=pltpu.SMEM)


def vmem():
    return pl.BlockSpec(memory_space=pltpu.VMEM)


def fourier_table(row_waves, points):
    return pl.pallas_call(
        functools.partial(fourier_kernel, points=points),
        out_shape=pltpu.VMEM((row_waves.shape[0], points), jnp.bfloat16),
        in_specs=[vmem()],
        out_specs=vmem(),
        name="fourier",
    )(near(row_waves))


def legendre_table(order, bands, band_rows, waves):
    step_a, step_c, *planes = legendre_inputs(order, bands, band_rows, waves, bands * band_rows)
    return pl.pallas_call(
        functools.partial(legendre_kernel, waves=waves, band_rows=band_rows),
        out_shape=pltpu.VMEM((waves, band_rows * LANES), jnp.bfloat16),
        in_specs=[smem(), smem(), vmem(), vmem(), vmem()],
        out_specs=vmem(),
        scratch_shapes=[pltpu.VMEM((BLOCK * band_rows, LANES), jnp.float32)],
        name="legendre",
    )(step_a, step_c, *map(near, planes))


def interpolate(prognostic, north, south, west, east, departure, lat_weight, lon_weight, copies):
    channels, band_rows, sector_cols = prognostic.shape
    tall = band_rows + 2 * HALO
    tiles = sector_cols // LANES
    used = -(-channels * band_rows // 16) * 16
    return pl.pallas_call(
        arrival_kernel,
        out_shape=pltpu.VMEM((copies, used, sector_cols), jnp.bfloat16),
        in_specs=[vmem()] * 8,
        out_specs=vmem(),
        scratch_shapes=[
            pltpu.VMEM((channels, tiles + 2, tall, LANES), jnp.float32),
            pltpu.VMEM((2 * HALO + 1, tiles, tall, LANES), jnp.float32),
            pltpu.VMEM((used, sector_cols), jnp.float32),
        ],
        name="arrival",
    )(prognostic, near(north), near(south), near(west), near(east), departure, lat_weight, lon_weight)


def transform(cycles, fourier, row_waves, limits):
    return pl.pallas_call(
        transform_kernel,
        out_shape=pltpu.VMEM((fourier.shape[0], LANES), jnp.bfloat16),
        in_specs=[vmem()] * 4,
        out_specs=vmem(),
        name="transform",
    )(near(cycles), near(fourier), near(row_waves), near(limits))


def synthesize(order, data, functions, channels):
    waves, span = functions.shape
    return pl.pallas_call(
        synthesis_kernel,
        out_shape=jax.ShapeDtypeStruct((channels, 2, waves), jnp.float32),
        in_specs=[smem(), vmem(), vmem()],
        out_specs=vmem(),
        scratch_shapes=[
            pltpu.VMEM((2 * LANES, LANES), jnp.float32),
            pltpu.VMEM((2, LANES, LANES), jnp.float32),
            pltpu.VMEM((32, span), jnp.float32),
        ],
        name="synthesis",
    )(order, near(data), near(functions))


def shards(prognostic, departure, lat_weight, lon_weight, cycle_waves, wave_order):
    band_rows = prognostic.shape[1]
    bands = lax.axis_size("lat")
    sectors = lax.axis_size("lon")
    total_lon = prognostic.shape[2] * sectors
    waves = wave_order.shape[0]
    band_index = lax.axis_index("lat")
    sector_index = lax.axis_index("lon")

    north = lax.ppermute(prognostic, "lat", [(i, i + 1) for i in range(bands - 1)])
    south = lax.ppermute(prognostic, "lat", [(i + 1, i) for i in range(bands - 1)])

    tall_west = jnp.concatenate(
        [north[:, :, -LANES:], prognostic[:, :, -LANES:], south[:, :, -LANES:]], axis=1
    )
    tall_east = jnp.concatenate(
        [north[:, :, :LANES], prognostic[:, :, :LANES], south[:, :, :LANES]], axis=1
    )
    west = lax.ppermute(tall_west, "lon", [(i, (i + 1) % sectors) for i in range(sectors)])
    east = lax.ppermute(tall_east, "lon", [((i + 1) % sectors, i) for i in range(sectors)])
    arrival = interpolate(
        prognostic, north, south, west, east, departure, lat_weight, lon_weight, sectors
    )
    arrival, wave_order, cycle_waves = lax.optimization_barrier((arrival, wave_order, cycle_waves))
    cycles = lax.all_to_all(arrival, "lon", split_axis=0, concat_axis=0, tiled=True)
    slot_waves = wave_order.reshape(bands, sectors)
    own_waves = lax.dynamic_slice_in_dim(slot_waves, sector_index, 1, axis=1)
    row_waves = jnp.broadcast_to(own_waves[:, :, None], (bands, 2, LANES)).reshape(
        2 * bands, LANES
    )
    order = lax.dynamic_slice_in_dim(wave_order, band_index * sectors + sector_index, 1)
    limits = jnp.broadcast_to(
        cycle_waves[None, None, :], (1, LANES // band_rows, band_rows)
    ).reshape(1, LANES)
    fourier = fourier_table(row_waves, total_lon)
    functions = legendre_table(order, bands, band_rows, waves)
    cycles, functions = lax.optimization_barrier((cycles, functions))
    masked = transform(cycles, fourier, row_waves, limits)
    data = lax.all_to_all(
        masked.reshape(bands, 2, LANES), "lat", split_axis=0, concat_axis=0, tiled=True
    ).reshape(2 * bands, LANES)
    spectral = synthesize(order, data, functions, prognostic.shape[0])
    return spectral.transpose(1, 0, 2)[None]


def solution(mesh):
    in_specs = (
        P(None, "lat", "lon"),
        P("lat", "lon"),
        P("lat", "lon"),
        P("lat", "lon"),
        P("lat"),
        P(),
    )
    out_specs = P(("lat", "lon"), None, None, None)
    return jax.shard_map(shards, mesh=mesh, in_specs=in_specs, out_specs=out_specs, check_vma=False)
```

```python
import functools
import math

import jax
import jax.numpy as jnp
from jax import lax
from jax.experimental import pallas as pl
from jax.experimental.pallas import tpu as pltpu
from jax.sharding import PartitionSpec as P

HALO = 4
LANES = 128
BLOCK = 32
WINDOW = 4 * HALO
LGAMMA_HALF_THREE = 0.5 * math.log(math.pi) - math.log(2.0)
SINE = (
    3.1415926535897932,
    -5.1677127800499700,
    2.5501640398773455,
    -0.59926452932079211,
    0.082145886611128233,
    -0.0073704309457143504,
)


def fourier_kernel(waves, out, *, points):
    rows, group = waves.shape[0], 64
    scale = 1.0 / math.sqrt(points)
    row = lax.broadcasted_iota(jnp.int32, (group, LANES), 0)
    turn = (row % 2 * (points // 4)).astype(jnp.float32)
    place = lax.broadcasted_iota(jnp.int32, (group, LANES), 1)
    lane = place.astype(jnp.float32)
    column = (
        (place // WINDOW + 1) * (points * WINDOW // LANES) - 2 * HALO + place % WINDOW
    ).astype(jnp.float32)

    def cosine(phase):
        phase = phase - jnp.floor(phase * (1.0 / points) + 0.5) * float(points)
        z = 0.5 - jnp.abs(phase) * (2.0 / points)
        square = z * z
        total = jnp.full_like(z, SINE[-1])
        for factor in SINE[-2::-1]:
            total = total * square + factor
        return total * z

    def block(g, carry):
        first = pl.multiple_of(g * group, group)
        wave = waves[pl.ds(first, group), :].astype(jnp.float32)
        phase = lane * wave + turn
        real = cosine(phase) * scale
        imag = cosine(phase - points / 4) * scale
        ahead = wave * float(LANES)
        turn_real = cosine(ahead)
        turn_imag = cosine(ahead - points / 4)
        for t in range(points // LANES):
            out[pl.ds(first, group), t * LANES : (t + 1) * LANES] = real.astype(jnp.bfloat16)
            real, imag = (
                real * turn_real - imag * turn_imag,
                imag * turn_real + real * turn_imag,
            )
        edge = cosine(column * wave + turn) * scale
        out[pl.ds(first, group), points : points + LANES] = edge.astype(jnp.bfloat16)
        return carry

    lax.fori_loop(0, rows // group, block, 0)


def legendre_kernel(step_a, step_c, cosine, log_start, weight, out, stage, *, waves, band_rows):
    cos = cosine[...]
    start = log_start[...]
    scale = weight[...]

    def block(t, carry):
        current, last, log_scale = carry
        base = t * BLOCK
        size = jnp.exp(log_scale + start) * scale
        for u in range(BLOCK):
            stage[band_rows * u : band_rows * (u + 1), :] = current * size
            fresh = (step_a[base + u] * cos) * current - step_c[base + u] * last
            last = current
            current = fresh
        row = pl.multiple_of(base, BLOCK)
        for r in range(band_rows):
            out[pl.ds(row, BLOCK), r * LANES : (r + 1) * LANES] = stage[
                pl.ds(r, BLOCK, stride=band_rows), :
            ].astype(jnp.bfloat16)
        factor = jnp.maximum(jnp.maximum(jnp.abs(current), jnp.abs(last)), 1.0)
        inverse = 1.0 / factor
        return current * inverse, last * inverse, log_scale + jnp.log(factor)

    initial = (jnp.ones_like(cos), jnp.zeros_like(cos), jnp.zeros_like(cos))
    lax.fori_loop(0, waves // BLOCK, block, initial)


def spread(place, share):
    return [
        jnp.where(place == d, 1.0 - share, jnp.where(place == d - 1, share, 0.0))
        for d in range(2 * HALO + 1)
    ]


def edges(tall, slot):
    lane = lax.broadcasted_iota(jnp.int32, tall[0].shape, 1)
    reach = 2 * HALO
    ends = jnp.where(
        lane < reach, tall[0], jnp.where(lane >= LANES - reach, tall[-1], jnp.zeros_like(tall[0]))
    )
    return pltpu.roll(ends, slot * WINDOW + reach, 1)


def stencil(read, write, row_parts, col_parts, tiles, rows):
    count = 2 * HALO + 1
    source = read()
    lane = lax.broadcasted_iota(jnp.int32, source[0].shape, 1)
    for d in range(count):
        move = d - HALO
        if move == 0:
            turned = source
        else:
            rolled = [pltpu.roll(tile, -move % LANES, 1) for tile in source]
            if tiles == 1:
                turned = rolled
            elif move > 0:
                turned = [
                    jnp.where(lane < LANES - move, rolled[t], rolled[(t + 1) % tiles])
                    for t in range(tiles)
                ]
            else:
                turned = [
                    jnp.where(lane < -move, rolled[t - 1], rolled[t]) for t in range(tiles)
                ]
        for t in range(tiles):
            write[d, t] = turned[t]
    sums = []
    for t in range(tiles):
        total = None
        for e in range(count):
            inner = None
            for d in range(count):
                term = col_parts(d, t) * write[d, t, e : e + rows, :]
                inner = term if inner is None else inner + term
            term = row_parts(e, t) * inner
            total = term if total is None else total + term
        sums.append(total)
    return sums


def split(value):
    high = value.astype(jnp.bfloat16).astype(jnp.float32)
    rest = value - high
    middle = rest.astype(jnp.bfloat16).astype(jnp.float32)
    return [high, middle, rest - middle]


def prepare_kernel(field, departure, lat_weight, lon_weight, field_out, parts, planes):
    cols = departure.shape[1]
    field_out[...] = field[...]
    cell = departure[...]
    a = lat_weight[...]
    b = lon_weight[...]
    for d, part in enumerate(spread(cell // (2 * HALO), a) + spread(cell % (2 * HALO), b)):
        parts[d] = part
    total = None
    for p, plane in enumerate([cell.astype(jnp.float32)] + split(a) + split(b)):
        tall = [plane[:, t * LANES : (t + 1) * LANES] for t in range(cols // LANES)]
        term = edges(tall, p + 1)
        total = term if total is None else total + term
    planes[...] = total


def arrival_kernel(sector, field, north, south, parts, planes, out, grid, shifted, stage):
    channels, rows, cols = field.shape
    tiles = cols // LANES
    count = 2 * HALO + 1
    used = channels * rows
    tall = rows + 2 * HALO
    lane = lax.broadcasted_iota(jnp.int32, (rows, LANES), 1)
    for c in range(channels):
        up = north[c].astype(jnp.float32)[rows - HALO :]
        mid = field[c].astype(jnp.float32)
        down = south[c].astype(jnp.float32)[:HALO]
        for t in range(tiles):
            span = slice(t * LANES, (t + 1) * LANES)
            grid[c, t, 0:HALO, :] = up[:, span]
            grid[c, t, HALO : HALO + rows, :] = mid[:, span]
            grid[c, t, HALO + rows :, :] = down[:, span]

    def part(first):
        return lambda d, t: parts[first + d, :, t * LANES : (t + 1) * LANES]

    def channel(c, carry):
        sums = stencil(
            lambda: [grid[c, t] for t in range(tiles)],
            shifted,
            part(0),
            part(count),
            tiles,
            rows,
        )
        sums[0] = jnp.where(lane < HALO, 0.0, sums[0])
        sums[-1] = jnp.where(lane >= LANES - HALO, 0.0, sums[-1])
        for t in range(tiles):
            span = slice(t * LANES, (t + 1) * LANES)
            stage[pl.ds(pl.multiple_of(c * rows, rows), rows), span] = sums[t]
        return carry

    lax.fori_loop(0, channels, channel, 0)
    slots = LANES // WINDOW
    turn = sector[0] * WINDOW
    for g in range(2):
        total = None
        for c in range(g * slots, min((g + 1) * slots, channels)):
            term = edges([grid[c, 0], grid[c, tiles - 1]], c - g * slots)
            total = term if total is None else total + term
        if g == 1:
            total = total + jnp.concatenate([planes[...], jnp.zeros_like(planes[...])], axis=0)
        stage[used : used + tall, g * LANES : (g + 1) * LANES] = pltpu.roll(total, turn, 1)
    stage[used : used + tall, 2 * LANES :] = jnp.zeros((tall, cols - 2 * LANES), jnp.float32)
    value = stage[...].astype(jnp.bfloat16)
    for copy in range(out.shape[0]):
        out[copy] = value


def transform_kernel(cycles, fourier, waves, limits, out, shifted, stage):
    sectors = cycles.shape[0]
    used, rows = stage.shape[0], shifted.shape[2] - 2 * HALO
    tall = rows + 2 * HALO
    channels = used // rows
    slots = LANES // WINDOW
    slot = lax.broadcasted_iota(jnp.int32, (tall, LANES), 1) // WINDOW
    inner = lax.broadcasted_iota(jnp.int32, (tall, LANES), 1) % WINDOW
    pieces = [
        [
            cycles[sector, used : used + tall, g * LANES : (g + 1) * LANES].astype(jnp.float32)
            for sector in range(sectors)
        ]
        for g in range(2)
    ]

    def window(index, height):
        g, c = divmod(index, slots)
        total = pieces[g][0][:height]
        for sector in range(1, sectors):
            total = jnp.where(
                slot[:height] == (c + sector) % slots, pieces[g][sector][:height], total
            )
        left = pltpu.roll(total, -c * WINDOW % LANES, 1) if c else total
        right = pltpu.roll(total, -(c + 1) * WINDOW % LANES, 1) if c + 1 < slots else total
        return jnp.where(inner[:height] < 2 * HALO, left, right)

    cell, *weights = [window(channels + p, rows) for p in range(7)]
    a = weights[0] + weights[1] + weights[2]
    b = weights[3] + weights[4] + weights[5]
    high = jnp.floor(cell * (1.0 / (2 * HALO)))
    row_parts = spread(high, a)
    col_parts = spread(cell - high * (2 * HALO), b)
    inside = (inner[:rows] >= HALO) & (inner[:rows] < 3 * HALO)
    for c in range(channels):
        (total,) = stencil(
            lambda: [window(c, tall)],
            shifted,
            lambda e, t: row_parts[e],
            lambda d, t: col_parts[d],
            1,
            rows,
        )
        stage[c * rows : (c + 1) * rows, :] = jnp.where(inside, total, 0.0)
    gathered = jnp.concatenate(
        [cycles[sector, :used, :] for sector in range(sectors)]
        + [stage[...].astype(jnp.bfloat16)],
        axis=1,
    )
    spectrum = lax.dot_general(
        fourier[...], gathered, (((1,), (1,)), ((), ())), preferred_element_type=jnp.float32
    )
    resolved = waves[:, :used] < limits[:, :used]
    out[:, :used] = jnp.where(resolved, spectrum, 0.0).astype(jnp.bfloat16)
    out[:, used:] = jnp.zeros((out.shape[0], out.shape[1] - used), jnp.bfloat16)


def synthesis_kernel(order, data, functions, out, rows, turned, packed):
    channels, parts, waves = out.shape
    bands = data.shape[0] // parts
    band_rows = packed.shape[1] // LANES
    rows[parts * bands :, :] = jnp.zeros_like(rows[parts * bands :, :])
    rows[: parts * bands, :] = data[...].astype(jnp.float32)
    packed[...] = jnp.zeros_like(packed)
    step = packed.shape[0] // parts
    for e in range(parts):
        turned[e] = rows[pl.ds(e, LANES, stride=parts), :].T
        for r in range(band_rows):
            packed[e * step : e * step + channels, r * LANES : (r + 1) * LANES] = turned[
                e, pl.ds(r, channels, stride=band_rows), :
            ]
    result = lax.dot_general(
        packed[...].astype(jnp.bfloat16),
        functions[...],
        (((1,), (1,)), ((), ())),
        preferred_element_type=jnp.float32,
    )
    index = lax.broadcasted_iota(jnp.int32, (channels, waves), 1)
    inside = index < waves - order[0]
    for e in range(parts):
        out[:, e, :] = jnp.where(inside, result[e * step : e * step + channels, :], 0.0)


def legendre_inputs(order, bands, band_rows, waves, total_lat):
    spread = lax.optimization_barrier(jnp.broadcast_to(order, (band_rows, LANES)))
    order_real = spread.astype(jnp.float32)
    band = jnp.minimum(lax.broadcasted_iota(jnp.int32, (band_rows, LANES), 1), bands - 1)
    cycle = band * band_rows + lax.broadcasted_iota(jnp.int32, (band_rows, LANES), 0)
    angles = (cycle.astype(jnp.float32) + 0.5) * (math.pi / total_lat)
    sine = jnp.sin(angles)
    log_start = (
        0.5 * math.log(0.5)
        + 0.5 * (lax.lgamma(order_real + 1.5) - LGAMMA_HALF_THREE - lax.lgamma(order_real + 1.0))
        + order_real * jnp.log(sine)
    )
    order_real = order.astype(jnp.float32)
    degree = order_real + jnp.arange(1, waves + 1, dtype=jnp.int32).astype(jnp.float32)
    step_a = jnp.sqrt((4.0 * degree * degree - 1.0) / (degree * degree - order_real * order_real))
    before = degree - 1.0
    step_b = jnp.sqrt(
        jnp.maximum(
            (before * before - order_real * order_real) / (4.0 * before * before - 1.0), 0.0
        )
    )
    return (
        step_a,
        step_a * step_b,
        jnp.cos(angles),
        log_start,
        sine * (math.pi / math.sqrt(total_lat)),
    )


def near(array):
    return pltpu.with_memory_space_constraint(array, pltpu.VMEM)


def smem():
    return pl.BlockSpec(memory_space=pltpu.SMEM)


def vmem():
    return pl.BlockSpec(memory_space=pltpu.VMEM)


def fourier_table(row_waves, points):
    return pl.pallas_call(
        functools.partial(fourier_kernel, points=points),
        out_shape=pltpu.VMEM((row_waves.shape[0], points + LANES), jnp.bfloat16),
        in_specs=[vmem()],
        out_specs=vmem(),
        name="fourier",
    )(near(row_waves))


def legendre_table(order, bands, band_rows, waves):
    step_a, step_c, *planes = legendre_inputs(order, bands, band_rows, waves, bands * band_rows)
    return pl.pallas_call(
        functools.partial(legendre_kernel, waves=waves, band_rows=band_rows),
        out_shape=pltpu.VMEM((waves, band_rows * LANES), jnp.bfloat16),
        in_specs=[smem(), smem(), vmem(), vmem(), vmem()],
        out_specs=vmem(),
        scratch_shapes=[pltpu.VMEM((BLOCK * band_rows, LANES), jnp.float32)],
        name="legendre",
    )(step_a, step_c, *map(near, planes))


def prepare(prognostic, departure, lat_weight, lon_weight):
    _, band_rows, sector_cols = prognostic.shape
    return pl.pallas_call(
        prepare_kernel,
        out_shape=(
            pltpu.VMEM(prognostic.shape, jnp.bfloat16),
            pltpu.VMEM((2 * (2 * HALO + 1), band_rows, sector_cols), jnp.float32),
            pltpu.VMEM((band_rows, LANES), jnp.float32),
        ),
        in_specs=[vmem()] * 4,
        out_specs=(vmem(),) * 3,
        name="prepare",
    )(prognostic, departure, lat_weight, lon_weight)


def interpolate(sector, field, north, south, parts, planes, copies):
    channels, band_rows, sector_cols = field.shape
    tall = band_rows + 2 * HALO
    tiles = sector_cols // LANES
    height = channels * band_rows + tall
    return pl.pallas_call(
        arrival_kernel,
        out_shape=pltpu.VMEM((copies, height, sector_cols), jnp.bfloat16),
        in_specs=[smem()] + [vmem()] * 5,
        out_specs=vmem(),
        scratch_shapes=[
            pltpu.VMEM((channels, tiles, tall, LANES), jnp.float32),
            pltpu.VMEM((2 * HALO + 1, tiles, tall, LANES), jnp.float32),
            pltpu.VMEM((height, sector_cols), jnp.float32),
        ],
        name="arrival",
    )(sector, *map(near, (field, north, south, parts, planes)))


def transform(cycles, fourier, row_waves, limits, channels, band_rows):
    return pl.pallas_call(
        transform_kernel,
        out_shape=pltpu.VMEM((fourier.shape[0], LANES), jnp.bfloat16),
        in_specs=[vmem()] * 4,
        out_specs=vmem(),
        scratch_shapes=[
            pltpu.VMEM((2 * HALO + 1, 1, band_rows + 2 * HALO, LANES), jnp.float32),
            pltpu.VMEM((channels * band_rows, LANES), jnp.float32),
        ],
        name="transform",
    )(*map(near, (cycles, fourier, row_waves, limits)))


def synthesize(order, data, functions, channels):
    waves, span = functions.shape
    return pl.pallas_call(
        synthesis_kernel,
        out_shape=jax.ShapeDtypeStruct((channels, 2, waves), jnp.float32),
        in_specs=[smem(), vmem(), vmem()],
        out_specs=vmem(),
        scratch_shapes=[
            pltpu.VMEM((2 * LANES, LANES), jnp.float32),
            pltpu.VMEM((2, LANES, LANES), jnp.float32),
            pltpu.VMEM((32, span), jnp.float32),
        ],
        name="synthesis",
    )(order, near(data), near(functions))


def shards(prognostic, departure, lat_weight, lon_weight, cycle_waves, wave_order):
    band_rows = prognostic.shape[1]
    bands = lax.axis_size("lat")
    sectors = lax.axis_size("lon")
    total_lon = prognostic.shape[2] * sectors
    waves = wave_order.shape[0]
    band_index = lax.axis_index("lat")
    sector_index = lax.axis_index("lon")

    north = lax.ppermute(prognostic, "lat", [(i, i + 1) for i in range(bands - 1)])
    south = lax.ppermute(prognostic, "lat", [(i + 1, i) for i in range(bands - 1)])

    field, parts, planes = prepare(prognostic, departure, lat_weight, lon_weight)
    arrival = interpolate(
        sector_index.astype(jnp.int32).reshape(1), field, north, south, parts, planes, sectors
    )
    cycles = lax.all_to_all(arrival, "lon", split_axis=0, concat_axis=0, tiled=True)

    slot_waves = wave_order.reshape(bands, sectors)
    own_waves = lax.dynamic_slice_in_dim(slot_waves, sector_index, 1, axis=1)
    row_waves = jnp.broadcast_to(own_waves[:, :, None], (bands, 2, LANES)).reshape(
        2 * bands, LANES
    )
    limits = jnp.broadcast_to(
        cycle_waves[None, None, :], (1, LANES // band_rows, band_rows)
    ).reshape(1, LANES)
    fourier = fourier_table(row_waves, total_lon)
    masked = transform(cycles, fourier, row_waves, limits, prognostic.shape[0], band_rows)
    data = lax.all_to_all(
        masked.reshape(bands, 2, LANES), "lat", split_axis=0, concat_axis=0, tiled=True
    ).reshape(2 * bands, LANES)
    order = lax.dynamic_slice_in_dim(wave_order, band_index * sectors + sector_index, 1)
    functions = legendre_table(order, bands, band_rows, waves)
    spectral = synthesize(order, data, functions, prognostic.shape[0])
    return spectral.transpose(1, 0, 2)[None]


def solution(mesh):
    in_specs = (
        P(None, "lat", "lon"),
        P("lat", "lon"),
        P("lat", "lon"),
        P("lat", "lon"),
        P("lat"),
        P(),
    )
    out_specs = P(("lat", "lon"), None, None, None)
    return jax.shard_map(shards, mesh=mesh, in_specs=in_specs, out_specs=out_specs, check_vma=False)
```

```python
import functools
import math

import jax
import jax.numpy as jnp
from jax import lax
from jax.experimental import pallas as pl
from jax.experimental.pallas import tpu as pltpu
from jax.sharding import PartitionSpec as P

HALO = 4
LANES = 128
BLOCK = 32
GRANT = 16 << 20
WINDOW = 4 * HALO
LGAMMA_HALF_THREE = 0.5 * math.log(math.pi) - math.log(2.0)
SINE = (
    3.1415926535897932,
    -5.1677127800499700,
    2.5501640398773455,
    -0.59926452932079211,
    0.082145886611128233,
    -0.0073704309457143504,
)


def fourier_kernel(waves, out, *, points):
    rows, group = waves.shape[0], 64
    scale = 1.0 / math.sqrt(points)
    row = lax.broadcasted_iota(jnp.int32, (group, LANES), 0)
    turn = (row % 2 * (points // 4)).astype(jnp.float32)
    place = lax.broadcasted_iota(jnp.int32, (group, LANES), 1)
    lane = place.astype(jnp.float32)
    column = (
        (place // WINDOW + 1) * (points * WINDOW // LANES) - 2 * HALO + place % WINDOW
    ).astype(jnp.float32)

    def cosine(phase):
        phase = phase - jnp.floor(phase * (1.0 / points) + 0.5) * float(points)
        z = 0.5 - jnp.abs(phase) * (2.0 / points)
        square = z * z
        total = jnp.full_like(z, SINE[-1])
        for factor in SINE[-2::-1]:
            total = total * square + factor
        return total * z

    def block(g, carry):
        first = pl.multiple_of(g * group, group)
        wave = waves[pl.ds(first, group), :].astype(jnp.float32)
        phase = lane * wave + turn
        real = cosine(phase) * scale
        imag = cosine(phase - points / 4) * scale
        ahead = wave * float(LANES)
        turn_real = cosine(ahead)
        turn_imag = cosine(ahead - points / 4)
        for t in range(points // LANES):
            out[pl.ds(first, group), t * LANES : (t + 1) * LANES] = real.astype(jnp.bfloat16)
            real, imag = (
                real * turn_real - imag * turn_imag,
                imag * turn_real + real * turn_imag,
            )
        edge = cosine(column * wave + turn) * scale
        out[pl.ds(first, group), points : points + LANES] = edge.astype(jnp.bfloat16)
        return carry

    lax.fori_loop(0, rows // group, block, 0)


def legendre_kernel(step_a, step_c, cosine, log_start, weight, out, stage, *, waves, band_rows):
    cos = cosine[...]
    start = log_start[...]
    scale = weight[...]

    def block(t, carry):
        current, last, log_scale = carry
        base = t * BLOCK
        size = jnp.exp(log_scale + start) * scale
        for u in range(BLOCK):
            stage[band_rows * u : band_rows * (u + 1), :] = current * size
            fresh = (step_a[base + u] * cos) * current - step_c[base + u] * last
            last = current
            current = fresh
        row = pl.multiple_of(base, BLOCK)
        for r in range(band_rows // 2):
            out[pl.ds(row, BLOCK), r * LANES : (r + 1) * LANES] = stage[
                pl.ds(r, BLOCK, stride=band_rows), :
            ].astype(jnp.bfloat16)
        factor = jnp.maximum(jnp.maximum(jnp.abs(current), jnp.abs(last)), 1.0)
        inverse = 1.0 / factor
        return current * inverse, last * inverse, log_scale + jnp.log(factor)

    initial = (jnp.ones_like(cos), jnp.zeros_like(cos), jnp.zeros_like(cos))
    lax.fori_loop(0, waves // BLOCK, block, initial)


def spread(place, share):
    return [
        jnp.where(place == d, 1.0 - share, jnp.where(place == d - 1, share, 0.0))
        for d in range(2 * HALO + 1)
    ]


def edges(tall, slot):
    lane = lax.broadcasted_iota(jnp.int32, tall[0].shape, 1)
    reach = 2 * HALO
    ends = jnp.where(
        lane < reach, tall[0], jnp.where(lane >= LANES - reach, tall[-1], jnp.zeros_like(tall[0]))
    )
    return pltpu.roll(ends, slot * WINDOW + reach, 1)


def stencil(read, write, row_parts, col_parts, tiles, rows):
    count = 2 * HALO + 1
    source = read()
    lane = lax.broadcasted_iota(jnp.int32, source[0].shape, 1)
    for d in range(count):
        move = d - HALO
        if move == 0:
            turned = source
        else:
            rolled = [pltpu.roll(tile, -move % LANES, 1) for tile in source]
            if tiles == 1:
                turned = rolled
            elif move > 0:
                turned = [
                    jnp.where(lane < LANES - move, rolled[t], rolled[(t + 1) % tiles])
                    for t in range(tiles)
                ]
            else:
                turned = [
                    jnp.where(lane < -move, rolled[t - 1], rolled[t]) for t in range(tiles)
                ]
        for t in range(tiles):
            write[d, t] = turned[t]
    sums = []
    for t in range(tiles):
        total = None
        for e in range(count):
            inner = None
            for d in range(count):
                term = col_parts(d, t) * write[d, t, e : e + rows, :]
                inner = term if inner is None else inner + term
            term = row_parts(e, t) * inner
            total = term if total is None else total + term
        sums.append(total)
    return sums


def split(value):
    high = value.astype(jnp.bfloat16).astype(jnp.float32)
    rest = value - high
    middle = rest.astype(jnp.bfloat16).astype(jnp.float32)
    return [high, middle, rest - middle]


def prepare_kernel(field, departure, lat_weight, lon_weight, field_out, parts, planes):
    cols = departure.shape[1]
    field_out[...] = field[...]
    cell = departure[...]
    a = lat_weight[...]
    b = lon_weight[...]
    for d, part in enumerate(spread(cell // (2 * HALO), a) + spread(cell % (2 * HALO), b)):
        parts[d] = part
    total = None
    for p, plane in enumerate([cell.astype(jnp.float32)] + split(a) + split(b)):
        tall = [plane[:, t * LANES : (t + 1) * LANES] for t in range(cols // LANES)]
        term = edges(tall, p + 1)
        total = term if total is None else total + term
    planes[...] = total


def arrival_kernel(sector, field, north, south, parts, planes, out, grid, shifted, stage):
    channels, rows, cols = field.shape
    tiles = cols // LANES
    count = 2 * HALO + 1
    used = channels * rows
    tall = rows + 2 * HALO
    lane = lax.broadcasted_iota(jnp.int32, (rows, LANES), 1)
    for c in range(channels):
        up = north[c].astype(jnp.float32)[rows - HALO :]
        mid = field[c].astype(jnp.float32)
        down = south[c].astype(jnp.float32)[:HALO]
        for t in range(tiles):
            span = slice(t * LANES, (t + 1) * LANES)
            grid[c, t, 0:HALO, :] = up[:, span]
            grid[c, t, HALO : HALO + rows, :] = mid[:, span]
            grid[c, t, HALO + rows :, :] = down[:, span]

    def part(first):
        return lambda d, t: parts[first + d, :, t * LANES : (t + 1) * LANES]

    def channel(c, carry):
        sums = stencil(
            lambda: [grid[c, t] for t in range(tiles)],
            shifted,
            part(0),
            part(count),
            tiles,
            rows,
        )
        sums[0] = jnp.where(lane < HALO, 0.0, sums[0])
        sums[-1] = jnp.where(lane >= LANES - HALO, 0.0, sums[-1])
        for t in range(tiles):
            span = slice(t * LANES, (t + 1) * LANES)
            stage[pl.ds(pl.multiple_of(c * rows, rows), rows), span] = sums[t]
        return carry

    lax.fori_loop(0, channels, channel, 0)
    slots = LANES // WINDOW
    turn = sector[0] * WINDOW
    for g in range(2):
        total = None
        for c in range(g * slots, min((g + 1) * slots, channels)):
            term = edges([grid[c, 0], grid[c, tiles - 1]], c - g * slots)
            total = term if total is None else total + term
        if g == 1:
            total = total + jnp.concatenate([planes[...], jnp.zeros_like(planes[...])], axis=0)
        stage[used : used + tall, g * LANES : (g + 1) * LANES] = pltpu.roll(total, turn, 1)
    stage[used : used + tall, 2 * LANES :] = jnp.zeros((tall, cols - 2 * LANES), jnp.float32)
    value = stage[...].astype(jnp.bfloat16)
    for copy in range(out.shape[0]):
        out[copy] = value


def transform_kernel(cycles, fourier, waves, limits, out, shifted, stage):
    sectors = cycles.shape[0]
    used, rows = stage.shape[0], shifted.shape[2] - 2 * HALO
    tall = rows + 2 * HALO
    channels = used // rows
    slots = LANES // WINDOW
    slot = lax.broadcasted_iota(jnp.int32, (tall, LANES), 1) // WINDOW
    inner = lax.broadcasted_iota(jnp.int32, (tall, LANES), 1) % WINDOW
    pieces = [
        [
            cycles[sector, used : used + tall, g * LANES : (g + 1) * LANES].astype(jnp.float32)
            for sector in range(sectors)
        ]
        for g in range(2)
    ]

    def window(index, height):
        g, c = divmod(index, slots)
        total = pieces[g][0][:height]
        for sector in range(1, sectors):
            total = jnp.where(
                slot[:height] == (c + sector) % slots, pieces[g][sector][:height], total
            )
        left = pltpu.roll(total, -c * WINDOW % LANES, 1) if c else total
        right = pltpu.roll(total, -(c + 1) * WINDOW % LANES, 1) if c + 1 < slots else total
        return jnp.where(inner[:height] < 2 * HALO, left, right)

    cell, *weights = [window(channels + p, rows) for p in range(7)]
    a = weights[0] + weights[1] + weights[2]
    b = weights[3] + weights[4] + weights[5]
    high = jnp.floor(cell * (1.0 / (2 * HALO)))
    row_parts = spread(high, a)
    col_parts = spread(cell - high * (2 * HALO), b)
    inside = (inner[:rows] >= HALO) & (inner[:rows] < 3 * HALO)
    for c in range(channels):
        (total,) = stencil(
            lambda: [window(c, tall)],
            shifted,
            lambda e, t: row_parts[e],
            lambda d, t: col_parts[d],
            1,
            rows,
        )
        stage[c * rows : (c + 1) * rows, :] = jnp.where(inside, total, 0.0)
    gathered = jnp.concatenate(
        [cycles[sector, :used, :] for sector in range(sectors)]
        + [stage[...].astype(jnp.bfloat16)],
        axis=1,
    )
    spectrum = lax.dot_general(
        fourier[...], gathered, (((1,), (1,)), ((), ())), preferred_element_type=jnp.float32
    )
    resolved = waves[:, :used] < limits[:, :used]
    out[:, :used] = jnp.where(resolved, spectrum, 0.0).astype(jnp.bfloat16)
    out[:, used:] = jnp.zeros((out.shape[0], out.shape[1] - used), jnp.bfloat16)


def synthesis_kernel(data, functions, out, turned, packed):
    channels, parts, waves = out.shape
    bands = data.shape[0] // parts
    kept = packed.shape[1] // LANES
    band_rows = 2 * kept
    source = lax.broadcasted_iota(jnp.int32, (parts * bands, LANES), 0)
    target = lax.broadcasted_iota(jnp.int32, (parts * bands, LANES), 1)
    chosen = [
        (source == parts * band + e).astype(jnp.float32).astype(jnp.bfloat16)
        for band in (target, bands - 1 - target)
        for e in range(parts)
    ]
    columns = lax.dot_general(
        data[...],
        jnp.concatenate(chosen, axis=1),
        (((0,), (0,)), ((), ())),
        preferred_element_type=jnp.float32,
    )
    for place in range(2 * parts):
        turned[place] = columns[:, place * LANES : (place + 1) * LANES]
    packed[...] = jnp.zeros_like(packed)
    step = packed.shape[0] // (2 * parts)
    for mirror in range(2):
        for e in range(parts):
            first = (mirror * parts + e) * step
            for r in range(kept):
                row = band_rows - 1 - r if mirror else r
                packed[first : first + channels, r * LANES : (r + 1) * LANES] = turned[
                    mirror * parts + e, pl.ds(row, channels, stride=band_rows), :
                ]
    result = lax.dot_general(
        packed[...].astype(jnp.bfloat16),
        functions[...],
        (((1,), (1,)), ((), ())),
        preferred_element_type=jnp.float32,
    )
    even = lax.broadcasted_iota(jnp.int32, (channels, waves), 1) % 2 == 0
    for e in range(parts):
        near_half = result[e * step : e * step + channels, :]
        far_half = result[(parts + e) * step : (parts + e) * step + channels, :]
        out[:, e, :] = near_half + jnp.where(even, far_half, -far_half)


def legendre_inputs(order, bands, band_rows, waves, total_lat):
    spread = lax.optimization_barrier(jnp.broadcast_to(order, (band_rows, LANES)))
    order_real = spread.astype(jnp.float32)
    band = jnp.minimum(lax.broadcasted_iota(jnp.int32, (band_rows, LANES), 1), bands - 1)
    cycle = band * band_rows + lax.broadcasted_iota(jnp.int32, (band_rows, LANES), 0)
    angles = (cycle.astype(jnp.float32) + 0.5) * (math.pi / total_lat)
    sine = jnp.sin(angles)
    log_start = (
        0.5 * math.log(0.5)
        + 0.5 * (lax.lgamma(order_real + 1.5) - LGAMMA_HALF_THREE - lax.lgamma(order_real + 1.0))
        + order_real * jnp.log(sine)
    )
    order_real = order.astype(jnp.float32)
    degree = order_real + jnp.arange(1, waves + 1, dtype=jnp.int32).astype(jnp.float32)
    step_a = jnp.sqrt((4.0 * degree * degree - 1.0) / (degree * degree - order_real * order_real))
    before = degree - 1.0
    step_b = jnp.sqrt(
        jnp.maximum(
            (before * before - order_real * order_real) / (4.0 * before * before - 1.0), 0.0
        )
    )
    inside = jnp.arange(1, waves + 1, dtype=jnp.int32) < waves - order
    return (
        jnp.where(inside, step_a, 0.0),
        jnp.where(inside, step_a * step_b, 0.0),
        jnp.cos(angles),
        log_start,
        sine * (math.pi / math.sqrt(total_lat)),
    )


def near(array):
    return pltpu.with_memory_space_constraint(array, pltpu.VMEM)


def smem():
    return pl.BlockSpec(memory_space=pltpu.SMEM)


def vmem():
    return pl.BlockSpec(memory_space=pltpu.VMEM)


def fourier_table(row_waves, points):
    return pl.pallas_call(
        functools.partial(fourier_kernel, points=points),
        out_shape=pltpu.VMEM((row_waves.shape[0], points + LANES), jnp.bfloat16),
        in_specs=[vmem()],
        out_specs=vmem(),
        name="fourier",
        compiler_params=pltpu.CompilerParams(vmem_limit_bytes=GRANT),
    )(near(row_waves))


def legendre_table(order, bands, band_rows, waves):
    step_a, step_c, *planes = legendre_inputs(order, bands, band_rows, waves, bands * band_rows)
    return pl.pallas_call(
        functools.partial(legendre_kernel, waves=waves, band_rows=band_rows),
        out_shape=pltpu.VMEM((waves, band_rows // 2 * LANES), jnp.bfloat16),
        in_specs=[smem(), smem(), vmem(), vmem(), vmem()],
        out_specs=vmem(),
        scratch_shapes=[pltpu.VMEM((BLOCK * band_rows, LANES), jnp.float32)],
        name="legendre",
        compiler_params=pltpu.CompilerParams(vmem_limit_bytes=GRANT),
    )(step_a, step_c, *map(near, planes))


def prepare(prognostic, departure, lat_weight, lon_weight):
    _, band_rows, sector_cols = prognostic.shape
    return pl.pallas_call(
        prepare_kernel,
        out_shape=(
            pltpu.VMEM(prognostic.shape, jnp.bfloat16),
            pltpu.VMEM((2 * (2 * HALO + 1), band_rows, sector_cols), jnp.float32),
            pltpu.VMEM((band_rows, LANES), jnp.float32),
        ),
        in_specs=[vmem()] * 4,
        out_specs=(vmem(),) * 3,
        name="prepare",
    )(prognostic, departure, lat_weight, lon_weight)


def interpolate(sector, field, north, south, parts, planes, copies):
    channels, band_rows, sector_cols = field.shape
    tall = band_rows + 2 * HALO
    tiles = sector_cols // LANES
    height = channels * band_rows + tall
    return pl.pallas_call(
        arrival_kernel,
        out_shape=pltpu.VMEM((copies, height, sector_cols), jnp.bfloat16),
        in_specs=[smem()] + [vmem()] * 5,
        out_specs=vmem(),
        scratch_shapes=[
            pltpu.VMEM((channels, tiles, tall, LANES), jnp.float32),
            pltpu.VMEM((2 * HALO + 1, tiles, tall, LANES), jnp.float32),
            pltpu.VMEM((height, sector_cols), jnp.float32),
        ],
        name="arrival",
    )(sector, *map(near, (field, north, south, parts, planes)))


def transform(cycles, fourier, row_waves, limits, channels, band_rows):
    return pl.pallas_call(
        transform_kernel,
        out_shape=pltpu.VMEM((fourier.shape[0], LANES), jnp.bfloat16),
        in_specs=[vmem()] * 4,
        out_specs=vmem(),
        scratch_shapes=[
            pltpu.VMEM((2 * HALO + 1, 1, band_rows + 2 * HALO, LANES), jnp.float32),
            pltpu.VMEM((channels * band_rows, LANES), jnp.float32),
        ],
        name="transform",
        compiler_params=pltpu.CompilerParams(vmem_limit_bytes=GRANT),
    )(*map(near, (cycles, fourier, row_waves, limits)))


def synthesize(data, functions, channels):
    waves, span = functions.shape
    return pl.pallas_call(
        synthesis_kernel,
        out_shape=jax.ShapeDtypeStruct((channels, 2, waves), jnp.float32),
        in_specs=[vmem()] * 2,
        out_specs=vmem(),
        scratch_shapes=[
            pltpu.VMEM((4, LANES, LANES), jnp.float32),
            pltpu.VMEM((64, span), jnp.float32),
        ],
        name="synthesis",
        compiler_params=pltpu.CompilerParams(vmem_limit_bytes=GRANT),
    )(near(data), near(functions))


def shards(prognostic, departure, lat_weight, lon_weight, cycle_waves, wave_order):
    band_rows = prognostic.shape[1]
    bands = lax.axis_size("lat")
    sectors = lax.axis_size("lon")
    total_lon = prognostic.shape[2] * sectors
    waves = wave_order.shape[0]
    band_index = lax.axis_index("lat")
    sector_index = lax.axis_index("lon")

    north = lax.ppermute(prognostic, "lat", [(i, i + 1) for i in range(bands - 1)])
    south = lax.ppermute(prognostic, "lat", [(i + 1, i) for i in range(bands - 1)])

    field, parts, planes = prepare(prognostic, departure, lat_weight, lon_weight)
    arrival = interpolate(
        sector_index.astype(jnp.int32).reshape(1), field, north, south, parts, planes, sectors
    )
    cycles = lax.all_to_all(arrival, "lon", split_axis=0, concat_axis=0, tiled=True)

    slot_waves = wave_order.reshape(bands, sectors)
    own_waves = lax.dynamic_slice_in_dim(slot_waves, sector_index, 1, axis=1)
    row_waves = jnp.broadcast_to(own_waves[:, :, None], (bands, 2, LANES)).reshape(
        2 * bands, LANES
    )
    limits = jnp.broadcast_to(
        cycle_waves[None, None, :], (1, LANES // band_rows, band_rows)
    ).reshape(1, LANES)
    fourier = fourier_table(row_waves, total_lon)
    order = lax.dynamic_slice_in_dim(wave_order, band_index * sectors + sector_index, 1)
    functions = legendre_table(order, bands, band_rows, waves)
    cycles, functions = lax.optimization_barrier((cycles, functions))
    masked = transform(cycles, fourier, row_waves, limits, prognostic.shape[0], band_rows)
    data = lax.all_to_all(
        masked.reshape(bands, 2, LANES), "lat", split_axis=0, concat_axis=0, tiled=True
    ).reshape(2 * bands, LANES)
    spectral = synthesize(data, functions, prognostic.shape[0])
    return spectral.transpose(1, 0, 2)[None]


def solution(mesh):
    in_specs = (
        P(None, "lat", "lon"),
        P("lat", "lon"),
        P("lat", "lon"),
        P("lat", "lon"),
        P("lat"),
        P(),
    )
    out_specs = P(("lat", "lon"), None, None, None)
    return jax.shard_map(shards, mesh=mesh, in_specs=in_specs, out_specs=out_specs, check_vma=False)
```

```python
import functools
import math

import jax
import jax.numpy as jnp
from jax import lax
from jax.experimental import pallas as pl
from jax.experimental.pallas import tpu as pltpu
from jax.sharding import PartitionSpec as P

HALO = 4
LANES = 128
BLOCK = 32
GRANT = 16 << 20
WINDOW = 4 * HALO
LGAMMA_HALF_THREE = 0.5 * math.log(math.pi) - math.log(2.0)
SINE = (
    3.1415926535897932,
    -5.1677127800499700,
    2.5501640398773455,
    -0.59926452932079211,
    0.082145886611128233,
    -0.0073704309457143504,
)


def fourier_kernel(waves, limits, following, out, bound, line, *, points):
    rows, group = waves.shape[0], 64
    scale = 1.0 / math.sqrt(points)
    row = lax.broadcasted_iota(jnp.int32, (group, LANES), 0)
    turn = (row % 2 * (points // 4)).astype(jnp.float32)
    place = lax.broadcasted_iota(jnp.int32, (group, LANES), 1)
    lane = place.astype(jnp.float32)
    column = (
        (place // WINDOW + 1) * (points * WINDOW // LANES) - 2 * HALO + place % WINDOW
    ).astype(jnp.float32)

    def cosine(phase):
        phase = phase - jnp.floor(phase * (1.0 / points) + 0.5) * float(points)
        z = 0.5 - jnp.abs(phase) * (2.0 / points)
        square = z * z
        total = jnp.full_like(z, SINE[-1])
        for factor in SINE[-2::-1]:
            total = total * square + factor
        return total * z

    def block(g, carry):
        first = pl.multiple_of(g * group, group)
        wave = waves[pl.ds(first, group), :].astype(jnp.float32)
        phase = lane * wave + turn
        real = cosine(phase) * scale
        imag = cosine(phase - points / 4) * scale
        ahead = wave * float(LANES)
        turn_real = cosine(ahead)
        turn_imag = cosine(ahead - points / 4)
        for t in range(points // LANES):
            out[pl.ds(first, group), t * LANES : (t + 1) * LANES] = real.astype(jnp.bfloat16)
            real, imag = (
                real * turn_real - imag * turn_imag,
                imag * turn_real + real * turn_imag,
            )
        edge = cosine(column * wave + turn) * scale
        out[pl.ds(first, group), points : points + LANES] = edge.astype(jnp.bfloat16)
        return carry

    lax.fori_loop(0, rows // group, block, 0)

    band_rows = limits.shape[1]
    line[...] = jnp.zeros_like(line)
    line[:1, :band_rows] = limits[...].astype(jnp.float32)
    own = line[...]
    last = following[following.shape[0] - 1].astype(jnp.float32)
    ahead = last[:, :LANES] * 256.0 + last[:, LANES : 2 * LANES]
    width = band_rows
    while width < LANES:
        own = own + pltpu.roll(own, width, 1)
        ahead = ahead + pltpu.roll(ahead, width, 1)
        width *= 2
    bound[...] = jnp.where(
        place[:1] % band_rows < HALO,
        pltpu.roll(own, LANES - HALO, 1)[:1],
        pltpu.roll(ahead, HALO, 1)[HALO : HALO + 1],
    )


def legendre_kernel(step_a, step_c, cosine, log_start, weight, out, stage, *, waves, band_rows):
    cos = cosine[...]
    start = log_start[...]
    scale = weight[...]

    def block(t, carry):
        current, last, log_scale = carry
        base = t * BLOCK
        size = jnp.exp(log_scale + start) * scale
        for u in range(BLOCK):
            stage[band_rows * u : band_rows * (u + 1), :] = current * size
            fresh = (step_a[base + u] * cos) * current - step_c[base + u] * last
            last = current
            current = fresh
        row = pl.multiple_of(base, BLOCK)
        for r in range(band_rows // 2):
            out[pl.ds(row, BLOCK), r * LANES : (r + 1) * LANES] = stage[
                pl.ds(r, BLOCK, stride=band_rows), :
            ].astype(jnp.bfloat16)
        factor = jnp.maximum(jnp.maximum(jnp.abs(current), jnp.abs(last)), 1.0)
        inverse = 1.0 / factor
        return current * inverse, last * inverse, log_scale + jnp.log(factor)

    initial = (jnp.ones_like(cos), jnp.zeros_like(cos), jnp.zeros_like(cos))
    lax.fori_loop(0, waves // BLOCK, block, initial)


def spread(place, share):
    return [
        jnp.where(place == d, 1.0 - share, jnp.where(place == d - 1, share, 0.0))
        for d in range(2 * HALO + 1)
    ]


def edges(tall, slot):
    lane = lax.broadcasted_iota(jnp.int32, tall[0].shape, 1)
    reach = 2 * HALO
    ends = jnp.where(
        lane < reach, tall[0], jnp.where(lane >= LANES - reach, tall[-1], jnp.zeros_like(tall[0]))
    )
    return pltpu.roll(ends, slot * WINDOW + reach, 1)


def stencil(read, write, row_parts, col_parts, tiles, rows):
    count = 2 * HALO + 1
    source = read()
    lane = lax.broadcasted_iota(jnp.int32, source[0].shape, 1)
    for d in range(count):
        move = d - HALO
        if move == 0:
            turned = source
        else:
            rolled = [pltpu.roll(tile, -move % LANES, 1) for tile in source]
            if tiles == 1:
                turned = rolled
            elif move > 0:
                turned = [
                    jnp.where(lane < LANES - move, rolled[t], rolled[(t + 1) % tiles])
                    for t in range(tiles)
                ]
            else:
                turned = [
                    jnp.where(lane < -move, rolled[t - 1], rolled[t]) for t in range(tiles)
                ]
        for t in range(tiles):
            write[d, t] = turned[t]
    sums = []
    for t in range(tiles):
        total = None
        for e in range(count):
            inner = None
            for d in range(count):
                term = col_parts(d, t) * write[d, t, e : e + rows, :]
                inner = term if inner is None else inner + term
            term = row_parts(e, t) * inner
            total = term if total is None else total + term
        sums.append(total)
    return sums


def split(value):
    high = value.astype(jnp.bfloat16).astype(jnp.float32)
    rest = value - high
    middle = rest.astype(jnp.bfloat16).astype(jnp.float32)
    return [high, middle, rest - middle]


def pack_kernel(limits, field, departure, lat_weight, lon_weight, out, field_out, own, line):
    channels = field.shape[0]
    cols = departure.shape[1]
    value = field[...]
    field_out[...] = value
    out[:channels] = value
    cell = departure[...].astype(jnp.float32)
    a = lat_weight[...]
    b = lon_weight[...]
    for p, plane in enumerate((cell, a, b)):
        own[p] = plane
    planes = [v[:HALO] for v in [cell] + split(a) + split(b)]
    for p in range(0, len(planes) - 1, 2):
        pair = jnp.concatenate(planes[p : p + 2], axis=0)
        out[channels + p // 2] = pair.astype(jnp.bfloat16)
    rows = limits.shape[1]
    bound = limits[...].astype(jnp.float32)
    high = jnp.floor(bound * (1.0 / 256.0))
    line[:HALO] = planes[-1]
    line[HALO:] = jnp.zeros_like(planes[-1])
    line[HALO : HALO + 1, :rows] = high
    line[HALO : HALO + 1, LANES : LANES + rows] = bound - high * 256.0
    out[channels + len(planes) // 2] = line[...].astype(jnp.bfloat16)


def arrival_kernel(place, field, own, following, out, grid, shifted, parts, stage):
    channels, rows, cols = field.shape
    tiles = cols // LANES
    count = 2 * HALO + 1
    used = channels * rows
    tall = rows + 2 * HALO
    lane = lax.broadcasted_iota(jnp.int32, (rows, LANES), 1)
    row = lax.broadcasted_iota(jnp.int32, (rows, cols), 0)
    last = jnp.concatenate([place[3]] * tiles, axis=1)
    pairs = [following[channels + p].astype(jnp.float32) for p in range(4)]
    ahead = [pairs[p // 2][p % 2 * HALO : (p % 2 + 1) * HALO] for p in range(7)]

    def rows_of(plane, rest):
        return jnp.concatenate([plane[HALO:], rest], axis=0)

    cell = rows_of(own[0], ahead[0])
    a = rows_of(own[1], ahead[1] + ahead[2] + ahead[3])
    b = rows_of(own[2], ahead[4] + ahead[5] + ahead[6])
    high = jnp.floor(cell * (1.0 / (2 * HALO)))
    for e, part in enumerate(spread(high, a)):
        parts[e] = jnp.where((row < HALO) == (row + e < rows), part, part * (1.0 - last))
    for d, part in enumerate(spread(cell - high * (2 * HALO), b)):
        parts[count + d] = part
    total = None
    for p, plane in enumerate([cell + last * (4 * HALO * HALO)] + split(a) + split(b)):
        term = edges([plane[:, t * LANES : (t + 1) * LANES] for t in range(tiles)], p + 1)
        total = term if total is None else total + term
    planes = total
    for c in range(channels):
        here = field[c].astype(jnp.float32)
        there = following[c].astype(jnp.float32)
        for t in range(tiles):
            span = slice(t * LANES, (t + 1) * LANES)
            grid[c, t, :rows, :] = here[:, span]
            grid[c, t, rows:, :] = there[:, span]

    def part(first):
        return lambda d, t: parts[first + d, :, t * LANES : (t + 1) * LANES]

    def channel(c, carry):
        sums = stencil(
            lambda: [grid[c, t] for t in range(tiles)],
            shifted,
            part(0),
            part(count),
            tiles,
            rows,
        )
        sums[0] = jnp.where(lane < HALO, 0.0, sums[0])
        sums[-1] = jnp.where(lane >= LANES - HALO, 0.0, sums[-1])
        for t in range(tiles):
            span = slice(t * LANES, (t + 1) * LANES)
            stage[pl.ds(pl.multiple_of(c * rows, rows), rows), span] = sums[t]
        return carry

    lax.fori_loop(0, channels, channel, 0)
    slots = LANES // WINDOW
    bits = [jnp.concatenate([place[k]] * 2, axis=0) > 0.0 for k in range(3)]
    for g in range(2):
        total = None
        for c in range(g * slots, min((g + 1) * slots, channels)):
            term = edges([grid[c, 0], grid[c, tiles - 1]], c - g * slots)
            total = term if total is None else total + term
        if g == 1:
            total = total + jnp.concatenate([planes, jnp.zeros_like(planes)], axis=0)
        for k in range(3):
            total = jnp.where(bits[k], pltpu.roll(total, WINDOW << k, 1), total)
        stage[used : used + tall, g * LANES : (g + 1) * LANES] = total
    stage[used : used + tall, 2 * LANES :] = jnp.zeros((tall, cols - 2 * LANES), jnp.float32)
    value = stage[...].astype(jnp.bfloat16)
    for copy in range(out.shape[0]):
        out[copy] = value


def transform_kernel(cycles, fourier, waves, limits, out, shifted, stage):
    sectors = cycles.shape[0]
    used, rows = stage.shape[0], shifted.shape[2] - 2 * HALO
    tall = rows + 2 * HALO
    channels = used // rows
    slots = LANES // WINDOW
    slot = lax.broadcasted_iota(jnp.int32, (tall, LANES), 1) // WINDOW
    inner = lax.broadcasted_iota(jnp.int32, (tall, LANES), 1) % WINDOW
    pieces = [
        [
            cycles[sector, used : used + tall, g * LANES : (g + 1) * LANES].astype(jnp.float32)
            for sector in range(sectors)
        ]
        for g in range(2)
    ]

    def window(index, height):
        g, c = divmod(index, slots)
        total = pieces[g][0][:height]
        for sector in range(1, sectors):
            total = jnp.where(
                slot[:height] == (c + sector) % slots, pieces[g][sector][:height], total
            )
        left = pltpu.roll(total, -c * WINDOW % LANES, 1) if c else total
        right = pltpu.roll(total, -(c + 1) * WINDOW % LANES, 1) if c + 1 < slots else total
        return jnp.where(inner[:height] < 2 * HALO, left, right)

    cell, *weights = [window(channels + p, rows) for p in range(7)]
    last = (cell >= 4 * HALO * HALO).astype(jnp.float32)
    cell = cell - last * (4 * HALO * HALO)
    row = lax.broadcasted_iota(jnp.int32, cell.shape, 0)
    a = weights[0] + weights[1] + weights[2]
    b = weights[3] + weights[4] + weights[5]
    high = jnp.floor(cell * (1.0 / (2 * HALO)))
    row_parts = [
        jnp.where((row < HALO) == (row + e < rows), part, part * (1.0 - last))
        for e, part in enumerate(spread(high, a))
    ]
    col_parts = spread(cell - high * (2 * HALO), b)
    inside = (inner[:rows] >= HALO) & (inner[:rows] < 3 * HALO)
    for c in range(channels):
        (total,) = stencil(
            lambda: [window(c, tall)],
            shifted,
            lambda e, t: row_parts[e],
            lambda d, t: col_parts[d],
            1,
            rows,
        )
        stage[c * rows : (c + 1) * rows, :] = jnp.where(inside, total, 0.0)
    gathered = jnp.concatenate(
        [cycles[sector, :used, :] for sector in range(sectors)]
        + [stage[...].astype(jnp.bfloat16)],
        axis=1,
    )
    spectrum = lax.dot_general(
        fourier[...], gathered, (((1,), (1,)), ((), ())), preferred_element_type=jnp.float32
    )
    resolved = waves[:, :used].astype(jnp.float32) < limits[:, :used]
    out[:, :used] = jnp.where(resolved, spectrum, 0.0).astype(jnp.bfloat16)
    out[:, used:] = jnp.zeros((out.shape[0], out.shape[1] - used), jnp.bfloat16)


def synthesis_kernel(data, functions, out, turned, packed):
    channels, parts, waves = out.shape
    bands = data.shape[0] // parts
    kept = packed.shape[1] // LANES
    band_rows = 2 * kept
    source = lax.broadcasted_iota(jnp.int32, (parts * bands, LANES), 0)
    target = lax.broadcasted_iota(jnp.int32, (parts * bands, LANES), 1)
    chosen = [
        (source == parts * band + e).astype(jnp.float32).astype(jnp.bfloat16)
        for band in (target, jnp.where(target == bands - 1, target, bands - 2 - target))
        for e in range(parts)
    ]
    columns = lax.dot_general(
        data[...],
        jnp.concatenate(chosen, axis=1),
        (((0,), (0,)), ((), ())),
        preferred_element_type=jnp.float32,
    )
    for place in range(2 * parts):
        turned[place] = columns[:, place * LANES : (place + 1) * LANES]
    packed[...] = jnp.zeros_like(packed)
    step = packed.shape[0] // (2 * parts)
    for mirror in range(2):
        for e in range(parts):
            first = (mirror * parts + e) * step
            for r in range(kept):
                row = band_rows - 1 - r if mirror else r
                packed[first : first + channels, r * LANES : (r + 1) * LANES] = turned[
                    mirror * parts + e, pl.ds(row, channels, stride=band_rows), :
                ]
    result = lax.dot_general(
        packed[...].astype(jnp.bfloat16),
        functions[...],
        (((1,), (1,)), ((), ())),
        preferred_element_type=jnp.float32,
    )
    even = lax.broadcasted_iota(jnp.int32, (channels, waves), 1) % 2 == 0
    for e in range(parts):
        near_half = result[e * step : e * step + channels, :]
        far_half = result[(parts + e) * step : (parts + e) * step + channels, :]
        out[:, e, :] = near_half + jnp.where(even, far_half, -far_half)


def legendre_inputs(order, bands, band_rows, waves, total_lat):
    spread = lax.optimization_barrier(jnp.broadcast_to(order, (band_rows, LANES)))
    order_real = spread.astype(jnp.float32)
    band = jnp.minimum(lax.broadcasted_iota(jnp.int32, (band_rows, LANES), 1), bands - 1)
    cycle = band * band_rows + lax.broadcasted_iota(jnp.int32, (band_rows, LANES), 0) + HALO
    cycle = cycle % total_lat
    angles = (cycle.astype(jnp.float32) + 0.5) * (math.pi / total_lat)
    sine = jnp.sin(angles)
    log_start = (
        0.5 * math.log(0.5)
        + 0.5 * (lax.lgamma(order_real + 1.5) - LGAMMA_HALF_THREE - lax.lgamma(order_real + 1.0))
        + order_real * jnp.log(sine)
    )
    order_real = order.astype(jnp.float32)
    degree = order_real + jnp.arange(1, waves + 1, dtype=jnp.int32).astype(jnp.float32)
    step_a = jnp.sqrt((4.0 * degree * degree - 1.0) / (degree * degree - order_real * order_real))
    before = degree - 1.0
    step_b = jnp.sqrt(
        jnp.maximum(
            (before * before - order_real * order_real) / (4.0 * before * before - 1.0), 0.0
        )
    )
    inside = jnp.arange(1, waves + 1, dtype=jnp.int32) < waves - order
    return (
        jnp.where(inside, step_a, 0.0),
        jnp.where(inside, step_a * step_b, 0.0),
        jnp.cos(angles),
        log_start,
        sine * (math.pi / math.sqrt(total_lat)),
    )


def near(array):
    return pltpu.with_memory_space_constraint(array, pltpu.VMEM)


def smem():
    return pl.BlockSpec(memory_space=pltpu.SMEM)


def vmem():
    return pl.BlockSpec(memory_space=pltpu.VMEM)


def fourier_table(row_waves, limits, following, points):
    return pl.pallas_call(
        functools.partial(fourier_kernel, points=points),
        out_shape=(
            pltpu.VMEM((row_waves.shape[0], points + LANES), jnp.bfloat16),
            pltpu.VMEM((1, LANES), jnp.float32),
        ),
        in_specs=[vmem()] * 3,
        out_specs=(vmem(),) * 2,
        scratch_shapes=[pltpu.VMEM((following.shape[1], LANES), jnp.float32)],
        name="fourier",
        compiler_params=pltpu.CompilerParams(vmem_limit_bytes=GRANT),
    )(*map(near, (row_waves, limits, following)))


def legendre_table(order, bands, band_rows, waves):
    step_a, step_c, *planes = legendre_inputs(order, bands, band_rows, waves, bands * band_rows)
    return pl.pallas_call(
        functools.partial(legendre_kernel, waves=waves, band_rows=band_rows),
        out_shape=pltpu.VMEM((waves, band_rows // 2 * LANES), jnp.bfloat16),
        in_specs=[smem(), smem(), vmem(), vmem(), vmem()],
        out_specs=vmem(),
        scratch_shapes=[pltpu.VMEM((BLOCK * band_rows, LANES), jnp.float32)],
        name="legendre",
        compiler_params=pltpu.CompilerParams(vmem_limit_bytes=GRANT),
    )(step_a, step_c, *map(near, planes))


def pack(limits, prognostic, departure, lat_weight, lon_weight):
    channels, band_rows, sector_cols = prognostic.shape
    return pl.pallas_call(
        pack_kernel,
        out_shape=(
            pltpu.VMEM((channels + 4, band_rows, sector_cols), jnp.bfloat16),
            pltpu.VMEM(prognostic.shape, jnp.bfloat16),
            pltpu.VMEM((3, band_rows, sector_cols), jnp.float32),
        ),
        in_specs=[vmem()] * 5,
        out_specs=(vmem(),) * 3,
        scratch_shapes=[pltpu.VMEM((band_rows, sector_cols), jnp.float32)],
        name="pack",
    )(limits, prognostic, departure, lat_weight, lon_weight)


def interpolate(place, field, own, following, copies):
    channels, band_rows, sector_cols = field.shape
    tall = band_rows + 2 * HALO
    tiles = sector_cols // LANES
    height = channels * band_rows + tall
    count = 2 * HALO + 1
    return pl.pallas_call(
        arrival_kernel,
        out_shape=pltpu.VMEM((copies, height, sector_cols), jnp.bfloat16),
        in_specs=[vmem()] * 4,
        out_specs=vmem(),
        scratch_shapes=[
            pltpu.VMEM((channels, tiles, tall, LANES), jnp.float32),
            pltpu.VMEM((count, tiles, tall, LANES), jnp.float32),
            pltpu.VMEM((2 * count, band_rows, sector_cols), jnp.float32),
            pltpu.VMEM((height, sector_cols), jnp.float32),
        ],
        name="arrival",
    )(*map(near, (place, field, own, following)))


def transform(cycles, fourier, row_waves, limits, channels, band_rows):
    return pl.pallas_call(
        transform_kernel,
        out_shape=pltpu.VMEM((fourier.shape[0], LANES), jnp.bfloat16),
        in_specs=[vmem()] * 4,
        out_specs=vmem(),
        scratch_shapes=[
            pltpu.VMEM((2 * HALO + 1, 1, band_rows + 2 * HALO, LANES), jnp.float32),
            pltpu.VMEM((channels * band_rows, LANES), jnp.float32),
        ],
        name="transform",
        compiler_params=pltpu.CompilerParams(vmem_limit_bytes=GRANT),
    )(*map(near, (cycles, fourier, row_waves, limits)))


def synthesize(data, functions, channels):
    waves, span = functions.shape
    return pl.pallas_call(
        synthesis_kernel,
        out_shape=jax.ShapeDtypeStruct((channels, 2, waves), jnp.float32),
        in_specs=[vmem()] * 2,
        out_specs=vmem(),
        scratch_shapes=[
            pltpu.VMEM((4, LANES, LANES), jnp.float32),
            pltpu.VMEM((64, span), jnp.float32),
        ],
        name="synthesis",
        compiler_params=pltpu.CompilerParams(vmem_limit_bytes=GRANT),
    )(near(data), near(functions))


def shards(prognostic, departure, lat_weight, lon_weight, cycle_waves, wave_order):
    band_rows = prognostic.shape[1]
    bands = lax.axis_size("lat")
    sectors = lax.axis_size("lon")
    total_lon = prognostic.shape[2] * sectors
    waves = wave_order.shape[0]
    band_index = lax.axis_index("lat")
    sector_index = lax.axis_index("lon")

    packed, field, own = pack(
        cycle_waves[None], prognostic, departure, lat_weight, lon_weight
    )
    following = lax.ppermute(packed, "lat", [((i + 1) % bands, i) for i in range(bands)])
    number = lax.broadcasted_iota(jnp.int32, (4, band_rows, LANES), 0)
    place = jnp.where(
        number < 3, (sector_index >> number) & 1, (band_index == bands - 1).astype(jnp.int32)
    ).astype(jnp.float32)
    arrival = interpolate(place, field, own, following, sectors)
    cycles = lax.all_to_all(arrival, "lon", split_axis=0, concat_axis=0, tiled=True)

    slot_waves = wave_order.reshape(bands, sectors)
    own_waves = lax.dynamic_slice_in_dim(slot_waves, sector_index, 1, axis=1)
    row_waves = jnp.broadcast_to(own_waves[:, :, None], (bands, 2, LANES)).reshape(
        2 * bands, LANES
    )
    fourier, limits = fourier_table(row_waves, cycle_waves[None], following, total_lon)
    order = lax.dynamic_slice_in_dim(wave_order, band_index * sectors + sector_index, 1)
    functions = legendre_table(order, bands, band_rows, waves)
    cycles, functions = lax.optimization_barrier((cycles, functions))
    masked = transform(cycles, fourier, row_waves, limits, prognostic.shape[0], band_rows)
    data = lax.all_to_all(
        masked.reshape(bands, 2, LANES), "lat", split_axis=0, concat_axis=0, tiled=True
    ).reshape(2 * bands, LANES)
    spectral = synthesize(data, functions, prognostic.shape[0])
    return spectral.transpose(1, 0, 2)[None]


def solution(mesh):
    in_specs = (
        P(None, "lat", "lon"),
        P("lat", "lon"),
        P("lat", "lon"),
        P("lat", "lon"),
        P("lat"),
        P(),
    )
    out_specs = P(("lat", "lon"), None, None, None)
    return jax.shard_map(shards, mesh=mesh, in_specs=in_specs, out_specs=out_specs, check_vma=False)
```

```python
import functools
import math

import jax
import jax.numpy as jnp
from jax import lax
from jax.experimental import pallas as pl
from jax.experimental.pallas import tpu as pltpu
from jax.sharding import PartitionSpec as P

HALO = 4
LANES = 128
BLOCK = 32
GRANT = 16 << 20
WINDOW = 4 * HALO
LGAMMA_HALF_THREE = 0.5 * math.log(math.pi) - math.log(2.0)
SINE = (
    3.1415926535897932,
    -5.1677127800499700,
    2.5501640398773455,
    -0.59926452932079211,
    0.082145886611128233,
    -0.0073704309457143504,
)


def fourier_kernel(waves, limits, following, out, bound, line, *, points):
    rows, group = waves.shape[0], 64
    scale = 1.0 / math.sqrt(points)
    row = lax.broadcasted_iota(jnp.int32, (group, LANES), 0)
    turn = (row % 2 * (points // 4)).astype(jnp.float32)
    place = lax.broadcasted_iota(jnp.int32, (group, LANES), 1)
    lane = place.astype(jnp.float32)
    column = (
        (place // WINDOW + 1) * (points * WINDOW // LANES) - 2 * HALO + place % WINDOW
    ).astype(jnp.float32)

    def cosine(phase):
        phase = phase - jnp.floor(phase * (1.0 / points) + 0.5) * float(points)
        z = 0.5 - jnp.abs(phase) * (2.0 / points)
        square = z * z
        total = jnp.full_like(z, SINE[-1])
        for factor in SINE[-2::-1]:
            total = total * square + factor
        return total * z

    def block(g, carry):
        first = pl.multiple_of(g * group, group)
        wave = waves[pl.ds(first, group), :].astype(jnp.float32)
        phase = lane * wave + turn
        real = cosine(phase) * scale
        imag = cosine(phase - points / 4) * scale
        ahead = wave * float(LANES)
        turn_real = cosine(ahead)
        turn_imag = cosine(ahead - points / 4)
        for t in range(points // LANES):
            out[pl.ds(first, group), t * LANES : (t + 1) * LANES] = real.astype(jnp.bfloat16)
            real, imag = (
                real * turn_real - imag * turn_imag,
                imag * turn_real + real * turn_imag,
            )
        edge = cosine(column * wave + turn) * scale
        out[pl.ds(first, group), points : points + LANES] = edge.astype(jnp.bfloat16)
        return carry

    lax.fori_loop(0, rows // group, block, 0)

    band_rows = limits.shape[1]
    line[...] = jnp.zeros_like(line)
    line[:1, :band_rows] = limits[...].astype(jnp.float32)
    own = line[...]
    last = following[following.shape[0] - 1].astype(jnp.float32)
    ahead = last[:, :LANES] * 256.0 + last[:, LANES : 2 * LANES]
    width = band_rows
    while width < LANES:
        own = own + pltpu.roll(own, width, 1)
        ahead = ahead + pltpu.roll(ahead, width, 1)
        width *= 2
    bound[...] = jnp.where(
        place[:1] % band_rows < HALO,
        pltpu.roll(own, LANES - HALO, 1)[:1],
        pltpu.roll(ahead, HALO, 1)[HALO : HALO + 1],
    )


def legendre_kernel(step_a, step_c, cosine, log_start, weight, out, stage, *, waves, band_rows):
    cos = cosine[...]
    start = log_start[...]
    scale = weight[...]

    def block(t, carry):
        current, last, log_scale = carry
        base = t * BLOCK
        size = jnp.exp(log_scale + start) * scale
        for u in range(0, BLOCK, 2):
            first_a = step_a[base + u] * cos
            second_a = step_a[base + u + 1] * cos
            first_c = step_c[base + u]
            middle = first_a * current - first_c * last
            fresh = (second_a * first_a - step_c[base + u + 1]) * current - (
                second_a * first_c
            ) * last
            stage[band_rows * u : band_rows * (u + 1), :] = current * size
            stage[band_rows * (u + 1) : band_rows * (u + 2), :] = middle * size
            last = middle
            current = fresh
        row = pl.multiple_of(base, BLOCK)
        for r in range(band_rows // 2):
            out[pl.ds(row, BLOCK), r * LANES : (r + 1) * LANES] = stage[
                pl.ds(r, BLOCK, stride=band_rows), :
            ].astype(jnp.bfloat16)
        factor = jnp.maximum(jnp.maximum(jnp.abs(current), jnp.abs(last)), 1.0)
        inverse = 1.0 / factor
        return current * inverse, last * inverse, log_scale + jnp.log(factor)

    initial = (jnp.ones_like(cos), jnp.zeros_like(cos), jnp.zeros_like(cos))
    lax.fori_loop(0, waves // BLOCK, block, initial)


def spread(place, share):
    return [
        jnp.where(place == d, 1.0 - share, jnp.where(place == d - 1, share, 0.0))
        for d in range(2 * HALO + 1)
    ]


def edges(tall, slot):
    lane = lax.broadcasted_iota(jnp.int32, tall[0].shape, 1)
    reach = 2 * HALO
    ends = jnp.where(
        lane < reach, tall[0], jnp.where(lane >= LANES - reach, tall[-1], jnp.zeros_like(tall[0]))
    )
    return pltpu.roll(ends, slot * WINDOW + reach, 1)


def stencil(read, write, row_parts, col_parts, tiles, rows):
    count = 2 * HALO + 1
    source = read()
    lane = lax.broadcasted_iota(jnp.int32, source[0].shape, 1)
    for d in range(count):
        move = d - HALO
        if move == 0:
            turned = source
        else:
            rolled = [pltpu.roll(tile, -move % LANES, 1) for tile in source]
            if tiles == 1:
                turned = rolled
            elif move > 0:
                turned = [
                    jnp.where(lane < LANES - move, rolled[t], rolled[(t + 1) % tiles])
                    for t in range(tiles)
                ]
            else:
                turned = [
                    jnp.where(lane < -move, rolled[t - 1], rolled[t]) for t in range(tiles)
                ]
        for t in range(tiles):
            write[d, t] = turned[t]
    sums = []
    for t in range(tiles):
        total = None
        for e in range(count):
            inner = None
            for d in range(count):
                term = col_parts(d, t) * write[d, t, e : e + rows, :]
                inner = term if inner is None else inner + term
            term = row_parts(e, t) * inner
            total = term if total is None else total + term
        sums.append(total)
    return sums


def split(value):
    high = value.astype(jnp.bfloat16).astype(jnp.float32)
    rest = value - high
    middle = rest.astype(jnp.bfloat16).astype(jnp.float32)
    return [high, middle, rest - middle]


def pack_kernel(limits, field, departure, lat_weight, lon_weight, out, field_out, own, line):
    channels = field.shape[0]
    cols = departure.shape[1]
    value = field[...]
    field_out[...] = value
    out[:channels] = value
    cell = departure[...].astype(jnp.float32)
    a = lat_weight[...]
    b = lon_weight[...]
    for p, plane in enumerate((cell, a, b)):
        own[p] = plane
    planes = [v[:HALO] for v in [cell] + split(a) + split(b)]
    for p in range(0, len(planes) - 1, 2):
        pair = jnp.concatenate(planes[p : p + 2], axis=0)
        out[channels + p // 2] = pair.astype(jnp.bfloat16)
    rows = limits.shape[1]
    bound = limits[...].astype(jnp.float32)
    high = jnp.floor(bound * (1.0 / 256.0))
    line[:HALO] = planes[-1]
    line[HALO:] = jnp.zeros_like(planes[-1])
    line[HALO : HALO + 1, :rows] = high
    line[HALO : HALO + 1, LANES : LANES + rows] = bound - high * 256.0
    out[channels + len(planes) // 2] = line[...].astype(jnp.bfloat16)


def arrival_kernel(place, field, own, following, out, grid, shifted, parts, stage):
    channels, rows, cols = field.shape
    tiles = cols // LANES
    count = 2 * HALO + 1
    used = channels * rows
    tall = rows + 2 * HALO
    lane = lax.broadcasted_iota(jnp.int32, (rows, LANES), 1)
    row = lax.broadcasted_iota(jnp.int32, (rows, cols), 0)
    last = jnp.concatenate([place[3]] * tiles, axis=1)
    pairs = [following[channels + p].astype(jnp.float32) for p in range(4)]
    ahead = [pairs[p // 2][p % 2 * HALO : (p % 2 + 1) * HALO] for p in range(7)]

    def rows_of(plane, rest):
        return jnp.concatenate([plane[HALO:], rest], axis=0)

    cell = rows_of(own[0], ahead[0])
    a = rows_of(own[1], ahead[1] + ahead[2] + ahead[3])
    b = rows_of(own[2], ahead[4] + ahead[5] + ahead[6])
    high = jnp.floor(cell * (1.0 / (2 * HALO)))
    for e, part in enumerate(spread(high, a)):
        parts[e] = jnp.where((row < HALO) == (row + e < rows), part, part * (1.0 - last))
    for d, part in enumerate(spread(cell - high * (2 * HALO), b)):
        parts[count + d] = part
    total = None
    for p, plane in enumerate([cell + last * (4 * HALO * HALO)] + split(a) + split(b)):
        term = edges([plane[:, t * LANES : (t + 1) * LANES] for t in range(tiles)], p + 1)
        total = term if total is None else total + term
    planes = total
    for c in range(channels):
        here = field[c].astype(jnp.float32)
        there = following[c].astype(jnp.float32)
        for t in range(tiles):
            span = slice(t * LANES, (t + 1) * LANES)
            grid[c, t, :rows, :] = here[:, span]
            grid[c, t, rows:, :] = there[:, span]

    def part(first):
        return lambda d, t: parts[first + d, :, t * LANES : (t + 1) * LANES]

    for c in range(channels):
        sums = stencil(
            lambda: [grid[c, t] for t in range(tiles)],
            shifted.at[c % 2],
            part(0),
            part(count),
            tiles,
            rows,
        )
        sums[0] = jnp.where(lane < HALO, 0.0, sums[0])
        sums[-1] = jnp.where(lane >= LANES - HALO, 0.0, sums[-1])
        for t in range(tiles):
            span = slice(t * LANES, (t + 1) * LANES)
            stage[c * rows : (c + 1) * rows, span] = sums[t]
    slots = LANES // WINDOW
    bits = [jnp.concatenate([place[k]] * 2, axis=0) > 0.0 for k in range(3)]
    for g in range(2):
        total = None
        for c in range(g * slots, min((g + 1) * slots, channels)):
            term = edges([grid[c, 0], grid[c, tiles - 1]], c - g * slots)
            total = term if total is None else total + term
        if g == 1:
            total = total + jnp.concatenate([planes, jnp.zeros_like(planes)], axis=0)
        for k in range(3):
            total = jnp.where(bits[k], pltpu.roll(total, WINDOW << k, 1), total)
        stage[used : used + tall, g * LANES : (g + 1) * LANES] = total
    stage[used : used + tall, 2 * LANES :] = jnp.zeros((tall, cols - 2 * LANES), jnp.float32)
    value = stage[...].astype(jnp.bfloat16)
    for copy in range(out.shape[0]):
        out[copy] = value


def transform_kernel(cycles, fourier, waves, limits, out, shifted, stage):
    sectors = cycles.shape[0]
    used, rows = stage.shape[0], shifted.shape[2] - 2 * HALO
    tall = rows + 2 * HALO
    channels = used // rows
    slots = LANES // WINDOW
    slot = lax.broadcasted_iota(jnp.int32, (tall, LANES), 1) // WINDOW
    inner = lax.broadcasted_iota(jnp.int32, (tall, LANES), 1) % WINDOW
    pieces = [
        [
            cycles[sector, used : used + tall, g * LANES : (g + 1) * LANES].astype(jnp.float32)
            for sector in range(sectors)
        ]
        for g in range(2)
    ]

    def window(index, height):
        g, c = divmod(index, slots)
        total = pieces[g][0][:height]
        for sector in range(1, sectors):
            total = jnp.where(
                slot[:height] == (c + sector) % slots, pieces[g][sector][:height], total
            )
        left = pltpu.roll(total, -c * WINDOW % LANES, 1) if c else total
        right = pltpu.roll(total, -(c + 1) * WINDOW % LANES, 1) if c + 1 < slots else total
        return jnp.where(inner[:height] < 2 * HALO, left, right)

    cell, *weights = [window(channels + p, rows) for p in range(7)]
    last = (cell >= 4 * HALO * HALO).astype(jnp.float32)
    cell = cell - last * (4 * HALO * HALO)
    row = lax.broadcasted_iota(jnp.int32, cell.shape, 0)
    a = weights[0] + weights[1] + weights[2]
    b = weights[3] + weights[4] + weights[5]
    high = jnp.floor(cell * (1.0 / (2 * HALO)))
    row_parts = [
        jnp.where((row < HALO) == (row + e < rows), part, part * (1.0 - last))
        for e, part in enumerate(spread(high, a))
    ]
    col_parts = spread(cell - high * (2 * HALO), b)
    inside = (inner[:rows] >= HALO) & (inner[:rows] < 3 * HALO)
    for c in range(channels):
        (total,) = stencil(
            lambda: [window(c, tall)],
            shifted,
            lambda e, t: row_parts[e],
            lambda d, t: col_parts[d],
            1,
            rows,
        )
        stage[c * rows : (c + 1) * rows, :] = jnp.where(inside, total, 0.0)
    gathered = jnp.concatenate(
        [cycles[sector, :used, :] for sector in range(sectors)]
        + [stage[...].astype(jnp.bfloat16)],
        axis=1,
    )
    spectrum = lax.dot_general(
        fourier[...], gathered, (((1,), (1,)), ((), ())), preferred_element_type=jnp.float32
    )
    resolved = waves[:, :used].astype(jnp.float32) < limits[:, :used]
    out[:, :used] = jnp.where(resolved, spectrum, 0.0).astype(jnp.bfloat16)
    out[:, used:] = jnp.zeros((out.shape[0], out.shape[1] - used), jnp.bfloat16)


def synthesis_kernel(data, functions, out, turned, packed):
    channels, parts, waves = out.shape
    bands = data.shape[0] // parts
    kept = packed.shape[1] // LANES
    band_rows = 2 * kept
    source = lax.broadcasted_iota(jnp.int32, (parts * bands, LANES), 0)
    target = lax.broadcasted_iota(jnp.int32, (parts * bands, LANES), 1)
    chosen = [
        (source == parts * band + e).astype(jnp.float32).astype(jnp.bfloat16)
        for band in (target, jnp.where(target == bands - 1, target, bands - 2 - target))
        for e in range(parts)
    ]
    columns = lax.dot_general(
        data[...],
        jnp.concatenate(chosen, axis=1),
        (((0,), (0,)), ((), ())),
        preferred_element_type=jnp.float32,
    )
    for place in range(2 * parts):
        turned[place] = columns[:, place * LANES : (place + 1) * LANES]
    packed[...] = jnp.zeros_like(packed)
    step = packed.shape[0] // (2 * parts)
    for mirror in range(2):
        for e in range(parts):
            first = (mirror * parts + e) * step
            for r in range(kept):
                row = band_rows - 1 - r if mirror else r
                packed[first : first + channels, r * LANES : (r + 1) * LANES] = turned[
                    mirror * parts + e, pl.ds(row, channels, stride=band_rows), :
                ]
    result = lax.dot_general(
        packed[...].astype(jnp.bfloat16),
        functions[...],
        (((1,), (1,)), ((), ())),
        preferred_element_type=jnp.float32,
    )
    even = lax.broadcasted_iota(jnp.int32, (channels, waves), 1) % 2 == 0
    for e in range(parts):
        near_half = result[e * step : e * step + channels, :]
        far_half = result[(parts + e) * step : (parts + e) * step + channels, :]
        out[:, e, :] = near_half + jnp.where(even, far_half, -far_half)


def legendre_inputs(order, bands, band_rows, waves, total_lat):
    spread = lax.optimization_barrier(jnp.broadcast_to(order, (band_rows, LANES)))
    order_real = spread.astype(jnp.float32)
    band = jnp.minimum(lax.broadcasted_iota(jnp.int32, (band_rows, LANES), 1), bands - 1)
    cycle = band * band_rows + lax.broadcasted_iota(jnp.int32, (band_rows, LANES), 0) + HALO
    cycle = cycle % total_lat
    angles = (cycle.astype(jnp.float32) + 0.5) * (math.pi / total_lat)
    sine = jnp.sin(angles)
    log_start = (
        0.5 * math.log(0.5)
        + 0.5 * (lax.lgamma(order_real + 1.5) - LGAMMA_HALF_THREE - lax.lgamma(order_real + 1.0))
        + order_real * jnp.log(sine)
    )
    order_real = order.astype(jnp.float32)
    degree = order_real + jnp.arange(1, waves + 1, dtype=jnp.int32).astype(jnp.float32)
    step_a = jnp.sqrt((4.0 * degree * degree - 1.0) / (degree * degree - order_real * order_real))
    before = degree - 1.0
    step_b = jnp.sqrt(
        jnp.maximum(
            (before * before - order_real * order_real) / (4.0 * before * before - 1.0), 0.0
        )
    )
    inside = jnp.arange(1, waves + 1, dtype=jnp.int32) < waves - order
    return (
        jnp.where(inside, step_a, 0.0),
        jnp.where(inside, step_a * step_b, 0.0),
        jnp.cos(angles),
        log_start,
        sine * (math.pi / math.sqrt(total_lat)),
    )


def near(array):
    return pltpu.with_memory_space_constraint(array, pltpu.VMEM)


def smem():
    return pl.BlockSpec(memory_space=pltpu.SMEM)


def vmem():
    return pl.BlockSpec(memory_space=pltpu.VMEM)


def fourier_table(row_waves, limits, following, points):
    return pl.pallas_call(
        functools.partial(fourier_kernel, points=points),
        out_shape=(
            pltpu.VMEM((row_waves.shape[0], points + LANES), jnp.bfloat16),
            pltpu.VMEM((1, LANES), jnp.float32),
        ),
        in_specs=[vmem()] * 3,
        out_specs=(vmem(),) * 2,
        scratch_shapes=[pltpu.VMEM((following.shape[1], LANES), jnp.float32)],
        name="fourier",
        compiler_params=pltpu.CompilerParams(vmem_limit_bytes=GRANT),
    )(*map(near, (row_waves, limits, following)))


def legendre_table(order, bands, band_rows, waves):
    step_a, step_c, *planes = legendre_inputs(order, bands, band_rows, waves, bands * band_rows)
    return pl.pallas_call(
        functools.partial(legendre_kernel, waves=waves, band_rows=band_rows),
        out_shape=pltpu.VMEM((waves, band_rows // 2 * LANES), jnp.bfloat16),
        in_specs=[smem(), smem(), vmem(), vmem(), vmem()],
        out_specs=vmem(),
        scratch_shapes=[pltpu.VMEM((BLOCK * band_rows, LANES), jnp.float32)],
        name="legendre",
        compiler_params=pltpu.CompilerParams(vmem_limit_bytes=GRANT),
    )(step_a, step_c, *map(near, planes))


def pack(limits, prognostic, departure, lat_weight, lon_weight):
    channels, band_rows, sector_cols = prognostic.shape
    return pl.pallas_call(
        pack_kernel,
        out_shape=(
            pltpu.VMEM((channels + 4, band_rows, sector_cols), jnp.bfloat16),
            pltpu.VMEM(prognostic.shape, jnp.bfloat16),
            pltpu.VMEM((3, band_rows, sector_cols), jnp.float32),
        ),
        in_specs=[vmem()] * 5,
        out_specs=(vmem(),) * 3,
        scratch_shapes=[pltpu.VMEM((band_rows, sector_cols), jnp.float32)],
        name="pack",
    )(limits, prognostic, departure, lat_weight, lon_weight)


def interpolate(place, field, own, following, copies):
    channels, band_rows, sector_cols = field.shape
    tall = band_rows + 2 * HALO
    tiles = sector_cols // LANES
    height = channels * band_rows + tall
    count = 2 * HALO + 1
    return pl.pallas_call(
        arrival_kernel,
        out_shape=pltpu.VMEM((copies, height, sector_cols), jnp.bfloat16),
        in_specs=[vmem()] * 4,
        out_specs=vmem(),
        scratch_shapes=[
            pltpu.VMEM((channels, tiles, tall, LANES), jnp.float32),
            pltpu.VMEM((2, count, tiles, tall, LANES), jnp.float32),
            pltpu.VMEM((2 * count, band_rows, sector_cols), jnp.float32),
            pltpu.VMEM((height, sector_cols), jnp.float32),
        ],
        name="arrival",
    )(*map(near, (place, field, own, following)))


def transform(cycles, fourier, row_waves, limits, channels, band_rows):
    return pl.pallas_call(
        transform_kernel,
        out_shape=pltpu.VMEM((fourier.shape[0], LANES), jnp.bfloat16),
        in_specs=[vmem()] * 4,
        out_specs=vmem(),
        scratch_shapes=[
            pltpu.VMEM((2 * HALO + 1, 1, band_rows + 2 * HALO, LANES), jnp.float32),
            pltpu.VMEM((channels * band_rows, LANES), jnp.float32),
        ],
        name="transform",
        compiler_params=pltpu.CompilerParams(vmem_limit_bytes=GRANT),
    )(*map(near, (cycles, fourier, row_waves, limits)))


def synthesize(data, functions, channels):
    waves, span = functions.shape
    return pl.pallas_call(
        synthesis_kernel,
        out_shape=jax.ShapeDtypeStruct((channels, 2, waves), jnp.float32),
        in_specs=[vmem()] * 2,
        out_specs=vmem(),
        scratch_shapes=[
            pltpu.VMEM((4, LANES, LANES), jnp.float32),
            pltpu.VMEM((64, span), jnp.float32),
        ],
        name="synthesis",
        compiler_params=pltpu.CompilerParams(vmem_limit_bytes=GRANT),
    )(near(data), near(functions))


def shards(prognostic, departure, lat_weight, lon_weight, cycle_waves, wave_order):
    band_rows = prognostic.shape[1]
    bands = lax.axis_size("lat")
    sectors = lax.axis_size("lon")
    total_lon = prognostic.shape[2] * sectors
    waves = wave_order.shape[0]
    band_index = lax.axis_index("lat")
    sector_index = lax.axis_index("lon")

    packed, field, own = pack(
        cycle_waves[None], prognostic, departure, lat_weight, lon_weight
    )
    following = lax.ppermute(packed, "lat", [((i + 1) % bands, i) for i in range(bands)])
    number = lax.broadcasted_iota(jnp.int32, (4, band_rows, LANES), 0)
    place = jnp.where(
        number < 3, (sector_index >> number) & 1, (band_index == bands - 1).astype(jnp.int32)
    ).astype(jnp.float32)
    slot_waves = wave_order.reshape(bands, sectors)
    own_waves = lax.dynamic_slice_in_dim(slot_waves, sector_index, 1, axis=1)
    order = lax.dynamic_slice_in_dim(wave_order, band_index * sectors + sector_index, 1)
    following, own_waves, order = lax.optimization_barrier((following, own_waves, order))
    arrival = interpolate(place, field, own, following, sectors)
    cycles = lax.all_to_all(arrival, "lon", split_axis=0, concat_axis=0, tiled=True)

    row_waves = jnp.broadcast_to(own_waves[:, :, None], (bands, 2, LANES)).reshape(
        2 * bands, LANES
    )
    fourier, limits = fourier_table(row_waves, cycle_waves[None], following, total_lon)
    functions = legendre_table(order, bands, band_rows, waves)
    cycles, functions = lax.optimization_barrier((cycles, functions))
    masked = transform(cycles, fourier, row_waves, limits, prognostic.shape[0], band_rows)
    data = lax.all_to_all(
        masked.reshape(bands, 2, LANES), "lat", split_axis=0, concat_axis=0, tiled=True
    ).reshape(2 * bands, LANES)
    spectral = synthesize(data, functions, prognostic.shape[0])
    return spectral.transpose(1, 0, 2)[None]


def solution(mesh):
    in_specs = (
        P(None, "lat", "lon"),
        P("lat", "lon"),
        P("lat", "lon"),
        P("lat", "lon"),
        P("lat"),
        P(),
    )
    out_specs = P(("lat", "lon"), None, None, None)
    return jax.shard_map(shards, mesh=mesh, in_specs=in_specs, out_specs=out_specs, check_vma=False)
```

```python
import functools
import math

import jax
import jax.numpy as jnp
from jax import lax
from jax.experimental import pallas as pl
from jax.experimental.pallas import tpu as pltpu
from jax.sharding import PartitionSpec as P

HALO = 4
LANES = 128
BLOCK = 32
GRANT = 16 << 20
WINDOW = 4 * HALO
LGAMMA_HALF_THREE = 0.5 * math.log(math.pi) - math.log(2.0)
SINE = (
    3.1415926535897932,
    -5.1677127800499700,
    2.5501640398773455,
    -0.59926452932079211,
    0.082145886611128233,
    -0.0073704309457143504,
)


def fourier_kernel(waves, limits, following, out, bound, line, *, points):
    rows, group = waves.shape[0], 64
    scale = 1.0 / math.sqrt(points)
    row = lax.broadcasted_iota(jnp.int32, (group, LANES), 0)
    turn = (row % 2 * (points // 4)).astype(jnp.float32)
    place = lax.broadcasted_iota(jnp.int32, (group, LANES), 1)
    lane = place.astype(jnp.float32)
    column = (
        (place // WINDOW + 1) * (points * WINDOW // LANES) - 2 * HALO + place % WINDOW
    ).astype(jnp.float32)

    def cosine(phase):
        phase = phase - jnp.floor(phase * (1.0 / points) + 0.5) * float(points)
        z = 0.5 - jnp.abs(phase) * (2.0 / points)
        square = z * z
        total = jnp.full_like(z, SINE[-1])
        for factor in SINE[-2::-1]:
            total = total * square + factor
        return total * z

    def block(g, carry):
        first = pl.multiple_of(g * group, group)
        wave = waves[pl.ds(first, group), :].astype(jnp.float32)
        phase = lane * wave + turn
        real = cosine(phase) * scale
        imag = cosine(phase - points / 4) * scale
        ahead = wave * float(LANES)
        turn_real = cosine(ahead)
        turn_imag = cosine(ahead - points / 4)
        for t in range(points // LANES):
            out[pl.ds(first, group), t * LANES : (t + 1) * LANES] = real.astype(jnp.bfloat16)
            real, imag = (
                real * turn_real - imag * turn_imag,
                imag * turn_real + real * turn_imag,
            )
        edge = cosine(column * wave + turn) * scale
        out[pl.ds(first, group), points : points + LANES] = edge.astype(jnp.bfloat16)
        return carry

    lax.fori_loop(0, rows // group, block, 0)

    band_rows = limits.shape[1]
    line[...] = jnp.zeros_like(line)
    line[:1, :band_rows] = limits[...].astype(jnp.float32)
    own = line[...]
    last = following[following.shape[0] - 1].astype(jnp.float32)
    ahead = last[:, :LANES] * 256.0 + last[:, LANES : 2 * LANES]
    width = band_rows
    while width < LANES:
        own = own + pltpu.roll(own, width, 1)
        ahead = ahead + pltpu.roll(ahead, width, 1)
        width *= 2
    bound[...] = jnp.where(
        place[:1] % band_rows < HALO,
        pltpu.roll(own, LANES - HALO, 1)[:1],
        pltpu.roll(ahead, HALO, 1)[HALO : HALO + 1],
    )


def legendre_kernel(step_a, step_c, cosine, log_start, weight, out, stage, *, waves, band_rows):
    cos = cosine[...]
    start = log_start[...]
    scale = weight[...]

    def block(t, carry):
        current, last, log_scale = carry
        base = t * BLOCK
        size = jnp.exp(log_scale + start) * scale
        for u in range(0, BLOCK, 2):
            first_a = step_a[base + u] * cos
            second_a = step_a[base + u + 1] * cos
            first_c = step_c[base + u]
            middle = first_a * current - first_c * last
            fresh = (second_a * first_a - step_c[base + u + 1]) * current - (
                second_a * first_c
            ) * last
            stage[band_rows * u : band_rows * (u + 1), :] = current * size
            stage[band_rows * (u + 1) : band_rows * (u + 2), :] = middle * size
            last = middle
            current = fresh
        row = pl.multiple_of(base, BLOCK)
        for r in range(band_rows // 2):
            out[pl.ds(row, BLOCK), r * LANES : (r + 1) * LANES] = stage[
                pl.ds(r, BLOCK, stride=band_rows), :
            ].astype(jnp.bfloat16)
        factor = jnp.maximum(jnp.maximum(jnp.abs(current), jnp.abs(last)), 1.0)
        inverse = 1.0 / factor
        return current * inverse, last * inverse, log_scale + jnp.log(factor)

    initial = (jnp.ones_like(cos), jnp.zeros_like(cos), jnp.zeros_like(cos))
    lax.fori_loop(0, waves // BLOCK, block, initial)


def spread(place, share):
    return [
        jnp.where(place == d, 1.0 - share, jnp.where(place == d - 1, share, 0.0))
        for d in range(2 * HALO + 1)
    ]


def edges(tall, slot):
    lane = lax.broadcasted_iota(jnp.int32, tall[0].shape, 1)
    reach = 2 * HALO
    ends = jnp.where(
        lane < reach, tall[0], jnp.where(lane >= LANES - reach, tall[-1], jnp.zeros_like(tall[0]))
    )
    return pltpu.roll(ends, slot * WINDOW + reach, 1)


def stencil(read, write, row_parts, col_parts, tiles, rows):
    count = 2 * HALO + 1
    source = read()
    lane = lax.broadcasted_iota(jnp.int32, source[0].shape, 1)
    for d in range(count):
        move = d - HALO
        if move == 0:
            turned = source
        else:
            rolled = [pltpu.roll(tile, -move % LANES, 1) for tile in source]
            if tiles == 1:
                turned = rolled
            elif move > 0:
                turned = [
                    jnp.where(lane < LANES - move, rolled[t], rolled[(t + 1) % tiles])
                    for t in range(tiles)
                ]
            else:
                turned = [
                    jnp.where(lane < -move, rolled[t - 1], rolled[t]) for t in range(tiles)
                ]
        for t in range(tiles):
            write[d, t] = turned[t]
    sums = []
    for t in range(tiles):
        total = None
        for e in range(count):
            inner = None
            for d in range(count):
                term = col_parts(d, t) * write[d, t, e : e + rows, :]
                inner = term if inner is None else inner + term
            term = row_parts(e, t) * inner
            total = term if total is None else total + term
        sums.append(total)
    return sums


def split(value):
    high = value.astype(jnp.bfloat16).astype(jnp.float32)
    rest = value - high
    middle = rest.astype(jnp.bfloat16).astype(jnp.float32)
    return [high, middle, rest - middle]


def pack_kernel(limits, field, departure, lat_weight, lon_weight, out, field_out, own, line):
    channels = field.shape[0]
    cols = departure.shape[1]
    value = field[...]
    field_out[...] = value
    out[:channels] = value
    cell = departure[...].astype(jnp.float32)
    a = lat_weight[...]
    b = lon_weight[...]
    for p, plane in enumerate((cell, a, b)):
        own[p] = plane
    planes = [v[:HALO] for v in [cell] + split(a) + split(b)]
    for p in range(0, len(planes) - 1, 2):
        pair = jnp.concatenate(planes[p : p + 2], axis=0)
        out[channels + p // 2] = pair.astype(jnp.bfloat16)
    rows = limits.shape[1]
    bound = limits[...].astype(jnp.float32)
    high = jnp.floor(bound * (1.0 / 256.0))
    line[:HALO] = planes[-1]
    line[HALO:] = jnp.zeros_like(planes[-1])
    line[HALO : HALO + 1, :rows] = high
    line[HALO : HALO + 1, LANES : LANES + rows] = bound - high * 256.0
    out[channels + len(planes) // 2] = line[...].astype(jnp.bfloat16)


def arrival_kernel(place, field, own, following, out, grid, shifted, parts, stage):
    channels, rows, cols = field.shape
    tiles = cols // LANES
    count = 2 * HALO + 1
    used = channels * rows
    tall = rows + 2 * HALO
    lane = lax.broadcasted_iota(jnp.int32, (rows, LANES), 1)
    row = lax.broadcasted_iota(jnp.int32, (rows, cols), 0)
    last = jnp.concatenate([place[3]] * tiles, axis=1)
    pairs = [following[channels + p].astype(jnp.float32) for p in range(4)]
    ahead = [pairs[p // 2][p % 2 * HALO : (p % 2 + 1) * HALO] for p in range(7)]

    def rows_of(plane, rest):
        return jnp.concatenate([plane[HALO:], rest], axis=0)

    cell = rows_of(own[0], ahead[0])
    a = rows_of(own[1], ahead[1] + ahead[2] + ahead[3])
    b = rows_of(own[2], ahead[4] + ahead[5] + ahead[6])
    high = jnp.floor(cell * (1.0 / (2 * HALO)))
    for e, part in enumerate(spread(high, a)):
        parts[e] = jnp.where((row < HALO) == (row + e < rows), part, part * (1.0 - last))
    for d, part in enumerate(spread(cell - high * (2 * HALO), b)):
        parts[count + d] = part
    total = None
    for p, plane in enumerate([cell + last * (4 * HALO * HALO)] + split(a) + split(b)):
        term = edges([plane[:, t * LANES : (t + 1) * LANES] for t in range(tiles)], p + 1)
        total = term if total is None else total + term
    planes = total
    for c in range(channels):
        here = field[c].astype(jnp.float32)
        there = following[c].astype(jnp.float32)
        for t in range(tiles):
            span = slice(t * LANES, (t + 1) * LANES)
            grid[c, t, :rows, :] = here[:, span]
            grid[c, t, rows:, :] = there[:, span]

    def part(first):
        return lambda d, t: parts[first + d, :, t * LANES : (t + 1) * LANES]

    for c in range(channels):
        sums = stencil(
            lambda: [grid[c, t] for t in range(tiles)],
            shifted.at[c % 2],
            part(0),
            part(count),
            tiles,
            rows,
        )
        sums[0] = jnp.where(lane < HALO, 0.0, sums[0])
        sums[-1] = jnp.where(lane >= LANES - HALO, 0.0, sums[-1])
        for t in range(tiles):
            span = slice(t * LANES, (t + 1) * LANES)
            stage[c * rows : (c + 1) * rows, span] = sums[t]
    slots = LANES // WINDOW
    bits = [jnp.concatenate([place[k]] * 2, axis=0) > 0.0 for k in range(3)]
    for g in range(2):
        total = None
        for c in range(g * slots, min((g + 1) * slots, channels)):
            term = edges([grid[c, 0], grid[c, tiles - 1]], c - g * slots)
            total = term if total is None else total + term
        if g == 1:
            total = total + jnp.concatenate([planes, jnp.zeros_like(planes)], axis=0)
        for k in range(3):
            total = jnp.where(bits[k], pltpu.roll(total, WINDOW << k, 1), total)
        stage[used : used + tall, g * LANES : (g + 1) * LANES] = total
    stage[used : used + tall, 2 * LANES :] = jnp.zeros((tall, cols - 2 * LANES), jnp.float32)
    value = stage[...].astype(jnp.bfloat16)
    for copy in range(out.shape[0]):
        out[copy] = value


def transform_kernel(cycles, fourier, waves, limits, out, shifted, stage):
    sectors = cycles.shape[0]
    used, rows = stage.shape[0], shifted.shape[2] - 2 * HALO
    tall = rows + 2 * HALO
    channels = used // rows
    slots = LANES // WINDOW
    slot = lax.broadcasted_iota(jnp.int32, (tall, LANES), 1) // WINDOW
    inner = lax.broadcasted_iota(jnp.int32, (tall, LANES), 1) % WINDOW
    pieces = [
        [
            cycles[sector, used : used + tall, g * LANES : (g + 1) * LANES].astype(jnp.float32)
            for sector in range(sectors)
        ]
        for g in range(2)
    ]

    def window(index, height):
        g, c = divmod(index, slots)
        total = pieces[g][0][:height]
        for sector in range(1, sectors):
            total = jnp.where(
                slot[:height] == (c + sector) % slots, pieces[g][sector][:height], total
            )
        left = pltpu.roll(total, -c * WINDOW % LANES, 1) if c else total
        right = pltpu.roll(total, -(c + 1) * WINDOW % LANES, 1) if c + 1 < slots else total
        return jnp.where(inner[:height] < 2 * HALO, left, right)

    cell, *weights = [window(channels + p, rows) for p in range(7)]
    last = (cell >= 4 * HALO * HALO).astype(jnp.float32)
    cell = cell - last * (4 * HALO * HALO)
    row = lax.broadcasted_iota(jnp.int32, cell.shape, 0)
    a = weights[0] + weights[1] + weights[2]
    b = weights[3] + weights[4] + weights[5]
    high = jnp.floor(cell * (1.0 / (2 * HALO)))
    row_parts = [
        jnp.where((row < HALO) == (row + e < rows), part, part * (1.0 - last))
        for e, part in enumerate(spread(high, a))
    ]
    col_parts = spread(cell - high * (2 * HALO), b)
    inside = (inner[:rows] >= HALO) & (inner[:rows] < 3 * HALO)
    for c in range(channels):
        (total,) = stencil(
            lambda: [window(c, tall)],
            shifted,
            lambda e, t: row_parts[e],
            lambda d, t: col_parts[d],
            1,
            rows,
        )
        stage[c * rows : (c + 1) * rows, :] = jnp.where(inside, total, 0.0)
    gathered = jnp.concatenate(
        [cycles[sector, :used, :] for sector in range(sectors)]
        + [stage[...].astype(jnp.bfloat16)],
        axis=1,
    )
    spectrum = lax.dot_general(
        fourier[...], gathered, (((1,), (1,)), ((), ())), preferred_element_type=jnp.float32
    )
    resolved = waves[:, :used].astype(jnp.float32) < limits[:, :used]
    out[:, :used] = jnp.where(resolved, spectrum, 0.0).astype(jnp.bfloat16)
    out[:, used:] = jnp.zeros((out.shape[0], out.shape[1] - used), jnp.bfloat16)


def synthesis_kernel(data, functions, out, turned, packed):
    channels, parts, waves = out.shape
    bands = data.shape[0] // parts
    kept = packed.shape[1] // LANES
    band_rows = 2 * kept
    source = lax.broadcasted_iota(jnp.int32, (parts * bands, LANES), 0)
    target = lax.broadcasted_iota(jnp.int32, (parts * bands, LANES), 1)
    chosen = [
        (source == parts * band + e).astype(jnp.float32).astype(jnp.bfloat16)
        for band in (target, jnp.where(target == bands - 1, target, bands - 2 - target))
        for e in range(parts)
    ]
    columns = lax.dot_general(
        data[...],
        jnp.concatenate(chosen, axis=1),
        (((0,), (0,)), ((), ())),
        preferred_element_type=jnp.float32,
    )
    for place in range(2 * parts):
        turned[place] = columns[:, place * LANES : (place + 1) * LANES]
    packed[...] = jnp.zeros_like(packed)
    step = packed.shape[0] // (2 * parts)
    for mirror in range(2):
        for e in range(parts):
            first = (mirror * parts + e) * step
            for r in range(kept):
                row = band_rows - 1 - r if mirror else r
                packed[first : first + channels, r * LANES : (r + 1) * LANES] = turned[
                    mirror * parts + e, pl.ds(row, channels, stride=band_rows), :
                ]
    result = lax.dot_general(
        packed[...].astype(jnp.bfloat16),
        functions[...],
        (((1,), (1,)), ((), ())),
        preferred_element_type=jnp.float32,
    )
    even = lax.broadcasted_iota(jnp.int32, (channels, waves), 1) % 2 == 0
    for e in range(parts):
        near_half = result[e * step : e * step + channels, :]
        far_half = result[(parts + e) * step : (parts + e) * step + channels, :]
        out[:, e, :] = near_half + jnp.where(even, far_half, -far_half)


def legendre_inputs(order, bands, band_rows, waves, total_lat):
    spread = lax.optimization_barrier(jnp.broadcast_to(order, (band_rows, LANES)))
    order_real = spread.astype(jnp.float32)
    band = jnp.minimum(lax.broadcasted_iota(jnp.int32, (band_rows, LANES), 1), bands - 1)
    cycle = band * band_rows + lax.broadcasted_iota(jnp.int32, (band_rows, LANES), 0) + HALO
    cycle = cycle % total_lat
    angles = (cycle.astype(jnp.float32) + 0.5) * (math.pi / total_lat)
    sine = jnp.sin(angles)
    log_start = (
        0.5 * math.log(0.5)
        + 0.5 * (lax.lgamma(order_real + 1.5) - LGAMMA_HALF_THREE - lax.lgamma(order_real + 1.0))
        + order_real * jnp.log(sine)
    )
    order_real = order.astype(jnp.float32)
    degree = order_real + jnp.arange(1, waves + 1, dtype=jnp.int32).astype(jnp.float32)
    step_a = jnp.sqrt((4.0 * degree * degree - 1.0) / (degree * degree - order_real * order_real))
    before = degree - 1.0
    step_b = jnp.sqrt(
        jnp.maximum(
            (before * before - order_real * order_real) / (4.0 * before * before - 1.0), 0.0
        )
    )
    inside = jnp.arange(1, waves + 1, dtype=jnp.int32) < waves - order
    return (
        jnp.where(inside, step_a, 0.0),
        jnp.where(inside, step_a * step_b, 0.0),
        jnp.cos(angles),
        log_start,
        sine * (math.pi / math.sqrt(total_lat)),
    )


def near(array):
    return pltpu.with_memory_space_constraint(array, pltpu.VMEM)


def smem():
    return pl.BlockSpec(memory_space=pltpu.SMEM)


def vmem():
    return pl.BlockSpec(memory_space=pltpu.VMEM)


def fourier_table(row_waves, limits, following, points):
    return pl.pallas_call(
        functools.partial(fourier_kernel, points=points),
        out_shape=(
            pltpu.VMEM((row_waves.shape[0], points + LANES), jnp.bfloat16),
            pltpu.VMEM((1, LANES), jnp.float32),
        ),
        in_specs=[vmem()] * 3,
        out_specs=(vmem(),) * 2,
        scratch_shapes=[pltpu.VMEM((following.shape[1], LANES), jnp.float32)],
        name="fourier",
        compiler_params=pltpu.CompilerParams(vmem_limit_bytes=GRANT),
    )(*map(near, (row_waves, limits, following)))


def legendre_table(order, bands, band_rows, waves):
    step_a, step_c, *planes = legendre_inputs(order, bands, band_rows, waves, bands * band_rows)
    return pl.pallas_call(
        functools.partial(legendre_kernel, waves=waves, band_rows=band_rows),
        out_shape=pltpu.VMEM((waves, band_rows // 2 * LANES), jnp.bfloat16),
        in_specs=[smem(), smem(), vmem(), vmem(), vmem()],
        out_specs=vmem(),
        scratch_shapes=[pltpu.VMEM((BLOCK * band_rows, LANES), jnp.float32)],
        name="legendre",
        compiler_params=pltpu.CompilerParams(vmem_limit_bytes=GRANT),
    )(step_a, step_c, *map(near, planes))


def pack(limits, prognostic, departure, lat_weight, lon_weight):
    channels, band_rows, sector_cols = prognostic.shape
    return pl.pallas_call(
        pack_kernel,
        out_shape=(
            pltpu.VMEM((channels + 4, band_rows, sector_cols), jnp.bfloat16),
            pltpu.VMEM(prognostic.shape, jnp.bfloat16),
            pltpu.VMEM((3, band_rows, sector_cols), jnp.float32),
        ),
        in_specs=[vmem()] * 5,
        out_specs=(vmem(),) * 3,
        scratch_shapes=[pltpu.VMEM((band_rows, sector_cols), jnp.float32)],
        name="pack",
    )(limits, prognostic, departure, lat_weight, lon_weight)


def interpolate(place, field, own, following, copies):
    channels, band_rows, sector_cols = field.shape
    tall = band_rows + 2 * HALO
    tiles = sector_cols // LANES
    height = channels * band_rows + tall
    count = 2 * HALO + 1
    return pl.pallas_call(
        arrival_kernel,
        out_shape=pltpu.VMEM((copies, height, sector_cols), jnp.bfloat16),
        in_specs=[vmem()] * 4,
        out_specs=vmem(),
        scratch_shapes=[
            pltpu.VMEM((channels, tiles, tall, LANES), jnp.float32),
            pltpu.VMEM((2, count, tiles, tall, LANES), jnp.float32),
            pltpu.VMEM((2 * count, band_rows, sector_cols), jnp.float32),
            pltpu.VMEM((height, sector_cols), jnp.float32),
        ],
        name="arrival",
    )(*map(near, (place, field, own, following)))


def transform(cycles, fourier, row_waves, limits, channels, band_rows):
    return pl.pallas_call(
        transform_kernel,
        out_shape=pltpu.VMEM((fourier.shape[0], LANES), jnp.bfloat16),
        in_specs=[vmem()] * 4,
        out_specs=vmem(),
        scratch_shapes=[
            pltpu.VMEM((2 * HALO + 1, 1, band_rows + 2 * HALO, LANES), jnp.float32),
            pltpu.VMEM((channels * band_rows, LANES), jnp.float32),
        ],
        name="transform",
        compiler_params=pltpu.CompilerParams(vmem_limit_bytes=GRANT),
    )(*map(near, (cycles, fourier, row_waves, limits)))


def synthesize(data, functions, channels):
    waves, span = functions.shape
    return pl.pallas_call(
        synthesis_kernel,
        out_shape=jax.ShapeDtypeStruct((channels, 2, waves), jnp.float32),
        in_specs=[vmem()] * 2,
        out_specs=vmem(),
        scratch_shapes=[
            pltpu.VMEM((4, LANES, LANES), jnp.float32),
            pltpu.VMEM((64, span), jnp.float32),
        ],
        name="synthesis",
        compiler_params=pltpu.CompilerParams(vmem_limit_bytes=GRANT),
    )(near(data), near(functions))


def shards(prognostic, departure, lat_weight, lon_weight, cycle_waves, wave_order):
    band_rows = prognostic.shape[1]
    bands = lax.axis_size("lat")
    sectors = lax.axis_size("lon")
    total_lon = prognostic.shape[2] * sectors
    waves = wave_order.shape[0]
    band_index = lax.axis_index("lat")
    sector_index = lax.axis_index("lon")

    packed, field, own = pack(
        cycle_waves[None], prognostic, departure, lat_weight, lon_weight
    )
    following = lax.ppermute(packed, "lat", [((i + 1) % bands, i) for i in range(bands)])
    number = lax.broadcasted_iota(jnp.int32, (4, band_rows, LANES), 0)
    place = jnp.where(
        number < 3, (sector_index >> number) & 1, (band_index == bands - 1).astype(jnp.int32)
    ).astype(jnp.float32)
    arrival = interpolate(place, field, own, following, sectors)
    cycles = lax.all_to_all(arrival, "lon", split_axis=0, concat_axis=0, tiled=True)

    slot_waves = wave_order.reshape(bands, sectors)
    own_waves = lax.dynamic_slice_in_dim(slot_waves, sector_index, 1, axis=1)
    order = lax.dynamic_slice_in_dim(wave_order, band_index * sectors + sector_index, 1)
    row_waves = jnp.broadcast_to(own_waves[:, :, None], (bands, 2, LANES)).reshape(
        2 * bands, LANES
    )
    fourier, limits = fourier_table(row_waves, cycle_waves[None], following, total_lon)
    functions = legendre_table(order, bands, band_rows, waves)
    cycles, functions = lax.optimization_barrier((cycles, functions))
    masked = transform(cycles, fourier, row_waves, limits, prognostic.shape[0], band_rows)
    data = lax.all_to_all(
        masked.reshape(bands, 2, LANES), "lat", split_axis=0, concat_axis=0, tiled=True
    ).reshape(2 * bands, LANES)
    spectral = synthesize(data, functions, prognostic.shape[0])
    return spectral.transpose(1, 0, 2)[None]


def solution(mesh):
    in_specs = (
        P(None, "lat", "lon"),
        P("lat", "lon"),
        P("lat", "lon"),
        P("lat", "lon"),
        P("lat"),
        P(),
    )
    out_specs = P(("lat", "lon"), None, None, None)
    return jax.shard_map(shards, mesh=mesh, in_specs=in_specs, out_specs=out_specs, check_vma=False)
```

```python
import functools
import math

import jax
import jax.numpy as jnp
from jax import lax
from jax.experimental import pallas as pl
from jax.experimental.pallas import tpu as pltpu
from jax.sharding import PartitionSpec as P

HALO = 4
LANES = 128
BLOCK = 32
GRANT = 16 << 20
WINDOW = 4 * HALO
LGAMMA_HALF_THREE = 0.5 * math.log(math.pi) - math.log(2.0)
SINE = (
    3.1415926535897932,
    -5.1677127800499700,
    2.5501640398773455,
    -0.59926452932079211,
    0.082145886611128233,
    -0.0073704309457143504,
)


def fourier_kernel(waves, limits, following, out, bound, line, *, points):
    rows, group = waves.shape[0], 64
    scale = 1.0 / math.sqrt(points)
    row = lax.broadcasted_iota(jnp.int32, (group, LANES), 0)
    turn = (row % 2 * (points // 4)).astype(jnp.float32)
    place = lax.broadcasted_iota(jnp.int32, (group, LANES), 1)
    lane = place.astype(jnp.float32)
    column = (
        (place // WINDOW + 1) * (points * WINDOW // LANES) - 2 * HALO + place % WINDOW
    ).astype(jnp.float32)

    def cosine(phase):
        phase = phase - jnp.floor(phase * (1.0 / points) + 0.5) * float(points)
        z = 0.5 - jnp.abs(phase) * (2.0 / points)
        square = z * z
        total = jnp.full_like(z, SINE[-1])
        for factor in SINE[-2::-1]:
            total = total * square + factor
        return total * z

    def block(g, carry):
        first = pl.multiple_of(g * group, group)
        wave = waves[pl.ds(first, group), :].astype(jnp.float32)
        phase = lane * wave + turn
        real = cosine(phase) * scale
        imag = cosine(phase - points / 4) * scale
        ahead = wave * float(LANES)
        turn_real = cosine(ahead)
        turn_imag = cosine(ahead - points / 4)
        for t in range(points // LANES):
            out[pl.ds(first, group), t * LANES : (t + 1) * LANES] = real.astype(jnp.bfloat16)
            real, imag = (
                real * turn_real - imag * turn_imag,
                imag * turn_real + real * turn_imag,
            )
        edge = cosine(column * wave + turn) * scale
        out[pl.ds(first, group), points : points + LANES] = edge.astype(jnp.bfloat16)
        return carry

    lax.fori_loop(0, rows // group, block, 0)

    band_rows = limits.shape[1]
    line[...] = jnp.zeros_like(line)
    line[:1, :band_rows] = limits[...].astype(jnp.float32)
    own = line[...]
    last = following[following.shape[0] - 1].astype(jnp.float32)
    ahead = last[:, :LANES] * 256.0 + last[:, LANES : 2 * LANES]
    width = band_rows
    while width < LANES:
        own = own + pltpu.roll(own, width, 1)
        ahead = ahead + pltpu.roll(ahead, width, 1)
        width *= 2
    bound[...] = jnp.where(
        place[:1] % band_rows < HALO,
        pltpu.roll(own, LANES - HALO, 1)[:1],
        pltpu.roll(ahead, HALO, 1)[HALO : HALO + 1],
    )


def legendre_kernel(step_a, step_c, cosine, log_start, weight, out, stage, *, waves, band_rows):
    cos = cosine[...]
    start = log_start[...]
    scale = weight[...]

    def block(t, carry):
        current, last, log_scale = carry
        base = t * BLOCK
        size = jnp.exp(log_scale + start) * scale
        for u in range(0, BLOCK, 2):
            first_a = step_a[base + u] * cos
            second_a = step_a[base + u + 1] * cos
            first_c = step_c[base + u]
            middle = first_a * current - first_c * last
            fresh = (second_a * first_a - step_c[base + u + 1]) * current - (
                second_a * first_c
            ) * last
            stage[band_rows * u : band_rows * (u + 1), :] = current * size
            stage[band_rows * (u + 1) : band_rows * (u + 2), :] = middle * size
            last = middle
            current = fresh
        row = pl.multiple_of(base, BLOCK)
        for r in range(band_rows // 2):
            out[pl.ds(row, BLOCK), r * LANES : (r + 1) * LANES] = stage[
                pl.ds(r, BLOCK, stride=band_rows), :
            ].astype(jnp.bfloat16)
        factor = jnp.maximum(jnp.maximum(jnp.abs(current), jnp.abs(last)), 1.0)
        inverse = 1.0 / factor
        return current * inverse, last * inverse, log_scale + jnp.log(factor)

    initial = (jnp.ones_like(cos), jnp.zeros_like(cos), jnp.zeros_like(cos))
    lax.fori_loop(0, waves // BLOCK, block, initial)


def spread(place, share):
    return [
        jnp.where(place == d, 1.0 - share, jnp.where(place == d - 1, share, 0.0))
        for d in range(2 * HALO + 1)
    ]


def edges(tall, slot):
    lane = lax.broadcasted_iota(jnp.int32, tall[0].shape, 1)
    reach = 2 * HALO
    ends = jnp.where(
        lane < reach, tall[0], jnp.where(lane >= LANES - reach, tall[-1], jnp.zeros_like(tall[0]))
    )
    return pltpu.roll(ends, slot * WINDOW + reach, 1)


def stencil(read, write, row_parts, col_parts, tiles, rows):
    count = 2 * HALO + 1
    source = read()
    lane = lax.broadcasted_iota(jnp.int32, source[0].shape, 1)
    for d in range(count):
        move = d - HALO
        if move == 0:
            turned = source
        else:
            rolled = [pltpu.roll(tile, -move % LANES, 1) for tile in source]
            if tiles == 1:
                turned = rolled
            elif move > 0:
                turned = [
                    jnp.where(lane < LANES - move, rolled[t], rolled[(t + 1) % tiles])
                    for t in range(tiles)
                ]
            else:
                turned = [
                    jnp.where(lane < -move, rolled[t - 1], rolled[t]) for t in range(tiles)
                ]
        for t in range(tiles):
            write[d, t] = turned[t]
    sums = []
    for t in range(tiles):
        total = None
        for e in range(count):
            inner = None
            for d in range(count):
                term = col_parts(d, t) * write[d, t, e : e + rows, :]
                inner = term if inner is None else inner + term
            term = row_parts(e, t) * inner
            total = term if total is None else total + term
        sums.append(total)
    return sums


def split(value):
    high = value.astype(jnp.bfloat16).astype(jnp.float32)
    rest = value - high
    middle = rest.astype(jnp.bfloat16).astype(jnp.float32)
    return [high, middle, rest - middle]


def pack_kernel(limits, field, departure, lat_weight, lon_weight, out, field_out, own, line):
    channels = field.shape[0]
    cols = departure.shape[1]
    value = field[...]
    field_out[...] = value
    out[:channels] = value
    cell = departure[...].astype(jnp.float32)
    a = lat_weight[...]
    b = lon_weight[...]
    for p, plane in enumerate((cell, a, b)):
        own[p] = plane
    planes = [v[:HALO] for v in [cell] + split(a) + split(b)]
    for p in range(0, len(planes) - 1, 2):
        pair = jnp.concatenate(planes[p : p + 2], axis=0)
        out[channels + p // 2] = pair.astype(jnp.bfloat16)
    rows = limits.shape[1]
    bound = limits[...].astype(jnp.float32)
    high = jnp.floor(bound * (1.0 / 256.0))
    line[:HALO] = planes[-1]
    line[HALO:] = jnp.zeros_like(planes[-1])
    line[HALO : HALO + 1, :rows] = high
    line[HALO : HALO + 1, LANES : LANES + rows] = bound - high * 256.0
    out[channels + len(planes) // 2] = line[...].astype(jnp.bfloat16)


def arrival_kernel(place, field, own, following, out, grid, shifted, parts, stage):
    channels, rows, cols = field.shape
    tiles = cols // LANES
    count = 2 * HALO + 1
    used = channels * rows
    pitch = used + rows
    lane = lax.broadcasted_iota(jnp.int32, (rows, LANES), 1)
    row = lax.broadcasted_iota(jnp.int32, (rows, cols), 0)
    last = jnp.concatenate([place[3]] * tiles, axis=1)
    pairs = [following[channels + p].astype(jnp.float32) for p in range(4)]
    ahead = [pairs[p // 2][p % 2 * HALO : (p % 2 + 1) * HALO] for p in range(7)]

    def rows_of(plane, rest):
        return jnp.concatenate([plane[HALO:], rest], axis=0)

    cell = rows_of(own[0], ahead[0])
    a = rows_of(own[1], ahead[1] + ahead[2] + ahead[3])
    b = rows_of(own[2], ahead[4] + ahead[5] + ahead[6])
    high = jnp.floor(cell * (1.0 / (2 * HALO)))
    for e, part in enumerate(spread(high, a)):
        parts[e] = jnp.where((row < HALO) == (row + e < rows), part, part * (1.0 - last))
    for d, part in enumerate(spread(cell - high * (2 * HALO), b)):
        parts[count + d] = part
    total = None
    for p, plane in enumerate([cell + last * (4 * HALO * HALO)] + split(a) + split(b)):
        term = edges([plane[:, t * LANES : (t + 1) * LANES] for t in range(tiles)], p + 1)
        total = term if total is None else total + term
    planes = total
    for c in range(channels):
        here = field[c].astype(jnp.float32)
        there = following[c].astype(jnp.float32)
        for t in range(tiles):
            span = slice(t * LANES, (t + 1) * LANES)
            grid[c, t, :rows, :] = here[:, span]
            grid[c, t, rows:, :] = there[:, span]

    def part(first):
        return lambda d, t: parts[first + d, :, t * LANES : (t + 1) * LANES]

    for c in range(channels):
        sums = stencil(
            lambda: [grid[c, t] for t in range(tiles)],
            shifted.at[c % 2],
            part(0),
            part(count),
            tiles,
            rows,
        )
        sums[0] = jnp.where(lane < HALO, 0.0, sums[0])
        sums[-1] = jnp.where(lane >= LANES - HALO, 0.0, sums[-1])
        for t in range(tiles):
            stage[t * pitch + c * rows : t * pitch + (c + 1) * rows, :] = sums[t]
    slots = LANES // WINDOW
    bits = [jnp.concatenate([place[k]] * 2, axis=0) > 0.0 for k in range(3)]
    for g in range(2):
        total = None
        for c in range(g * slots, min((g + 1) * slots, channels)):
            term = edges([grid[c, 0], grid[c, tiles - 1]], c - g * slots)
            total = term if total is None else total + term
        if g == 1:
            total = total + jnp.concatenate([planes, jnp.zeros_like(planes)], axis=0)
        for k in range(3):
            total = jnp.where(bits[k], pltpu.roll(total, WINDOW << k, 1), total)
        if g == 0:
            stage[used:pitch, :] = total[:rows]
            stage[pitch + used : 2 * pitch, :] = total[rows:]
        else:
            stage[2 * pitch + used :, :] = total
    value = stage[...].astype(jnp.bfloat16)
    for copy in range(out.shape[0]):
        out[copy] = value


def transform_kernel(cycles, fourier, waves, limits, out, shifted, stage):
    sectors = cycles.shape[0]
    used, rows = stage.shape[0], shifted.shape[2] - 2 * HALO
    tall = rows + 2 * HALO
    channels = used // rows
    slots = LANES // WINDOW
    slot = lax.broadcasted_iota(jnp.int32, (tall, LANES), 1) // WINDOW
    inner = lax.broadcasted_iota(jnp.int32, (tall, LANES), 1) % WINDOW
    pitch = used + rows
    tiles = cycles.shape[1] // pitch

    def piece(sector, first, count):
        return cycles[sector, first : first + count, :].astype(jnp.float32)

    pieces = [
        [
            jnp.concatenate(
                [piece(sector, used, rows), piece(sector, pitch + used, rows)], axis=0
            )
            for sector in range(sectors)
        ],
        [piece(sector, 2 * pitch + used, tall) for sector in range(sectors)],
    ]

    def window(index, height):
        g, c = divmod(index, slots)
        total = pieces[g][0][:height]
        for sector in range(1, sectors):
            total = jnp.where(
                slot[:height] == (c + sector) % slots, pieces[g][sector][:height], total
            )
        left = pltpu.roll(total, -c * WINDOW % LANES, 1) if c else total
        right = pltpu.roll(total, -(c + 1) * WINDOW % LANES, 1) if c + 1 < slots else total
        return jnp.where(inner[:height] < 2 * HALO, left, right)

    cell, *weights = [window(channels + p, rows) for p in range(7)]
    last = (cell >= 4 * HALO * HALO).astype(jnp.float32)
    cell = cell - last * (4 * HALO * HALO)
    row = lax.broadcasted_iota(jnp.int32, cell.shape, 0)
    a = weights[0] + weights[1] + weights[2]
    b = weights[3] + weights[4] + weights[5]
    high = jnp.floor(cell * (1.0 / (2 * HALO)))
    row_parts = [
        jnp.where((row < HALO) == (row + e < rows), part, part * (1.0 - last))
        for e, part in enumerate(spread(high, a))
    ]
    col_parts = spread(cell - high * (2 * HALO), b)
    inside = (inner[:rows] >= HALO) & (inner[:rows] < 3 * HALO)
    for c in range(channels):
        (total,) = stencil(
            lambda: [window(c, tall)],
            shifted,
            lambda e, t: row_parts[e],
            lambda d, t: col_parts[d],
            1,
            rows,
        )
        stage[c * rows : (c + 1) * rows, :] = jnp.where(inside, total, 0.0)
    gathered = jnp.concatenate(
        [
            cycles[sector, t * pitch : t * pitch + used, :]
            for sector in range(sectors)
            for t in range(tiles)
        ]
        + [stage[...].astype(jnp.bfloat16)],
        axis=1,
    )
    spectrum = lax.dot_general(
        fourier[...], gathered, (((1,), (1,)), ((), ())), preferred_element_type=jnp.float32
    )
    resolved = waves[:, :used].astype(jnp.float32) < limits[:, :used]
    out[:, :used] = jnp.where(resolved, spectrum, 0.0).astype(jnp.bfloat16)
    out[:, used:] = jnp.zeros((out.shape[0], out.shape[1] - used), jnp.bfloat16)


def synthesis_kernel(data, functions, out, turned, packed):
    channels, parts, waves = out.shape
    bands = data.shape[0] // parts
    kept = packed.shape[1] // LANES
    band_rows = 2 * kept
    source = lax.broadcasted_iota(jnp.int32, (parts * bands, LANES), 0)
    target = lax.broadcasted_iota(jnp.int32, (parts * bands, LANES), 1)
    chosen = [
        (source == parts * band + e).astype(jnp.float32).astype(jnp.bfloat16)
        for band in (target, jnp.where(target == bands - 1, target, bands - 2 - target))
        for e in range(parts)
    ]
    columns = lax.dot_general(
        data[...],
        jnp.concatenate(chosen, axis=1),
        (((0,), (0,)), ((), ())),
        preferred_element_type=jnp.float32,
    )
    for place in range(2 * parts):
        turned[place] = columns[:, place * LANES : (place + 1) * LANES]
    packed[...] = jnp.zeros_like(packed)
    step = packed.shape[0] // (2 * parts)
    for mirror in range(2):
        for e in range(parts):
            first = (mirror * parts + e) * step
            for r in range(kept):
                row = band_rows - 1 - r if mirror else r
                packed[first : first + channels, r * LANES : (r + 1) * LANES] = turned[
                    mirror * parts + e, pl.ds(row, channels, stride=band_rows), :
                ]
    result = lax.dot_general(
        packed[...].astype(jnp.bfloat16),
        functions[...],
        (((1,), (1,)), ((), ())),
        preferred_element_type=jnp.float32,
    )
    even = lax.broadcasted_iota(jnp.int32, (channels, waves), 1) % 2 == 0
    for e in range(parts):
        near_half = result[e * step : e * step + channels, :]
        far_half = result[(parts + e) * step : (parts + e) * step + channels, :]
        out[:, e, :] = near_half + jnp.where(even, far_half, -far_half)


def legendre_inputs(order, bands, band_rows, waves, total_lat):
    spread = lax.optimization_barrier(jnp.broadcast_to(order, (band_rows, LANES)))
    order_real = spread.astype(jnp.float32)
    band = jnp.minimum(lax.broadcasted_iota(jnp.int32, (band_rows, LANES), 1), bands - 1)
    cycle = band * band_rows + lax.broadcasted_iota(jnp.int32, (band_rows, LANES), 0) + HALO
    cycle = cycle % total_lat
    angles = (cycle.astype(jnp.float32) + 0.5) * (math.pi / total_lat)
    sine = jnp.sin(angles)
    log_start = (
        0.5 * math.log(0.5)
        + 0.5 * (lax.lgamma(order_real + 1.5) - LGAMMA_HALF_THREE - lax.lgamma(order_real + 1.0))
        + order_real * jnp.log(sine)
    )
    order_real = order.astype(jnp.float32)
    degree = order_real + jnp.arange(1, waves + 1, dtype=jnp.int32).astype(jnp.float32)
    step_a = jnp.sqrt((4.0 * degree * degree - 1.0) / (degree * degree - order_real * order_real))
    before = degree - 1.0
    step_b = jnp.sqrt(
        jnp.maximum(
            (before * before - order_real * order_real) / (4.0 * before * before - 1.0), 0.0
        )
    )
    inside = jnp.arange(1, waves + 1, dtype=jnp.int32) < waves - order
    return (
        jnp.where(inside, step_a, 0.0),
        jnp.where(inside, step_a * step_b, 0.0),
        jnp.cos(angles),
        log_start,
        sine * (math.pi / math.sqrt(total_lat)),
    )


def near(array):
    return pltpu.with_memory_space_constraint(array, pltpu.VMEM)


def smem():
    return pl.BlockSpec(memory_space=pltpu.SMEM)


def vmem():
    return pl.BlockSpec(memory_space=pltpu.VMEM)


def fourier_table(row_waves, limits, following, points):
    return pl.pallas_call(
        functools.partial(fourier_kernel, points=points),
        out_shape=(
            pltpu.VMEM((row_waves.shape[0], points + LANES), jnp.bfloat16),
            pltpu.VMEM((1, LANES), jnp.float32),
        ),
        in_specs=[vmem()] * 3,
        out_specs=(vmem(),) * 2,
        scratch_shapes=[pltpu.VMEM((following.shape[1], LANES), jnp.float32)],
        name="fourier",
        compiler_params=pltpu.CompilerParams(vmem_limit_bytes=GRANT),
    )(*map(near, (row_waves, limits, following)))


def legendre_table(order, bands, band_rows, waves):
    step_a, step_c, *planes = legendre_inputs(order, bands, band_rows, waves, bands * band_rows)
    return pl.pallas_call(
        functools.partial(legendre_kernel, waves=waves, band_rows=band_rows),
        out_shape=pltpu.VMEM((waves, band_rows // 2 * LANES), jnp.bfloat16),
        in_specs=[smem(), smem(), vmem(), vmem(), vmem()],
        out_specs=vmem(),
        scratch_shapes=[pltpu.VMEM((BLOCK * band_rows, LANES), jnp.float32)],
        name="legendre",
        compiler_params=pltpu.CompilerParams(vmem_limit_bytes=GRANT),
    )(step_a, step_c, *map(near, planes))


def pack(limits, prognostic, departure, lat_weight, lon_weight):
    channels, band_rows, sector_cols = prognostic.shape
    return pl.pallas_call(
        pack_kernel,
        out_shape=(
            pltpu.VMEM((channels + 4, band_rows, sector_cols), jnp.bfloat16),
            pltpu.VMEM(prognostic.shape, jnp.bfloat16),
            pltpu.VMEM((3, band_rows, sector_cols), jnp.float32),
        ),
        in_specs=[vmem()] * 5,
        out_specs=(vmem(),) * 3,
        scratch_shapes=[pltpu.VMEM((band_rows, sector_cols), jnp.float32)],
        name="pack",
    )(limits, prognostic, departure, lat_weight, lon_weight)


def interpolate(place, field, own, following, copies):
    channels, band_rows, sector_cols = field.shape
    tall = band_rows + 2 * HALO
    tiles = sector_cols // LANES
    height = tiles * (channels + 1) * band_rows + band_rows
    count = 2 * HALO + 1
    return pl.pallas_call(
        arrival_kernel,
        out_shape=pltpu.VMEM((copies, height, LANES), jnp.bfloat16),
        in_specs=[vmem()] * 4,
        out_specs=vmem(),
        scratch_shapes=[
            pltpu.VMEM((channels, tiles, tall, LANES), jnp.float32),
            pltpu.VMEM((2, count, tiles, tall, LANES), jnp.float32),
            pltpu.VMEM((2 * count, band_rows, sector_cols), jnp.float32),
            pltpu.VMEM((height, LANES), jnp.float32),
        ],
        name="arrival",
    )(*map(near, (place, field, own, following)))


def transform(cycles, fourier, row_waves, limits, channels, band_rows):
    return pl.pallas_call(
        transform_kernel,
        out_shape=pltpu.VMEM((fourier.shape[0], LANES), jnp.bfloat16),
        in_specs=[vmem()] * 4,
        out_specs=vmem(),
        scratch_shapes=[
            pltpu.VMEM((2 * HALO + 1, 1, band_rows + 2 * HALO, LANES), jnp.float32),
            pltpu.VMEM((channels * band_rows, LANES), jnp.float32),
        ],
        name="transform",
        compiler_params=pltpu.CompilerParams(vmem_limit_bytes=GRANT),
    )(*map(near, (cycles, fourier, row_waves, limits)))


def synthesize(data, functions, channels):
    waves, span = functions.shape
    return pl.pallas_call(
        synthesis_kernel,
        out_shape=jax.ShapeDtypeStruct((channels, 2, waves), jnp.float32),
        in_specs=[vmem()] * 2,
        out_specs=vmem(),
        scratch_shapes=[
            pltpu.VMEM((4, LANES, LANES), jnp.float32),
            pltpu.VMEM((64, span), jnp.float32),
        ],
        name="synthesis",
        compiler_params=pltpu.CompilerParams(vmem_limit_bytes=GRANT),
    )(near(data), near(functions))


def shards(prognostic, departure, lat_weight, lon_weight, cycle_waves, wave_order):
    band_rows = prognostic.shape[1]
    bands = lax.axis_size("lat")
    sectors = lax.axis_size("lon")
    total_lon = prognostic.shape[2] * sectors
    waves = wave_order.shape[0]
    band_index = lax.axis_index("lat")
    sector_index = lax.axis_index("lon")

    packed, field, own = pack(
        cycle_waves[None], prognostic, departure, lat_weight, lon_weight
    )
    following = lax.ppermute(packed, "lat", [((i + 1) % bands, i) for i in range(bands)])
    number = lax.broadcasted_iota(jnp.int32, (4, band_rows, LANES), 0)
    place = jnp.where(
        number < 3, (sector_index >> number) & 1, (band_index == bands - 1).astype(jnp.int32)
    ).astype(jnp.float32)
    arrival = interpolate(place, field, own, following, sectors)
    cycles = lax.all_to_all(arrival, "lon", split_axis=0, concat_axis=0, tiled=True)

    slot_waves = wave_order.reshape(bands, sectors)
    own_waves = lax.dynamic_slice_in_dim(slot_waves, sector_index, 1, axis=1)
    order = lax.dynamic_slice_in_dim(wave_order, band_index * sectors + sector_index, 1)
    row_waves = jnp.broadcast_to(own_waves[:, :, None], (bands, 2, LANES)).reshape(
        2 * bands, LANES
    )
    fourier, limits = fourier_table(row_waves, cycle_waves[None], following, total_lon)
    functions = legendre_table(order, bands, band_rows, waves)
    cycles, functions = lax.optimization_barrier((cycles, functions))
    masked = transform(cycles, fourier, row_waves, limits, prognostic.shape[0], band_rows)
    data = lax.all_to_all(
        masked.reshape(bands, 2, LANES), "lat", split_axis=0, concat_axis=0, tiled=True
    ).reshape(2 * bands, LANES)
    spectral = synthesize(data, functions, prognostic.shape[0])
    return spectral.transpose(1, 0, 2)[None]


def solution(mesh):
    in_specs = (
        P(None, "lat", "lon"),
        P("lat", "lon"),
        P("lat", "lon"),
        P("lat", "lon"),
        P("lat"),
        P(),
    )
    out_specs = P(("lat", "lon"), None, None, None)
    return jax.shard_map(shards, mesh=mesh, in_specs=in_specs, out_specs=out_specs, check_vma=False)
```

```python
import functools
import math

import jax
import jax.numpy as jnp
from jax import lax
from jax.experimental import pallas as pl
from jax.experimental.pallas import tpu as pltpu
from jax.sharding import PartitionSpec as P

HALO = 4
LANES = 128
BLOCK = 32
GRANT = 16 << 20
WINDOW = 4 * HALO
LGAMMA_HALF_THREE = 0.5 * math.log(math.pi) - math.log(2.0)
SINE = (
    3.1415926535897932,
    -5.1677127800499700,
    2.5501640398773455,
    -0.59926452932079211,
    0.082145886611128233,
    -0.0073704309457143504,
)


def fourier_kernel(waves, limits, following, out, bound, line, *, points):
    rows, group = waves.shape[0], 64
    scale = 1.0 / math.sqrt(points)
    row = lax.broadcasted_iota(jnp.int32, (group, LANES), 0)
    turn = (row % 2 * (points // 4)).astype(jnp.float32)
    place = lax.broadcasted_iota(jnp.int32, (group, LANES), 1)
    lane = place.astype(jnp.float32)
    column = (
        (place // WINDOW + 1) * (points * WINDOW // LANES) - 2 * HALO + place % WINDOW
    ).astype(jnp.float32)

    def cosine(phase):
        phase = phase - jnp.floor(phase * (1.0 / points) + 0.5) * float(points)
        z = 0.5 - jnp.abs(phase) * (2.0 / points)
        square = z * z
        total = jnp.full_like(z, SINE[-1])
        for factor in SINE[-2::-1]:
            total = total * square + factor
        return total * z

    def block(g, carry):
        first = pl.multiple_of(g * group, group)
        wave = waves[pl.ds(first, group), :].astype(jnp.float32)
        phase = lane * wave + turn
        real = cosine(phase) * scale
        imag = cosine(phase - points / 4) * scale
        ahead = wave * float(LANES)
        turn_real = cosine(ahead)
        turn_imag = cosine(ahead - points / 4)
        for t in range(points // LANES):
            out[pl.ds(first, group), t * LANES : (t + 1) * LANES] = real.astype(jnp.bfloat16)
            real, imag = (
                real * turn_real - imag * turn_imag,
                imag * turn_real + real * turn_imag,
            )
        edge = cosine(column * wave + turn) * scale
        out[pl.ds(first, group), points : points + LANES] = edge.astype(jnp.bfloat16)
        return carry

    lax.fori_loop(0, rows // group, block, 0)

    band_rows = limits.shape[1]
    line[...] = jnp.zeros_like(line)
    line[:1, :band_rows] = limits[...].astype(jnp.float32)
    own = line[...]
    last = following[following.shape[0] - 1].astype(jnp.float32)
    ahead = last[:, :LANES] * 256.0 + last[:, LANES : 2 * LANES]
    width = band_rows
    while width < LANES:
        own = own + pltpu.roll(own, width, 1)
        ahead = ahead + pltpu.roll(ahead, width, 1)
        width *= 2
    bound[...] = jnp.where(
        place[:1] % band_rows < HALO,
        pltpu.roll(own, LANES - HALO, 1)[:1],
        pltpu.roll(ahead, HALO, 1)[HALO : HALO + 1],
    )


def legendre_kernel(step_a, step_c, cosine, log_start, weight, out, stage, *, waves, band_rows):
    cos = cosine[...]
    start = log_start[...]
    scale = weight[...]

    def block(t, carry):
        current, last, log_scale = carry
        base = t * BLOCK
        size = jnp.exp(log_scale + start) * scale
        for u in range(0, BLOCK, 2):
            first_a = step_a[base + u] * cos
            second_a = step_a[base + u + 1] * cos
            first_c = step_c[base + u]
            middle = first_a * current - first_c * last
            fresh = (second_a * first_a - step_c[base + u + 1]) * current - (
                second_a * first_c
            ) * last
            stage[band_rows * u : band_rows * (u + 1), :] = current * size
            stage[band_rows * (u + 1) : band_rows * (u + 2), :] = middle * size
            last = middle
            current = fresh
        row = pl.multiple_of(base, BLOCK)
        for r in range(band_rows // 2):
            out[pl.ds(row, BLOCK), r * LANES : (r + 1) * LANES] = stage[
                pl.ds(r, BLOCK, stride=band_rows), :
            ].astype(jnp.bfloat16)
        factor = jnp.maximum(jnp.maximum(jnp.abs(current), jnp.abs(last)), 1.0)
        inverse = 1.0 / factor
        return current * inverse, last * inverse, log_scale + jnp.log(factor)

    initial = (jnp.ones_like(cos), jnp.zeros_like(cos), jnp.zeros_like(cos))
    lax.fori_loop(0, waves // BLOCK, block, initial)


def spread(place, share):
    return [
        jnp.where(place == d, 1.0 - share, jnp.where(place == d - 1, share, 0.0))
        for d in range(2 * HALO + 1)
    ]


def edges(tall, slot):
    lane = lax.broadcasted_iota(jnp.int32, tall[0].shape, 1)
    reach = 2 * HALO
    ends = jnp.where(
        lane < reach, tall[0], jnp.where(lane >= LANES - reach, tall[-1], jnp.zeros_like(tall[0]))
    )
    return pltpu.roll(ends, slot * WINDOW + reach, 1)


def stencil(read, write, row_parts, col_parts, tiles, rows):
    count = 2 * HALO + 1
    source = read()
    lane = lax.broadcasted_iota(jnp.int32, source[0].shape, 1)
    for d in range(count):
        move = d - HALO
        if move == 0:
            turned = source
        else:
            rolled = [pltpu.roll(tile, -move % LANES, 1) for tile in source]
            if tiles == 1:
                turned = rolled
            elif move > 0:
                turned = [
                    jnp.where(lane < LANES - move, rolled[t], rolled[(t + 1) % tiles])
                    for t in range(tiles)
                ]
            else:
                turned = [
                    jnp.where(lane < -move, rolled[t - 1], rolled[t]) for t in range(tiles)
                ]
        for t in range(tiles):
            write[d, t] = turned[t]
    sums = []
    for t in range(tiles):
        total = None
        for e in range(count):
            inner = None
            for d in range(count):
                term = col_parts(d, t) * write[d, t, e : e + rows, :]
                inner = term if inner is None else inner + term
            term = row_parts(e, t) * inner
            total = term if total is None else total + term
        sums.append(total)
    return sums


def split(value):
    high = value.astype(jnp.bfloat16).astype(jnp.float32)
    rest = value - high
    middle = rest.astype(jnp.bfloat16).astype(jnp.float32)
    return [high, middle, rest - middle]


def pack_kernel(limits, field, departure, lat_weight, lon_weight, out, field_out, own, line):
    channels = field.shape[0]
    cols = departure.shape[1]
    value = field[...]
    field_out[...] = value
    out[:channels] = value
    cell = departure[...].astype(jnp.float32)
    a = lat_weight[...]
    b = lon_weight[...]
    for p, plane in enumerate((cell, a, b)):
        own[p] = plane
    planes = [v[:HALO] for v in [cell] + split(a) + split(b)]
    for p in range(0, len(planes) - 1, 2):
        pair = jnp.concatenate(planes[p : p + 2], axis=0)
        out[channels + p // 2] = pair.astype(jnp.bfloat16)
    rows = limits.shape[1]
    bound = limits[...].astype(jnp.float32)
    high = jnp.floor(bound * (1.0 / 256.0))
    line[:HALO] = planes[-1]
    line[HALO:] = jnp.zeros_like(planes[-1])
    line[HALO : HALO + 1, :rows] = high
    line[HALO : HALO + 1, LANES : LANES + rows] = bound - high * 256.0
    out[channels + len(planes) // 2] = line[...].astype(jnp.bfloat16)


def arrival_kernel(place, field, own, following, out, grid, shifted, parts, stage):
    channels, rows, cols = field.shape
    tiles = cols // LANES
    count = 2 * HALO + 1
    used = channels * rows
    pitch = used + rows
    lane = lax.broadcasted_iota(jnp.int32, (rows, LANES), 1)
    row = lax.broadcasted_iota(jnp.int32, (rows, cols), 0)
    last = jnp.concatenate([place[3]] * tiles, axis=1)
    pairs = [following[channels + p].astype(jnp.float32) for p in range(4)]
    ahead = [pairs[p // 2][p % 2 * HALO : (p % 2 + 1) * HALO] for p in range(7)]

    def rows_of(plane, rest):
        return jnp.concatenate([plane[HALO:], rest], axis=0)

    cell = rows_of(own[0], ahead[0])
    a = rows_of(own[1], ahead[1] + ahead[2] + ahead[3])
    b = rows_of(own[2], ahead[4] + ahead[5] + ahead[6])
    high = jnp.floor(cell * (1.0 / (2 * HALO)))
    for e, part in enumerate(spread(high, a)):
        parts[e] = jnp.where((row < HALO) == (row + e < rows), part, part * (1.0 - last))
    for d, part in enumerate(spread(cell - high * (2 * HALO), b)):
        parts[count + d] = part
    total = None
    for p, plane in enumerate([cell + last * (4 * HALO * HALO)] + split(a) + split(b)):
        term = edges([plane[:, t * LANES : (t + 1) * LANES] for t in range(tiles)], p + 1)
        total = term if total is None else total + term
    planes = total
    for c in range(channels):
        here = field[c].astype(jnp.float32)
        there = following[c].astype(jnp.float32)
        for t in range(tiles):
            span = slice(t * LANES, (t + 1) * LANES)
            grid[c, t, :rows, :] = here[:, span]
            grid[c, t, rows:, :] = there[:, span]

    def part(first):
        return lambda d, t: parts[first + d, :, t * LANES : (t + 1) * LANES]

    for c in range(channels):
        sums = stencil(
            lambda: [grid[c, t] for t in range(tiles)],
            shifted.at[c % shifted.shape[0]],
            part(0),
            part(count),
            tiles,
            rows,
        )
        sums[0] = jnp.where(lane < HALO, 0.0, sums[0])
        sums[-1] = jnp.where(lane >= LANES - HALO, 0.0, sums[-1])
        for t in range(tiles):
            stage[t * pitch + c * rows : t * pitch + (c + 1) * rows, :] = sums[t]
    slots = LANES // WINDOW
    bits = [jnp.concatenate([place[k]] * 2, axis=0) > 0.0 for k in range(3)]
    for g in range(2):
        total = None
        for c in range(g * slots, min((g + 1) * slots, channels)):
            term = edges([grid[c, 0], grid[c, tiles - 1]], c - g * slots)
            total = term if total is None else total + term
        if g == 1:
            total = total + jnp.concatenate([planes, jnp.zeros_like(planes)], axis=0)
        for k in range(3):
            total = jnp.where(bits[k], pltpu.roll(total, WINDOW << k, 1), total)
        if g == 0:
            stage[used:pitch, :] = total[:rows]
            stage[pitch + used : 2 * pitch, :] = total[rows:]
        else:
            stage[2 * pitch + used :, :] = total
    value = stage[...].astype(jnp.bfloat16)
    for copy in range(out.shape[0]):
        out[copy] = value


def transform_kernel(cycles, fourier, waves, limits, out, shifted, stage):
    sectors = cycles.shape[0]
    used, rows = stage.shape[0], shifted.shape[3] - 2 * HALO
    tall = rows + 2 * HALO
    channels = used // rows
    slots = LANES // WINDOW
    slot = lax.broadcasted_iota(jnp.int32, (tall, LANES), 1) // WINDOW
    inner = lax.broadcasted_iota(jnp.int32, (tall, LANES), 1) % WINDOW
    pitch = used + rows
    tiles = cycles.shape[1] // pitch

    def piece(sector, first, count):
        return cycles[sector, first : first + count, :].astype(jnp.float32)

    pieces = [
        [
            jnp.concatenate(
                [piece(sector, used, rows), piece(sector, pitch + used, rows)], axis=0
            )
            for sector in range(sectors)
        ],
        [piece(sector, 2 * pitch + used, tall) for sector in range(sectors)],
    ]

    def window(index, height):
        g, c = divmod(index, slots)
        total = pieces[g][0][:height]
        for sector in range(1, sectors):
            total = jnp.where(
                slot[:height] == (c + sector) % slots, pieces[g][sector][:height], total
            )
        left = pltpu.roll(total, -c * WINDOW % LANES, 1) if c else total
        right = pltpu.roll(total, -(c + 1) * WINDOW % LANES, 1) if c + 1 < slots else total
        return jnp.where(inner[:height] < 2 * HALO, left, right)

    cell, *weights = [window(channels + p, rows) for p in range(7)]
    last = (cell >= 4 * HALO * HALO).astype(jnp.float32)
    cell = cell - last * (4 * HALO * HALO)
    row = lax.broadcasted_iota(jnp.int32, cell.shape, 0)
    a = weights[0] + weights[1] + weights[2]
    b = weights[3] + weights[4] + weights[5]
    high = jnp.floor(cell * (1.0 / (2 * HALO)))
    row_parts = [
        jnp.where((row < HALO) == (row + e < rows), part, part * (1.0 - last))
        for e, part in enumerate(spread(high, a))
    ]
    col_parts = spread(cell - high * (2 * HALO), b)
    inside = (inner[:rows] >= HALO) & (inner[:rows] < 3 * HALO)
    for c in range(channels):
        (total,) = stencil(
            lambda: [window(c, tall)],
            shifted.at[c % shifted.shape[0]],
            lambda e, t: row_parts[e],
            lambda d, t: col_parts[d],
            1,
            rows,
        )
        stage[c * rows : (c + 1) * rows, :] = jnp.where(inside, total, 0.0)
    gathered = jnp.concatenate(
        [
            cycles[sector, t * pitch : t * pitch + used, :]
            for sector in range(sectors)
            for t in range(tiles)
        ]
        + [stage[...].astype(jnp.bfloat16)],
        axis=1,
    )
    spectrum = lax.dot_general(
        fourier[...], gathered, (((1,), (1,)), ((), ())), preferred_element_type=jnp.float32
    )
    resolved = waves[:, :used].astype(jnp.float32) < limits[:, :used]
    out[:, :used] = jnp.where(resolved, spectrum, 0.0).astype(jnp.bfloat16)
    out[:, used:] = jnp.zeros((out.shape[0], out.shape[1] - used), jnp.bfloat16)


def synthesis_kernel(data, functions, out, turned, packed):
    channels, parts, waves = out.shape
    bands = data.shape[0] // parts
    kept = packed.shape[1] // LANES
    band_rows = 2 * kept
    source = lax.broadcasted_iota(jnp.int32, (parts * bands, LANES), 0)
    target = lax.broadcasted_iota(jnp.int32, (parts * bands, LANES), 1)
    chosen = [
        (source == parts * band + e).astype(jnp.float32).astype(jnp.bfloat16)
        for band in (target, jnp.where(target == bands - 1, target, bands - 2 - target))
        for e in range(parts)
    ]
    columns = lax.dot_general(
        data[...],
        jnp.concatenate(chosen, axis=1),
        (((0,), (0,)), ((), ())),
        preferred_element_type=jnp.float32,
    )
    for place in range(2 * parts):
        turned[place] = columns[:, place * LANES : (place + 1) * LANES]
    packed[...] = jnp.zeros_like(packed)
    step = packed.shape[0] // (2 * parts)
    for mirror in range(2):
        for e in range(parts):
            first = (mirror * parts + e) * step
            for r in range(kept):
                row = band_rows - 1 - r if mirror else r
                packed[first : first + channels, r * LANES : (r + 1) * LANES] = turned[
                    mirror * parts + e, pl.ds(row, channels, stride=band_rows), :
                ]
    result = lax.dot_general(
        packed[...].astype(jnp.bfloat16),
        functions[...],
        (((1,), (1,)), ((), ())),
        preferred_element_type=jnp.float32,
    )
    even = lax.broadcasted_iota(jnp.int32, (channels, waves), 1) % 2 == 0
    for e in range(parts):
        near_half = result[e * step : e * step + channels, :]
        far_half = result[(parts + e) * step : (parts + e) * step + channels, :]
        out[:, e, :] = near_half + jnp.where(even, far_half, -far_half)


def legendre_inputs(order, bands, band_rows, waves, total_lat):
    spread = lax.optimization_barrier(jnp.broadcast_to(order, (band_rows, LANES)))
    order_real = spread.astype(jnp.float32)
    band = jnp.minimum(lax.broadcasted_iota(jnp.int32, (band_rows, LANES), 1), bands - 1)
    cycle = band * band_rows + lax.broadcasted_iota(jnp.int32, (band_rows, LANES), 0) + HALO
    cycle = cycle % total_lat
    angles = (cycle.astype(jnp.float32) + 0.5) * (math.pi / total_lat)
    sine = jnp.sin(angles)
    log_start = (
        0.5 * math.log(0.5)
        + 0.5 * (lax.lgamma(order_real + 1.5) - LGAMMA_HALF_THREE - lax.lgamma(order_real + 1.0))
        + order_real * jnp.log(sine)
    )
    order_real = order.astype(jnp.float32)
    degree = order_real + jnp.arange(1, waves + 1, dtype=jnp.int32).astype(jnp.float32)
    step_a = jnp.sqrt((4.0 * degree * degree - 1.0) / (degree * degree - order_real * order_real))
    before = degree - 1.0
    step_b = jnp.sqrt(
        jnp.maximum(
            (before * before - order_real * order_real) / (4.0 * before * before - 1.0), 0.0
        )
    )
    inside = jnp.arange(1, waves + 1, dtype=jnp.int32) < waves - order
    return (
        jnp.where(inside, step_a, 0.0),
        jnp.where(inside, step_a * step_b, 0.0),
        jnp.cos(angles),
        log_start,
        sine * (math.pi / math.sqrt(total_lat)),
    )


def near(array):
    return pltpu.with_memory_space_constraint(array, pltpu.VMEM)


def smem():
    return pl.BlockSpec(memory_space=pltpu.SMEM)


def vmem():
    return pl.BlockSpec(memory_space=pltpu.VMEM)


def fourier_table(row_waves, limits, following, points):
    return pl.pallas_call(
        functools.partial(fourier_kernel, points=points),
        out_shape=(
            pltpu.VMEM((row_waves.shape[0], points + LANES), jnp.bfloat16),
            pltpu.VMEM((1, LANES), jnp.float32),
        ),
        in_specs=[vmem()] * 3,
        out_specs=(vmem(),) * 2,
        scratch_shapes=[pltpu.VMEM((following.shape[1], LANES), jnp.float32)],
        name="fourier",
        compiler_params=pltpu.CompilerParams(vmem_limit_bytes=GRANT),
    )(*map(near, (row_waves, limits, following)))


def legendre_table(order, bands, band_rows, waves):
    step_a, step_c, *planes = legendre_inputs(order, bands, band_rows, waves, bands * band_rows)
    return pl.pallas_call(
        functools.partial(legendre_kernel, waves=waves, band_rows=band_rows),
        out_shape=pltpu.VMEM((waves, band_rows // 2 * LANES), jnp.bfloat16),
        in_specs=[smem(), smem(), vmem(), vmem(), vmem()],
        out_specs=vmem(),
        scratch_shapes=[pltpu.VMEM((BLOCK * band_rows, LANES), jnp.float32)],
        name="legendre",
        compiler_params=pltpu.CompilerParams(vmem_limit_bytes=GRANT),
    )(step_a, step_c, *map(near, planes))


def pack(limits, prognostic, departure, lat_weight, lon_weight):
    channels, band_rows, sector_cols = prognostic.shape
    return pl.pallas_call(
        pack_kernel,
        out_shape=(
            pltpu.VMEM((channels + 4, band_rows, sector_cols), jnp.bfloat16),
            pltpu.VMEM(prognostic.shape, jnp.bfloat16),
            pltpu.VMEM((3, band_rows, sector_cols), jnp.float32),
        ),
        in_specs=[vmem()] * 5,
        out_specs=(vmem(),) * 3,
        scratch_shapes=[pltpu.VMEM((band_rows, sector_cols), jnp.float32)],
        name="pack",
    )(limits, prognostic, departure, lat_weight, lon_weight)


def interpolate(place, field, own, following, copies):
    channels, band_rows, sector_cols = field.shape
    tall = band_rows + 2 * HALO
    tiles = sector_cols // LANES
    height = tiles * (channels + 1) * band_rows + band_rows
    count = 2 * HALO + 1
    return pl.pallas_call(
        arrival_kernel,
        out_shape=pltpu.VMEM((copies, height, LANES), jnp.bfloat16),
        in_specs=[vmem()] * 4,
        out_specs=vmem(),
        scratch_shapes=[
            pltpu.VMEM((channels, tiles, tall, LANES), jnp.float32),
            pltpu.VMEM((3, count, tiles, tall, LANES), jnp.float32),
            pltpu.VMEM((2 * count, band_rows, sector_cols), jnp.float32),
            pltpu.VMEM((height, LANES), jnp.float32),
        ],
        name="arrival",
    )(*map(near, (place, field, own, following)))


def transform(cycles, fourier, row_waves, limits, channels, band_rows):
    return pl.pallas_call(
        transform_kernel,
        out_shape=pltpu.VMEM((fourier.shape[0], LANES), jnp.bfloat16),
        in_specs=[vmem()] * 4,
        out_specs=vmem(),
        scratch_shapes=[
            pltpu.VMEM((3, 2 * HALO + 1, 1, band_rows + 2 * HALO, LANES), jnp.float32),
            pltpu.VMEM((channels * band_rows, LANES), jnp.float32),
        ],
        name="transform",
        compiler_params=pltpu.CompilerParams(vmem_limit_bytes=GRANT),
    )(*map(near, (cycles, fourier, row_waves, limits)))


def synthesize(data, functions, channels):
    waves, span = functions.shape
    return pl.pallas_call(
        synthesis_kernel,
        out_shape=jax.ShapeDtypeStruct((channels, 2, waves), jnp.float32),
        in_specs=[vmem()] * 2,
        out_specs=vmem(),
        scratch_shapes=[
            pltpu.VMEM((4, LANES, LANES), jnp.float32),
            pltpu.VMEM((64, span), jnp.float32),
        ],
        name="synthesis",
        compiler_params=pltpu.CompilerParams(vmem_limit_bytes=GRANT),
    )(near(data), near(functions))


def shards(prognostic, departure, lat_weight, lon_weight, cycle_waves, wave_order):
    band_rows = prognostic.shape[1]
    bands = lax.axis_size("lat")
    sectors = lax.axis_size("lon")
    total_lon = prognostic.shape[2] * sectors
    waves = wave_order.shape[0]
    band_index = lax.axis_index("lat")
    sector_index = lax.axis_index("lon")

    packed, field, own = pack(
        cycle_waves[None], prognostic, departure, lat_weight, lon_weight
    )
    following = lax.ppermute(packed, "lat", [((i + 1) % bands, i) for i in range(bands)])
    number = lax.broadcasted_iota(jnp.int32, (4, band_rows, LANES), 0)
    place = jnp.where(
        number < 3, (sector_index >> number) & 1, (band_index == bands - 1).astype(jnp.int32)
    ).astype(jnp.float32)
    arrival = interpolate(place, field, own, following, sectors)
    cycles = lax.all_to_all(arrival, "lon", split_axis=0, concat_axis=0, tiled=True)

    slot_waves = wave_order.reshape(bands, sectors)
    own_waves = lax.dynamic_slice_in_dim(slot_waves, sector_index, 1, axis=1)
    order = lax.dynamic_slice_in_dim(wave_order, band_index * sectors + sector_index, 1)
    row_waves = jnp.broadcast_to(own_waves[:, :, None], (bands, 2, LANES)).reshape(
        2 * bands, LANES
    )
    fourier, limits = fourier_table(row_waves, cycle_waves[None], following, total_lon)
    functions = legendre_table(order, bands, band_rows, waves)
    cycles, functions = lax.optimization_barrier((cycles, functions))
    masked = transform(cycles, fourier, row_waves, limits, prognostic.shape[0], band_rows)
    data = lax.all_to_all(
        masked.reshape(bands, 2, LANES), "lat", split_axis=0, concat_axis=0, tiled=True
    ).reshape(2 * bands, LANES)
    spectral = synthesize(data, functions, prognostic.shape[0])
    return spectral.transpose(1, 0, 2)[None]


def solution(mesh):
    in_specs = (
        P(None, "lat", "lon"),
        P("lat", "lon"),
        P("lat", "lon"),
        P("lat", "lon"),
        P("lat"),
        P(),
    )
    out_specs = P(("lat", "lon"), None, None, None)
    return jax.shard_map(shards, mesh=mesh, in_specs=in_specs, out_specs=out_specs, check_vma=False)
```

```python
import functools
import math

import jax
import jax.numpy as jnp
from jax import lax
from jax.experimental import pallas as pl
from jax.experimental.pallas import tpu as pltpu
from jax.sharding import PartitionSpec as P

HALO = 4
LANES = 128
BLOCK = 32
GRANT = 16 << 20
WINDOW = 4 * HALO
LGAMMA_HALF_THREE = 0.5 * math.log(math.pi) - math.log(2.0)
SINE = (
    3.1415926535897932,
    -5.1677127800499700,
    2.5501640398773455,
    -0.59926452932079211,
    0.082145886611128233,
    -0.0073704309457143504,
)


def fourier_kernel(waves, limits, following, out, bound, line, *, points):
    rows, group = waves.shape[0], 64
    scale = 1.0 / math.sqrt(points)
    row = lax.broadcasted_iota(jnp.int32, (group, LANES), 0)
    turn = (row % 2 * (points // 4)).astype(jnp.float32)
    place = lax.broadcasted_iota(jnp.int32, (group, LANES), 1)
    lane = place.astype(jnp.float32)
    column = (
        (place // WINDOW + 1) * (points * WINDOW // LANES) - 2 * HALO + place % WINDOW
    ).astype(jnp.float32)

    def cosine(phase):
        phase = phase - jnp.floor(phase * (1.0 / points) + 0.5) * float(points)
        z = 0.5 - jnp.abs(phase) * (2.0 / points)
        square = z * z
        total = jnp.full_like(z, SINE[-1])
        for factor in SINE[-2::-1]:
            total = total * square + factor
        return total * z

    def block(g, carry):
        first = pl.multiple_of(g * group, group)
        wave = waves[pl.ds(first, group), :].astype(jnp.float32)
        phase = lane * wave + turn
        real = cosine(phase) * scale
        imag = cosine(phase - points / 4) * scale
        ahead = wave * float(LANES)
        turn_real = cosine(ahead)
        turn_imag = cosine(ahead - points / 4)
        for t in range(points // LANES):
            out[pl.ds(first, group), t * LANES : (t + 1) * LANES] = real.astype(jnp.bfloat16)
            real, imag = (
                real * turn_real - imag * turn_imag,
                imag * turn_real + real * turn_imag,
            )
        edge = cosine(column * wave + turn) * scale
        out[pl.ds(first, group), points : points + LANES] = edge.astype(jnp.bfloat16)
        return carry

    lax.fori_loop(0, rows // group, block, 0)

    band_rows = limits.shape[1]
    line[...] = jnp.zeros_like(line)
    line[:1, :band_rows] = limits[...].astype(jnp.float32)
    own = line[...]
    last = following[following.shape[0] - 1].astype(jnp.float32)
    ahead = last[:, :LANES] * 256.0 + last[:, LANES : 2 * LANES]
    width = band_rows
    while width < LANES:
        own = own + pltpu.roll(own, width, 1)
        ahead = ahead + pltpu.roll(ahead, width, 1)
        width *= 2
    bound[...] = jnp.where(
        place[:1] % band_rows < HALO,
        pltpu.roll(own, LANES - HALO, 1)[:1],
        pltpu.roll(ahead, HALO, 1)[HALO : HALO + 1],
    )


def legendre_kernel(step_a, step_c, cosine, log_start, weight, out, stage, *, waves, band_rows):
    cos = cosine[...]
    start = log_start[...]
    scale = weight[...]

    def block(t, carry):
        current, last, log_scale = carry
        base = t * BLOCK
        size = jnp.exp(log_scale + start) * scale
        for u in range(0, BLOCK, 2):
            first_a = step_a[base + u] * cos
            second_a = step_a[base + u + 1] * cos
            first_c = step_c[base + u]
            middle = first_a * current - first_c * last
            fresh = (second_a * first_a - step_c[base + u + 1]) * current - (
                second_a * first_c
            ) * last
            stage[band_rows * u : band_rows * (u + 1), :] = current * size
            stage[band_rows * (u + 1) : band_rows * (u + 2), :] = middle * size
            last = middle
            current = fresh
        row = pl.multiple_of(base, BLOCK)
        for r in range(band_rows // 2):
            out[pl.ds(row, BLOCK), r * LANES : (r + 1) * LANES] = stage[
                pl.ds(r, BLOCK, stride=band_rows), :
            ].astype(jnp.bfloat16)
        factor = jnp.maximum(jnp.maximum(jnp.abs(current), jnp.abs(last)), 1.0)
        inverse = 1.0 / factor
        return current * inverse, last * inverse, log_scale + jnp.log(factor)

    initial = (jnp.ones_like(cos), jnp.zeros_like(cos), jnp.zeros_like(cos))
    lax.fori_loop(0, waves // BLOCK, block, initial)


def spread(place, share):
    return [
        jnp.where(place == d, 1.0 - share, jnp.where(place == d - 1, share, 0.0))
        for d in range(2 * HALO + 1)
    ]


def edges(tall, slot):
    lane = lax.broadcasted_iota(jnp.int32, tall[0].shape, 1)
    reach = 2 * HALO
    ends = jnp.where(
        lane < reach, tall[0], jnp.where(lane >= LANES - reach, tall[-1], jnp.zeros_like(tall[0]))
    )
    return pltpu.roll(ends, slot * WINDOW + reach, 1)


def stencil(read, write, row_parts, col_parts, tiles, rows):
    count = 2 * HALO + 1
    source = read()
    lane = lax.broadcasted_iota(jnp.int32, source[0].shape, 1)
    for d in range(count):
        move = d - HALO
        if move == 0:
            turned = source
        else:
            rolled = [pltpu.roll(tile, -move % LANES, 1) for tile in source]
            if tiles == 1:
                turned = rolled
            elif move > 0:
                turned = [
                    jnp.where(lane < LANES - move, rolled[t], rolled[(t + 1) % tiles])
                    for t in range(tiles)
                ]
            else:
                turned = [
                    jnp.where(lane < -move, rolled[t - 1], rolled[t]) for t in range(tiles)
                ]
        for t in range(tiles):
            write[d, t] = turned[t]
    sums = []
    for t in range(tiles):
        total = None
        for e in range(count):
            inner = None
            for d in range(count):
                term = col_parts(d, t) * write[d, t, e : e + rows, :]
                inner = term if inner is None else inner + term
            term = row_parts(e, t) * inner
            total = term if total is None else total + term
        sums.append(total)
    return sums


def split(value):
    high = value.astype(jnp.bfloat16).astype(jnp.float32)
    rest = value - high
    middle = rest.astype(jnp.bfloat16).astype(jnp.float32)
    return [high, middle, rest - middle]


def pack_kernel(limits, field, departure, lat_weight, lon_weight, out, field_out, own, line):
    channels = field.shape[0]
    cols = departure.shape[1]
    value = field[...]
    field_out[...] = value
    out[:channels] = value
    cell = departure[...].astype(jnp.float32)
    a = lat_weight[...]
    b = lon_weight[...]
    for p, plane in enumerate((cell, a, b)):
        own[p] = plane
    planes = [v[:HALO] for v in [cell] + split(a) + split(b)]
    for p in range(0, len(planes) - 1, 2):
        pair = jnp.concatenate(planes[p : p + 2], axis=0)
        out[channels + p // 2] = pair.astype(jnp.bfloat16)
    rows = limits.shape[1]
    bound = limits[...].astype(jnp.float32)
    high = jnp.floor(bound * (1.0 / 256.0))
    line[:HALO] = planes[-1]
    line[HALO:] = jnp.zeros_like(planes[-1])
    line[HALO : HALO + 1, :rows] = high
    line[HALO : HALO + 1, LANES : LANES + rows] = bound - high * 256.0
    out[channels + len(planes) // 2] = line[...].astype(jnp.bfloat16)


def arrival_kernel(place, field, own, following, out, grid, shifted, parts, stage):
    channels, rows, cols = field.shape
    tiles = cols // LANES
    count = 2 * HALO + 1
    used = channels * rows
    pitch = used + rows
    lane = lax.broadcasted_iota(jnp.int32, (rows, LANES), 1)
    row = lax.broadcasted_iota(jnp.int32, (rows, cols), 0)
    last = jnp.concatenate([place[3]] * tiles, axis=1)
    pairs = [following[channels + p].astype(jnp.float32) for p in range(4)]
    ahead = [pairs[p // 2][p % 2 * HALO : (p % 2 + 1) * HALO] for p in range(7)]

    def rows_of(plane, rest):
        return jnp.concatenate([plane[HALO:], rest], axis=0)

    cell = rows_of(own[0], ahead[0])
    a = rows_of(own[1], ahead[1] + ahead[2] + ahead[3])
    b = rows_of(own[2], ahead[4] + ahead[5] + ahead[6])
    high = jnp.floor(cell * (1.0 / (2 * HALO)))
    for e, part in enumerate(spread(high, a)):
        parts[e] = jnp.where((row < HALO) == (row + e < rows), part, part * (1.0 - last))
    for d, part in enumerate(spread(cell - high * (2 * HALO), b)):
        parts[count + d] = part
    total = None
    for p, plane in enumerate([cell + last * (4 * HALO * HALO)] + split(a) + split(b)):
        term = edges([plane[:, t * LANES : (t + 1) * LANES] for t in range(tiles)], p + 1)
        total = term if total is None else total + term
    planes = total
    for c in range(channels):
        here = field[c].astype(jnp.float32)
        there = following[c].astype(jnp.float32)
        for t in range(tiles):
            span = slice(t * LANES, (t + 1) * LANES)
            grid[c, t, :rows, :] = here[:, span]
            grid[c, t, rows:, :] = there[:, span]

    def part(first):
        return lambda d, t: parts[first + d, :, t * LANES : (t + 1) * LANES]

    for c in range(channels):
        sums = stencil(
            lambda: [grid[c, t] for t in range(tiles)],
            shifted.at[c % shifted.shape[0]],
            part(0),
            part(count),
            tiles,
            rows,
        )
        sums[0] = jnp.where(lane < HALO, 0.0, sums[0])
        sums[-1] = jnp.where(lane >= LANES - HALO, 0.0, sums[-1])
        for t in range(tiles):
            stage[t * pitch + c * rows : t * pitch + (c + 1) * rows, :] = sums[t]
    slots = LANES // WINDOW
    bits = [jnp.concatenate([place[k]] * 2, axis=0) > 0.0 for k in range(3)]
    for g in range(2):
        total = None
        for c in range(g * slots, min((g + 1) * slots, channels)):
            term = edges([grid[c, 0], grid[c, tiles - 1]], c - g * slots)
            total = term if total is None else total + term
        if g == 1:
            total = total + jnp.concatenate([planes, jnp.zeros_like(planes)], axis=0)
        for k in range(3):
            total = jnp.where(bits[k], pltpu.roll(total, WINDOW << k, 1), total)
        if g == 0:
            stage[used:pitch, :] = total[:rows]
            stage[pitch + used : 2 * pitch, :] = total[rows:]
        else:
            stage[2 * pitch + used :, :] = total
    value = stage[...].astype(jnp.bfloat16)
    for copy in range(out.shape[0]):
        out[copy] = value


def transform_kernel(cycles, fourier, waves, limits, out, shifted, stage):
    sectors = cycles.shape[0]
    used, rows = stage.shape[0], shifted.shape[3] - 2 * HALO
    tall = rows + 2 * HALO
    channels = used // rows
    slots = LANES // WINDOW
    slot = lax.broadcasted_iota(jnp.int32, (tall, LANES), 1) // WINDOW
    inner = lax.broadcasted_iota(jnp.int32, (tall, LANES), 1) % WINDOW
    pitch = used + rows
    tiles = cycles.shape[1] // pitch

    def piece(sector, first, count):
        return cycles[sector, first : first + count, :].astype(jnp.float32)

    pieces = [
        [
            jnp.concatenate(
                [piece(sector, used, rows), piece(sector, pitch + used, rows)], axis=0
            )
            for sector in range(sectors)
        ],
        [piece(sector, 2 * pitch + used, tall) for sector in range(sectors)],
    ]

    def window(index, height):
        g, c = divmod(index, slots)
        total = pieces[g][0][:height]
        for sector in range(1, sectors):
            total = jnp.where(
                slot[:height] == (c + sector) % slots, pieces[g][sector][:height], total
            )
        left = pltpu.roll(total, -c * WINDOW % LANES, 1) if c else total
        right = pltpu.roll(total, -(c + 1) * WINDOW % LANES, 1) if c + 1 < slots else total
        return jnp.where(inner[:height] < 2 * HALO, left, right)

    cell, *weights = [window(channels + p, rows) for p in range(7)]
    last = (cell >= 4 * HALO * HALO).astype(jnp.float32)
    cell = cell - last * (4 * HALO * HALO)
    row = lax.broadcasted_iota(jnp.int32, cell.shape, 0)
    a = weights[0] + weights[1] + weights[2]
    b = weights[3] + weights[4] + weights[5]
    high = jnp.floor(cell * (1.0 / (2 * HALO)))
    row_parts = [
        jnp.where((row < HALO) == (row + e < rows), part, part * (1.0 - last))
        for e, part in enumerate(spread(high, a))
    ]
    col_parts = spread(cell - high * (2 * HALO), b)
    inside = (inner[:rows] >= HALO) & (inner[:rows] < 3 * HALO)
    for c in range(channels):
        (total,) = stencil(
            lambda: [window(c, tall)],
            shifted.at[c % shifted.shape[0]],
            lambda e, t: row_parts[e],
            lambda d, t: col_parts[d],
            1,
            rows,
        )
        stage[c * rows : (c + 1) * rows, :] = jnp.where(inside, total, 0.0)
    gathered = jnp.concatenate(
        [
            cycles[sector, t * pitch : t * pitch + used, :]
            for sector in range(sectors)
            for t in range(tiles)
        ]
        + [stage[...].astype(jnp.bfloat16)],
        axis=1,
    )
    spectrum = lax.dot_general(
        fourier[...], gathered, (((1,), (1,)), ((), ())), preferred_element_type=jnp.float32
    )
    resolved = waves[:, :used].astype(jnp.float32) < limits[:, :used]
    out[:, :used] = jnp.where(resolved, spectrum, 0.0).astype(jnp.bfloat16)
    out[:, used:] = jnp.zeros((out.shape[0], out.shape[1] - used), jnp.bfloat16)


def synthesis_kernel(data, functions, out, turned, packed):
    channels, parts, waves = out.shape
    bands = data.shape[0] // parts
    kept = packed.shape[1] // LANES
    band_rows = 2 * kept
    source = lax.broadcasted_iota(jnp.int32, (parts * bands, LANES), 0)
    target = lax.broadcasted_iota(jnp.int32, (parts * bands, LANES), 1)
    chosen = [
        (source == parts * band + e).astype(jnp.float32).astype(jnp.bfloat16)
        for band in (target, jnp.where(target == bands - 1, target, bands - 2 - target))
        for e in range(parts)
    ]
    columns = lax.dot_general(
        data[...],
        jnp.concatenate(chosen, axis=1),
        (((0,), (0,)), ((), ())),
        preferred_element_type=jnp.float32,
    )
    for place in range(2 * parts):
        turned[place] = columns[:, place * LANES : (place + 1) * LANES]
    packed[...] = jnp.zeros_like(packed)
    step = packed.shape[0] // (2 * parts)
    for mirror in range(2):
        for e in range(parts):
            first = (mirror * parts + e) * step
            for r in range(kept):
                row = band_rows - 1 - r if mirror else r
                packed[first : first + channels, r * LANES : (r + 1) * LANES] = turned[
                    mirror * parts + e, pl.ds(row, channels, stride=band_rows), :
                ]
    result = lax.dot_general(
        packed[...].astype(jnp.bfloat16),
        functions[...],
        (((1,), (1,)), ((), ())),
        preferred_element_type=jnp.float32,
    )
    even = lax.broadcasted_iota(jnp.int32, (channels, waves), 1) % 2 == 0
    for e in range(parts):
        near_half = result[e * step : e * step + channels, :]
        far_half = result[(parts + e) * step : (parts + e) * step + channels, :]
        out[:, e, :] = near_half + jnp.where(even, far_half, -far_half)


def legendre_inputs(order, bands, band_rows, waves, total_lat):
    spread = lax.optimization_barrier(jnp.broadcast_to(order, (band_rows, LANES)))
    order_real = spread.astype(jnp.float32)
    band = jnp.minimum(lax.broadcasted_iota(jnp.int32, (band_rows, LANES), 1), bands - 1)
    cycle = band * band_rows + lax.broadcasted_iota(jnp.int32, (band_rows, LANES), 0) + HALO
    cycle = cycle % total_lat
    angles = (cycle.astype(jnp.float32) + 0.5) * (math.pi / total_lat)
    sine = jnp.sin(angles)
    log_start = (
        0.5 * math.log(0.5)
        + 0.5 * (lax.lgamma(order_real + 1.5) - LGAMMA_HALF_THREE - lax.lgamma(order_real + 1.0))
        + order_real * jnp.log(sine)
    )
    order_real = order.astype(jnp.float32)
    degree = order_real + jnp.arange(1, waves + 1, dtype=jnp.int32).astype(jnp.float32)
    step_a = jnp.sqrt((4.0 * degree * degree - 1.0) / (degree * degree - order_real * order_real))
    before = degree - 1.0
    step_b = jnp.sqrt(
        jnp.maximum(
            (before * before - order_real * order_real) / (4.0 * before * before - 1.0), 0.0
        )
    )
    inside = jnp.arange(1, waves + 1, dtype=jnp.int32) < waves - order
    return (
        jnp.where(inside, step_a, 0.0),
        jnp.where(inside, step_a * step_b, 0.0),
        jnp.cos(angles),
        log_start,
        sine * (math.pi / math.sqrt(total_lat)),
    )


def near(array):
    return pltpu.with_memory_space_constraint(array, pltpu.VMEM)


def smem():
    return pl.BlockSpec(memory_space=pltpu.SMEM)


def vmem():
    return pl.BlockSpec(memory_space=pltpu.VMEM)


def fourier_table(row_waves, limits, following, points):
    return pl.pallas_call(
        functools.partial(fourier_kernel, points=points),
        out_shape=(
            pltpu.VMEM((row_waves.shape[0], points + LANES), jnp.bfloat16),
            pltpu.VMEM((1, LANES), jnp.float32),
        ),
        in_specs=[vmem()] * 3,
        out_specs=(vmem(),) * 2,
        scratch_shapes=[pltpu.VMEM((following.shape[1], LANES), jnp.float32)],
        name="fourier",
        compiler_params=pltpu.CompilerParams(vmem_limit_bytes=GRANT),
    )(*map(near, (row_waves, limits, following)))


def legendre_table(order, bands, band_rows, waves):
    step_a, step_c, *planes = legendre_inputs(order, bands, band_rows, waves, bands * band_rows)
    return pl.pallas_call(
        functools.partial(legendre_kernel, waves=waves, band_rows=band_rows),
        out_shape=pltpu.VMEM((waves, band_rows // 2 * LANES), jnp.bfloat16),
        in_specs=[smem(), smem(), vmem(), vmem(), vmem()],
        out_specs=vmem(),
        scratch_shapes=[pltpu.VMEM((BLOCK * band_rows, LANES), jnp.float32)],
        name="legendre",
        compiler_params=pltpu.CompilerParams(vmem_limit_bytes=GRANT),
    )(step_a, step_c, *map(near, planes))


def pack(limits, prognostic, departure, lat_weight, lon_weight):
    channels, band_rows, sector_cols = prognostic.shape
    return pl.pallas_call(
        pack_kernel,
        out_shape=(
            pltpu.VMEM((channels + 4, band_rows, sector_cols), jnp.bfloat16),
            pltpu.VMEM(prognostic.shape, jnp.bfloat16),
            pltpu.VMEM((3, band_rows, sector_cols), jnp.float32),
        ),
        in_specs=[vmem()] * 5,
        out_specs=(vmem(),) * 3,
        scratch_shapes=[pltpu.VMEM((band_rows, sector_cols), jnp.float32)],
        name="pack",
    )(limits, prognostic, departure, lat_weight, lon_weight)


def interpolate(place, field, own, following, copies):
    channels, band_rows, sector_cols = field.shape
    tall = band_rows + 2 * HALO
    tiles = sector_cols // LANES
    height = tiles * (channels + 1) * band_rows + band_rows
    count = 2 * HALO + 1
    return pl.pallas_call(
        arrival_kernel,
        out_shape=pltpu.VMEM((copies, height, LANES), jnp.bfloat16),
        in_specs=[vmem()] * 4,
        out_specs=vmem(),
        scratch_shapes=[
            pltpu.VMEM((channels, tiles, tall, LANES), jnp.float32),
            pltpu.VMEM((4, count, tiles, tall, LANES), jnp.float32),
            pltpu.VMEM((2 * count, band_rows, sector_cols), jnp.float32),
            pltpu.VMEM((height, LANES), jnp.float32),
        ],
        name="arrival",
    )(*map(near, (place, field, own, following)))


def transform(cycles, fourier, row_waves, limits, channels, band_rows):
    return pl.pallas_call(
        transform_kernel,
        out_shape=pltpu.VMEM((fourier.shape[0], LANES), jnp.bfloat16),
        in_specs=[vmem()] * 4,
        out_specs=vmem(),
        scratch_shapes=[
            pltpu.VMEM((9, 2 * HALO + 1, 1, band_rows + 2 * HALO, LANES), jnp.float32),
            pltpu.VMEM((channels * band_rows, LANES), jnp.float32),
        ],
        name="transform",
        compiler_params=pltpu.CompilerParams(vmem_limit_bytes=GRANT),
    )(*map(near, (cycles, fourier, row_waves, limits)))


def synthesize(data, functions, channels):
    waves, span = functions.shape
    return pl.pallas_call(
        synthesis_kernel,
        out_shape=jax.ShapeDtypeStruct((channels, 2, waves), jnp.float32),
        in_specs=[vmem()] * 2,
        out_specs=vmem(),
        scratch_shapes=[
            pltpu.VMEM((4, LANES, LANES), jnp.float32),
            pltpu.VMEM((64, span), jnp.float32),
        ],
        name="synthesis",
        compiler_params=pltpu.CompilerParams(vmem_limit_bytes=GRANT),
    )(near(data), near(functions))


def shards(prognostic, departure, lat_weight, lon_weight, cycle_waves, wave_order):
    band_rows = prognostic.shape[1]
    bands = lax.axis_size("lat")
    sectors = lax.axis_size("lon")
    total_lon = prognostic.shape[2] * sectors
    waves = wave_order.shape[0]
    band_index = lax.axis_index("lat")
    sector_index = lax.axis_index("lon")

    packed, field, own = pack(
        cycle_waves[None], prognostic, departure, lat_weight, lon_weight
    )
    following = lax.ppermute(packed, "lat", [((i + 1) % bands, i) for i in range(bands)])
    number = lax.broadcasted_iota(jnp.int32, (4, band_rows, LANES), 0)
    place = jnp.where(
        number < 3, (sector_index >> number) & 1, (band_index == bands - 1).astype(jnp.int32)
    ).astype(jnp.float32)
    arrival = interpolate(place, field, own, following, sectors)
    cycles = lax.all_to_all(arrival, "lon", split_axis=0, concat_axis=0, tiled=True)

    slot_waves = wave_order.reshape(bands, sectors)
    own_waves = lax.dynamic_slice_in_dim(slot_waves, sector_index, 1, axis=1)
    order = lax.dynamic_slice_in_dim(wave_order, band_index * sectors + sector_index, 1)
    row_waves = jnp.broadcast_to(own_waves[:, :, None], (bands, 2, LANES)).reshape(
        2 * bands, LANES
    )
    fourier, limits = fourier_table(row_waves, cycle_waves[None], following, total_lon)
    functions = legendre_table(order, bands, band_rows, waves)
    cycles, functions = lax.optimization_barrier((cycles, functions))
    masked = transform(cycles, fourier, row_waves, limits, prognostic.shape[0], band_rows)
    data = lax.all_to_all(
        masked.reshape(bands, 2, LANES), "lat", split_axis=0, concat_axis=0, tiled=True
    ).reshape(2 * bands, LANES)
    spectral = synthesize(data, functions, prognostic.shape[0])
    return spectral.transpose(1, 0, 2)[None]


def solution(mesh):
    in_specs = (
        P(None, "lat", "lon"),
        P("lat", "lon"),
        P("lat", "lon"),
        P("lat", "lon"),
        P("lat"),
        P(),
    )
    out_specs = P(("lat", "lon"), None, None, None)
    return jax.shard_map(shards, mesh=mesh, in_specs=in_specs, out_specs=out_specs, check_vma=False)
```
